32 devices in a mesh: dp: 8 (over z, x), tensor: 4 (over y, core).
Axes of the slice: x: 2, y: 2, z: 4, core: 2. Of those that a mesh axis runs over, the one named last changes fastest.
Arguments:
- block_in: bfloat16 [16384, 1024], P(('dp', 'tensor')), may hold values from -6 to 6
- segments: int32 [16, 1024], P('dp'), may hold values from 0 to 4, as said below
- first_gain: float32 [1024], replicated, may hold values from 0.5 to 1.5
- first_shift: float32 [1024], replicated, may hold values from -1.25 to 1.25
- w_qkv: bfloat16 [1024, 3, 1024], P(None, None, 'tensor'), may hold values from -0.1875 to 0.1875
- qv_bias: float32 [2, 1024], P(None, 'tensor'), may hold values from -1.75 to 1.75
- w_mix: bfloat16 [1024, 1024], P('tensor'), may hold values from -0.75 to 0.75
- mix_bias: float32 [1024], replicated, may hold values from -1.25 to 1.25
- second_gain: float32 [1024], replicated, may hold values from 0.5 to 1.5
- second_shift: float32 [1024], replicated, may hold values from -1.25 to 1.25
- w_expand: bfloat16 [1024, 4096], P(None, 'tensor'), may hold values from -0.1875 to 0.1875
- expand_bias: float32 [4096], P('tensor'), may hold values from -1.75 to 1.75
- w_reduce: bfloat16 [4096, 1024], P('tensor'), may hold values from -0.125 to 0.125
- reduce_bias: float32 [1024], replicated, may hold values from -1.25 to 1.25
- out_grad: bfloat16 [16384, 1024], P(('dp', 'tensor')), may hold values from -6 to 6
Outputs:
- block_out: bfloat16 [16384, 1024], P(('dp', 'tensor'))
- in_grad: float32 [16384, 1024], P(('dp', 'tensor'))
- first_gain_grad: float32 [1024], replicated
- first_shift_grad: float32 [1024], replicated
- qkv_grad: float32 [1024, 3, 1024], P(None, None, 'tensor')
- qv_bias_grad: float32 [2, 1024], P(None, 'tensor')
- mix_grad: float32 [1024, 1024], P('tensor')
- mix_bias_grad: float32 [1024], replicated
- second_gain_grad: float32 [1024], replicated
- second_shift_grad: float32 [1024], replicated
- expand_grad: float32 [1024, 4096], P(None, 'tensor')
- expand_bias_grad: float32 [4096], P('tensor')
- reduce_grad: float32 [4096, 1024], P('tensor')
- reduce_bias_grad: float32 [1024], replicated
The draws below stay inside these ranges and needn't reach their ends.
Inputs may be any that keep to these rules, and one draw needn't show every extreme that they name: `segments`: each row of 1024 tokens holds five documents numbered 0 to 4 in order, each a run of consecutive tokens; document 2 starts before token 256 and its last token is at position 768 or later.
All inputs are finite; a program needn't handle non-finite values.
Results may differ from the reference program's by a relative error of at most 0.014.
Values may be sent and summed in bfloat16 or wider, within the bound.
A program may use at most 192 MiB of HBM per device.

```python
import jax
import jax.numpy as jnp
from jax import lax

D = 1024
HEADS = 16
HD = 64
FF = 4096
SEQ = 1024
SEQS = 16
TOKENS = 16384


def draw_segments(key, part):
    keys = jax.random.split(key, 4)
    front = jax.random.randint(keys[0], (SEQS, 1), SEQ // 8, SEQ // 4)
    back = jax.random.randint(keys[1], (SEQS, 1), 3 * SEQ // 4 + 1, 7 * SEQ // 8 + 1)
    first_cut = front // 3 + jax.random.randint(keys[2], (SEQS, 1), 0, 1048576) % (front // 3 + 1)
    tail = SEQ - back
    last_cut = back + tail // 3 + jax.random.randint(keys[3], (SEQS, 1), 0, 1048576) % (tail // 3 + 1)
    positions = jnp.arange(SEQ, dtype=jnp.int32)[None, :]
    result = (positions >= first_cut).astype(jnp.int32) + (positions >= front).astype(jnp.int32)
    result = result + (positions >= back).astype(jnp.int32) + (positions >= last_cut).astype(jnp.int32)
    return result.astype(jnp.int32)


def shard_levels(rng, shape, cuts, smallest, top_value):
    def one(dim, parts):
        steps = jax.random.uniform(jax.random.fold_in(jax.random.fold_in(rng, 6), dim), (parts,), jnp.float32, smallest / len(cuts), top_value / len(cuts))
        return jnp.repeat(jnp.exp(steps), shape[dim] // parts).reshape((-1,) + (1,) * (len(shape) - dim - 1))

    gain = one(*cuts[0])
    for cut in cuts[1:]:
        gain = gain * one(*cut)
    return gain


def centred(key, extent, spread, bound, pieces=(), held_as=jnp.bfloat16):
    entries = spread * jax.random.normal(key, extent, jnp.float32)
    if pieces:
        entries = entries * shard_levels(key, extent, pieces, -0.22, 0.18)
    return jnp.clip(entries, -bound, bound).astype(held_as)


def setup_inputs(seed: int = 0) -> dict:
    key_of = jax.random.split(jax.random.key(seed), 16)
    block_in = centred(key_of[0], (TOKENS, D), 1.0, 6.0, ((0, 32),))
    segments = draw_segments(jax.random.fold_in(key_of[15], 71), 0)
    first_gain = jnp.clip(1.0 + 0.1 * jax.random.normal(key_of[2], (D,), jnp.float32), 0.5, 1.5)
    first_shift = centred(key_of[3], (D,), 0.2, 1.25, (), jnp.float32)
    w_qkv = centred(key_of[4], (D, 3, D), D ** -0.5, 0.1875, ((2, 4),))
    qv_bias = centred(key_of[5], (2, D), 0.3, 1.75, ((1, 4),), jnp.float32)
    w_mix = centred(key_of[6], (D, D), (D // 16) ** -0.5, 0.75, ((0, 4),))
    mix_bias = centred(key_of[7], (D,), 0.2, 1.25, (), jnp.float32)
    second_gain = jnp.clip(1.0 + 0.1 * jax.random.normal(key_of[8], (D,), jnp.float32), 0.5, 1.5)
    second_shift = centred(key_of[9], (D,), 0.2, 1.25, (), jnp.float32)
    w_expand = centred(key_of[10], (D, FF), D ** -0.5, 0.1875, ((1, 4),))
    expand_bias = centred(key_of[11], (FF,), 0.3, 1.75, ((0, 4),), jnp.float32)
    w_reduce = centred(key_of[12], (FF, D), (FF // 2) ** -0.5, 0.125, ((0, 4),))
    reduce_bias = centred(key_of[13], (D,), 0.2, 1.25, (), jnp.float32)
    out_grad = centred(key_of[14], (TOKENS, D), 1.0, 6.0, ((0, 32),))
    return {"block_in": block_in, "segments": segments, "first_gain": first_gain, "first_shift": first_shift, "w_qkv": w_qkv, "qv_bias": qv_bias, "w_mix": w_mix, "mix_bias": mix_bias, "second_gain": second_gain, "second_shift": second_shift, "w_expand": w_expand, "expand_bias": expand_bias, "w_reduce": w_reduce, "reduce_bias": reduce_bias, "out_grad": out_grad}


@jax.custom_vjp
def low(v):
    return lax.optimization_barrier(v.astype(jnp.bfloat16)).astype(jnp.float32)

@jax.custom_vjp
def low_back(v):
    return v

def low_keep(v):
    return (low(v), None)

def low_pass(kept, grad):
    return (grad,)

def back_keep(v):
    return (v, None)

def back_low(kept, grad):
    return (low(grad),)
low.defvjp(low_keep, low_pass)
low_back.defvjp(back_keep, back_low)
epsilon = 1e-05

def layer_norm(values, norm_gain, norm_shift):
    row_mean = lax.optimization_barrier(jnp.mean(values, axis=-1, keepdims=True))
    centered = values - row_mean
    variance = lax.optimization_barrier(jnp.mean(centered * centered, axis=-1, keepdims=True))
    return centered * lax.rsqrt(variance + epsilon) * norm_gain + norm_shift

def matmul(left_mat, right_mat):
    return jnp.dot(left_mat, right_mat, precision=lax.Precision.HIGHEST)

def attend(queries, key_rows, value_rows, seg_row):
    block_len = min(512, SEQ)
    block_count = SEQ // block_len
    positions = jnp.arange(SEQ, dtype=jnp.int32)
    score_scale = HD ** (-0.5)

    def one_block(index):
        row_start = index * block_len
        query_block = lax.dynamic_slice_in_dim(queries, row_start, block_len, 0)
        query_pos = row_start + jnp.arange(block_len, dtype=jnp.int32)
        query_seg = lax.dynamic_slice_in_dim(seg_row, row_start, block_len, 0)
        scores = jnp.einsum('qhd,khd->hqk', query_block, key_rows, precision=lax.Precision.HIGHEST) * score_scale
        scores = low_back(scores)
        allowed = jnp.logical_and(query_pos[:, None] >= positions[None, :], query_seg[:, None] == seg_row[None, :])
        scores = jnp.where(allowed[None], scores, -1e+30)
        probs = low(jax.nn.softmax(scores, axis=-1))
        return jnp.einsum('hqk,khd->qhd', probs, value_rows, precision=lax.Precision.HIGHEST)
    blocks = lax.map(jax.checkpoint(one_block), jnp.arange(block_count, dtype=jnp.int32))
    return blocks.reshape(SEQ, HEADS * HD)

def forward(params, seq_in, seg_row):
    first_gain, first_shift, w_qkv, qv_bias, w_mix, mix_bias, second_gain, second_shift, w_expand, expand_bias, w_reduce, reduce_bias = params
    normed_one = low(layer_norm(seq_in, first_gain, first_shift))
    queries = low(low_back(matmul(normed_one, w_qkv[:, 0, :]) + qv_bias[0]))
    key_rows = low(low_back(matmul(normed_one, w_qkv[:, 1, :])))
    value_rows = low(low_back(matmul(normed_one, w_qkv[:, 2, :]) + qv_bias[1]))
    shape_three = (SEQ, HEADS, HD)
    attended = attend(queries.reshape(shape_three), key_rows.reshape(shape_three), value_rows.reshape(shape_three), seg_row)
    attended = low(low_back(attended))
    mixed = low_back(matmul(attended, w_mix) + mix_bias)
    resid = seq_in + mixed
    normed_two = low(layer_norm(resid, second_gain, second_shift))
    pre_act = low_back(matmul(normed_two, w_expand) + expand_bias)
    activated = low(jax.nn.gelu(pre_act, approximate=True))
    branch = low_back(matmul(activated, w_reduce) + reduce_bias)
    return resid + branch

def reference(block_in, segments, first_gain, first_shift, w_qkv, qv_bias, w_mix, mix_bias, second_gain, second_shift, w_expand, expand_bias, w_reduce, reduce_bias, out_grad):
    params = tuple((item.astype(jnp.float32) for item in (first_gain, first_shift, w_qkv, qv_bias, w_mix, mix_bias, second_gain, second_shift, w_expand, expand_bias, w_reduce, reduce_bias)))
    seq_inputs = block_in.astype(jnp.float32).reshape(SEQS, SEQ, D)
    seq_grads = out_grad.astype(jnp.float32).reshape(SEQS, SEQ, D)
    zero_grads = jax.tree.map(jnp.zeros_like, params)

    def one_seq(running, item):
        seq_in, seg_row, grad_row = item
        result, pullback = jax.vjp(lambda weights, values: forward(weights, values, seg_row), params, seq_in)
        param_grads, input_grad = pullback(grad_row)
        return (jax.tree.map(jnp.add, running, param_grads), (result.astype(jnp.bfloat16), input_grad))
    totals, (outputs, input_grads) = lax.scan(one_seq, zero_grads, (seq_inputs, segments, seq_grads))
    return (outputs.reshape(TOKENS, D), input_grads.reshape(TOKENS, D), totals[0], totals[1], totals[2], totals[3], totals[4], totals[5], totals[6], totals[7], totals[8], totals[9], totals[10], totals[11])
```

```python
import functools

import jax
import jax.numpy as jnp
from jax import lax
from jax.experimental import pallas as pl
from jax.experimental.pallas import tpu as pltpu
from jax.sharding import PartitionSpec as P

HD = 64
PAIR = 2 * HD
QB = 256
EPS = 1e-5
BF = jnp.bfloat16
F32 = jnp.float32
SCALE = HD ** (-0.5)
NT = (((1,), (1,)), ((), ()))
TN = (((0,), (0,)), ((), ()))


def dot(a, b, dims=(((1,), (0,)), ((), ()))):
    return lax.dot_general(a, b, dims, preferred_element_type=F32)


def after(a, other):
    return lax.optimization_barrier((a, other))[0]


def swap(a, bit):
    return lax.ppermute(a, "tensor", [(i, i ^ bit) for i in range(4)])


def fill_bias(segc_ref, segr_ref, bias_ref, blocks):
    off = 0
    for i in range(blocks):
        keys = (i + 1) * QB
        kpos = lax.broadcasted_iota(jnp.int32, (keys, QB), 0)
        qpos = lax.broadcasted_iota(jnp.int32, (keys, QB), 1) + i * QB
        same = segc_ref[:keys, :] == segr_ref[:, i * QB : (i + 1) * QB]
        allowed = jnp.logical_and(kpos <= qpos, same)
        bias_ref[off : off + keys, :] = jnp.where(allowed, 0.0, -1e30)
        off += keys


def half_masks():
    lane = lax.broadcasted_iota(jnp.int32, (1, PAIR), 1)
    return (lane < HD, lane >= HD)


def attn_fwd_kernel(blocks, segc_ref, segr_ref, q_ref, k_ref, v_ref, o_ref, bias_ref):
    @pl.when(pl.program_id(0) == 0)
    def _():
        fill_bias(segc_ref, segr_ref, bias_ref, blocks)

    masks = half_masks()
    vt = v_ref[...].T
    off = 0
    for i in range(blocks):
        keys = (i + 1) * QB
        qi = q_ref[i * QB : (i + 1) * QB, :] * jnp.asarray(SCALE, BF)
        outs = []
        for h in range(2):
            qm = jnp.where(masks[h], qi, jnp.zeros_like(qi))
            s = dot(k_ref[:keys, :], qm, NT) + bias_ref[off : off + keys, :]
            e = jnp.exp(s - jnp.max(s, axis=0, keepdims=True))
            total = jnp.sum(e, axis=0, keepdims=True)
            o = dot(vt[h * HD : (h + 1) * HD, :keys], e.astype(BF))
            outs.append(o * (1.0 / total))
        o_ref[i * QB : (i + 1) * QB, :] = jnp.concatenate(outs, axis=0).T.astype(BF)
        off += keys


def attn_fwd(qkv, segc, segr):
    rows, cols = qkv.shape
    pairs = cols // 3 // PAIR
    blocks = rows // QB

    def col(base):
        return pl.BlockSpec((rows, PAIR), lambda p: (0, base * pairs + p))

    return pl.pallas_call(
        functools.partial(attn_fwd_kernel, blocks),
        grid=(pairs,),
        in_specs=[
            pl.BlockSpec((rows, 1), lambda p: (0, 0)),
            pl.BlockSpec((1, rows), lambda p: (0, 0)),
            col(0),
            col(1),
            col(2),
        ],
        out_specs=pl.BlockSpec((rows, PAIR), lambda p: (0, p)),
        out_shape=jax.ShapeDtypeStruct((rows, cols // 3), BF),
        scratch_shapes=[pltpu.VMEM((QB * blocks * (blocks + 1) // 2, QB), F32)],
        compiler_params=pltpu.CompilerParams(vmem_limit_bytes=48 << 20),
        cost_estimate=pl.CostEstimate(
            flops=8 * pairs * rows * rows * HD,
            bytes_accessed=qkv.size * 4,
            transcendentals=pairs * rows * rows,
        ),
        name="attn_fwd",
    )(segc, segr, qkv, qkv, qkv)


def attn_bwd_kernel(
    blocks, pairs, segc_ref, segr_ref, q_ref, k_ref, v_ref, g_ref, d_ref, sum_ref, bias_ref, dk_ref, dv_ref
):
    p_id = pl.program_id(0)

    @pl.when(p_id == 0)
    def _():
        fill_bias(segc_ref, segr_ref, bias_ref, blocks)

    def place(base):
        return pl.ds(pl.multiple_of((base * pairs + p_id) * PAIR, PAIR), PAIR)

    masks = half_masks()
    kt = k_ref[...].T
    dk_ref[...] = jnp.zeros_like(dk_ref)
    dv_ref[...] = jnp.zeros_like(dv_ref)
    off = 0
    qsum = jnp.zeros((1, PAIR), F32)
    for i in range(blocks):
        keys = (i + 1) * QB
        rows = slice(i * QB, (i + 1) * QB)
        qi = q_ref[rows, :] * jnp.asarray(SCALE, BF)
        gi = g_ref[rows, :]
        outs = []
        for h in range(2):
            qm = jnp.where(masks[h], qi, jnp.zeros_like(qi))
            gm = jnp.where(masks[h], gi, jnp.zeros_like(gi))
            s = dot(k_ref[:keys, :], qm, NT) + bias_ref[off : off + keys, :]
            e = jnp.exp(s - jnp.max(s, axis=0, keepdims=True))
            prob = e * (1.0 / jnp.sum(e, axis=0, keepdims=True))
            weighted = prob * dot(v_ref[:keys, :], gm, NT)
            ds = (weighted - prob * jnp.sum(weighted, axis=0, keepdims=True)).astype(BF)
            dv_ref[:keys, :] += dot(prob.astype(BF), gm)
            dk_ref[:keys, :] += dot(ds, qm)
            outs.append(dot(kt[h * HD : (h + 1) * HD, :keys], ds))
        dq = (jnp.concatenate(outs, axis=0).T * SCALE).astype(BF)
        d_ref[rows, place(0)] = dq
        qsum += jnp.sum(dq.astype(F32), axis=0, keepdims=True)
        off += keys
    dv = dv_ref[...].astype(BF)
    d_ref[:, place(1)] = dk_ref[...].astype(BF)
    d_ref[:, place(2)] = dv
    at = pl.ds(pl.multiple_of(p_id * PAIR, PAIR), PAIR)
    sum_ref[0:1, at] = qsum
    sum_ref[1:2, at] = jnp.sum(dv.astype(F32), axis=0, keepdims=True)


def attn_bwd(qkv, grad, segc, segr):
    rows, cols = qkv.shape
    pairs = cols // 3 // PAIR
    blocks = rows // QB

    def col(base):
        return pl.BlockSpec((rows, PAIR), lambda p: (0, base * pairs + p))

    return pl.pallas_call(
        functools.partial(attn_bwd_kernel, blocks, pairs),
        grid=(pairs,),
        in_specs=[
            pl.BlockSpec((rows, 1), lambda p: (0, 0)),
            pl.BlockSpec((1, rows), lambda p: (0, 0)),
            col(0),
            col(1),
            col(2),
            col(0),
        ],
        out_specs=[
            pl.BlockSpec((rows, cols), lambda p: (0, 0)),
            pl.BlockSpec((2, cols // 3), lambda p: (0, 0)),
        ],
        out_shape=[
            jax.ShapeDtypeStruct((rows, cols), BF),
            jax.ShapeDtypeStruct((2, cols // 3), F32),
        ],
        scratch_shapes=[
            pltpu.VMEM((QB * blocks * (blocks + 1) // 2, QB), F32),
            pltpu.VMEM((rows, PAIR), F32),
            pltpu.VMEM((rows, PAIR), F32),
        ],
        compiler_params=pltpu.CompilerParams(vmem_limit_bytes=48 << 20),
        cost_estimate=pl.CostEstimate(
            flops=24 * pairs * rows * rows * HD,
            bytes_accessed=qkv.size * 6,
            transcendentals=pairs * rows * rows,
        ),
        name="attn_bwd",
    )(segc, segr, qkv, qkv, qkv, grad)


GA = 0.7978845608028654
GB = 0.044715


def ff_kernel(
    half, n_a, n_b, g_a, g_b, we_ref, wr_ref, be_ref, _act, _pg, act_ref, pg_ref, branch_ref, ng_ref, sum_ref
):
    i = pl.program_id(0)
    first = i < half
    rows = jnp.where(first, n_a[...], n_b[...])
    grads = jnp.where(first, g_a[...], g_b[...])
    u = dot(rows, we_ref[...]) + be_ref[...]
    act_grad = dot(grads, wr_ref[...], NT)
    sq = u * u
    th = jnp.tanh(u * (GA + (GA * GB) * sq))
    cdf = 0.5 * (1.0 + th)
    act = (u * cdf).astype(BF)
    slope = cdf + (0.5 * u) * (1.0 - th * th) * (GA + (3.0 * GA * GB) * sq)
    pre = (act_grad * slope).astype(BF)
    act_ref[...] = act
    pg_ref[...] = pre
    branch_ref[...] = dot(act, wr_ref[...]).astype(BF)
    ng_ref[...] = dot(pre, we_ref[...], NT).astype(BF)

    @pl.when(i == 0)
    def _():
        sum_ref[...] = jnp.zeros_like(sum_ref)

    sum_ref[...] += jnp.sum(pre.astype(F32), axis=0, keepdims=True)


def ff_part(part, n_a, n_b, g_a, g_b, we, wr, be, act, pg):
    rows, width = n_a.shape
    units = we.shape[1]
    block = 256
    half = rows // block
    base = 2 * half * part

    def lo():
        return pl.BlockSpec((block, width), lambda i: (jnp.minimum(i, half - 1), 0))

    def hi():
        return pl.BlockSpec((block, width), lambda i: (jnp.maximum(i - half, 0), 0))

    def whole(a):
        return pl.BlockSpec(a.shape, lambda i: (0, 0), pipeline_mode=pl.Buffered(1))

    here = pl.BlockSpec((block, units), lambda i: (i + base, 0))
    out = pl.BlockSpec((block, width), lambda i: (i, 0))
    return pl.pallas_call(
        functools.partial(ff_kernel, half),
        grid=(2 * half,),
        in_specs=[
            lo(),
            hi(),
            lo(),
            hi(),
            whole(we),
            whole(wr),
            whole(be),
            pl.BlockSpec(memory_space=pl.ANY),
            pl.BlockSpec(memory_space=pl.ANY),
        ],
        out_specs=[here, here, out, out, pl.BlockSpec((1, units), lambda i: (0, 0))],
        out_shape=[
            jax.ShapeDtypeStruct(act.shape, BF),
            jax.ShapeDtypeStruct(pg.shape, BF),
            jax.ShapeDtypeStruct((2 * rows, width), BF),
            jax.ShapeDtypeStruct((2 * rows, width), BF),
            jax.ShapeDtypeStruct((1, units), F32),
        ],
        input_output_aliases={7: 0, 8: 1},
        compiler_params=pltpu.CompilerParams(vmem_limit_bytes=52 << 20),
        cost_estimate=pl.CostEstimate(
            flops=16 * rows * width * units,
            bytes_accessed=4 * width * units + 20 * rows * width,
            transcendentals=2 * rows * units,
        ),
        name="ff_part",
    )(n_a, n_b, g_a, g_b, we, wr, be, act, pg)


MESH_ID = pl.DeviceIdType.MESH


def ring_kernel(
    n, x_ref, small_ref, r_ref, e_ref, xo_ref, so_ref, ro_ref, eo_ref, xbuf, sbuf, send, recv, local
):
    half = n // 2
    mine = lax.axis_index("dp")
    odd = mine % 2
    pos = (1 - odd) * (mine // 2) + odd * (n - 1 - mine // 2)

    def index_of(at):
        at = (at + 2 * n) % n
        far = at // half
        return (1 - far) * 2 * at + far * (2 * (n - 1 - at) + 1)

    sides = (index_of(pos + 1), index_of(pos - 1))
    barrier = pltpu.get_barrier_semaphore()
    for side in sides:
        pl.semaphore_signal(barrier, inc=1, device_id={"dp": side}, device_id_type=MESH_ID)
    pl.semaphore_wait(barrier, 2)

    def remote(src, dst, kind, d, s):
        return pltpu.make_async_remote_copy(
            src_ref=src,
            dst_ref=dst,
            send_sem=send.at[kind, d],
            recv_sem=recv.at[kind, d, s],
            device_id={"dp": sides[d]},
            device_id_type=MESH_ID,
        )

    def gather(out, kind, d, s):
        chunk = index_of(pos - s if d == 0 else pos + s)
        return remote(out.at[chunk, d], out.at[chunk, d], kind, d, s)

    def gather_small(s):
        chunk = index_of(pos - s)
        return remote(so_ref.at[chunk], so_ref.at[chunk], 5, 0, s)

    def part(d, s):
        return index_of(pos - 1 - s if d == 0 else pos + 1 + s)

    def reduce_first(d):
        return remote(x_ref.at[part(d, 0), d], xbuf.at[0, d], 0, d, 0)

    def reduce_next(d, s):
        return remote(xbuf.at[s - 1, d], xbuf.at[s, d], 0, d, s)

    def small_first():
        return remote(small_ref.at[part(0, 0)], sbuf.at[0], 4, 0, 0)

    def small_next(s):
        return remote(sbuf.at[s - 1], sbuf.at[s], 4, 0, s)

    def add(d, s):
        chunk = part(d, s + 1)
        xbuf[s, d] = (xbuf[s, d].astype(F32) + x_ref[chunk, d].astype(F32)).astype(BF)

    def add_small(s):
        sbuf[s] = sbuf[s] + small_ref[part(0, s + 1)]

    own_r = pltpu.make_async_copy(r_ref, ro_ref.at[mine], local.at[0])
    own_e = pltpu.make_async_copy(e_ref, eo_ref.at[mine], local.at[1])
    own_r.start()
    own_e.start()
    for d in range(2):
        reduce_first(d).start()
    small_first().start()
    own_r.wait()
    own_e.wait()
    for d in range(2):
        gather(ro_ref, 1, d, 0).start()

    @pl.loop(1, n - 1)
    def _(s):
        for d in range(2):
            reduce_first(d).wait_send()
            remote(xbuf.at[s - 1, d], xbuf.at[s - 1, d], 0, d, s - 1).wait_recv()
            add(d, s - 1)
            reduce_next(d, s).start()
        small_first().wait_send()
        remote(sbuf.at[s - 1], sbuf.at[s - 1], 4, 0, s - 1).wait_recv()
        add_small(s - 1)
        small_next(s).start()
        for d in range(2):
            gather(ro_ref, 1, d, s - 1).wait()
            gather(ro_ref, 1, d, s).start()

    last = n - 2
    for d in range(2):
        reduce_first(d).wait_send()
        remote(xbuf.at[last, d], xbuf.at[last, d], 0, d, last).wait_recv()
        add(d, last)
    small_first().wait_send()
    remote(sbuf.at[last], sbuf.at[last], 4, 0, last).wait_recv()
    add_small(last)
    own_x = pltpu.make_async_copy(xbuf.at[last], xo_ref.at[mine], local.at[0])
    own_s = pltpu.make_async_copy(sbuf.at[last], so_ref.at[mine], local.at[1])
    own_x.start()
    own_s.start()
    for d in range(2):
        gather(ro_ref, 1, d, last).wait()
        gather(eo_ref, 2, d, 0).start()
    own_x.wait()
    own_s.wait()
    for d in range(2):
        gather(xo_ref, 3, d, 0).start()
    gather_small(0).start()

    @pl.loop(1, n - 1)
    def _(s):
        for d in range(2):
            gather(eo_ref, 2, d, s - 1).wait()
            gather(eo_ref, 2, d, s).start()
        for d in range(2):
            gather(xo_ref, 3, d, s - 1).wait()
            gather(xo_ref, 3, d, s).start()
        gather_small(s - 1).wait()
        gather_small(s).start()

    for d in range(2):
        gather(eo_ref, 2, d, last).wait()
        gather(xo_ref, 3, d, last).wait()
    gather_small(last).wait()


def ring_sum(x, small, r_own, e_own, n):
    rows, width = x.shape
    h = rows // (2 * n)
    m = small.size // n
    full = jax.ShapeDtypeStruct((n, 2, h, width), BF)
    vmem = pl.BlockSpec(memory_space=pltpu.VMEM)
    anyspace = pl.BlockSpec(memory_space=pl.ANY)
    xo, so, ro, eo = pl.pallas_call(
        functools.partial(ring_kernel, n),
        in_specs=[vmem, vmem, anyspace, anyspace],
        out_specs=[anyspace] * 4,
        out_shape=[full, jax.ShapeDtypeStruct((n, 1, m), F32), full, full],
        scratch_shapes=[
            pltpu.VMEM((n - 1, 2, h, width), BF),
            pltpu.VMEM((n - 1, 1, m), F32),
            pltpu.SemaphoreType.DMA((6, 2)),
            pltpu.SemaphoreType.DMA((6, 2, n - 1)),
            pltpu.SemaphoreType.DMA((2,)),
        ],
        compiler_params=pltpu.CompilerParams(
            collective_id=1, has_side_effects=True, vmem_limit_bytes=32 << 20
        ),
        name="ring_sum",
    )(
        x.reshape(n, 2, h, width),
        small.reshape(n, 1, m),
        r_own.reshape(2, h, width),
        e_own.reshape(2, h, width),
    )
    flat = (rows, width)
    return xo.reshape(flat), so.reshape(small.shape), ro.reshape(flat), eo.reshape(flat)


def norm_stats(values):
    mean = jnp.mean(values, axis=-1, keepdims=True)
    centered = values - mean
    variance = jnp.mean(centered * centered, axis=-1, keepdims=True)
    scale = lax.rsqrt(variance + EPS)
    return centered * scale, scale


def norm_back(grad, gain, normed, scale):
    g = grad * gain
    inner = g - jnp.mean(g, axis=-1, keepdims=True)
    inner = inner - normed * jnp.mean(g * normed, axis=-1, keepdims=True)
    return scale * inner, jnp.sum(grad * normed, axis=0), jnp.sum(grad, axis=0)


def body(
    block_in,
    segments,
    first_gain,
    first_shift,
    w_qkv,
    qv_bias,
    w_mix,
    mix_bias,
    second_gain,
    second_shift,
    w_expand,
    expand_bias,
    w_reduce,
    reduce_bias,
    out_grad,
):
    rows, width = block_in.shape
    cols = w_qkv.shape[2]
    units = w_expand.shape[1]
    place = lax.axis_index("tensor")
    core = place % 2
    seg = lax.dynamic_slice_in_dim(segments, place // 2, 1, 0)
    segc = seg.reshape(-1, 1)

    def in_order(own, other):
        return jnp.where(
            core == 0,
            jnp.concatenate([own, other], axis=0),
            jnp.concatenate([other, own], axis=0),
        )

    def own_rows(a):
        return lax.dynamic_slice_in_dim(a, core * rows, rows, 0)

    def other_rows(a):
        return lax.dynamic_slice_in_dim(a, (1 - core) * rows, rows, 0)

    dp_size = lax.axis_size("dp")
    dp_place = lax.axis_index("dp")

    wq = w_qkv.reshape(width, 3 * cols)
    top = width // 2
    mid = cols // 2
    near_half = jnp.concatenate([wq[:top], w_mix[:mid].reshape(top, cols)], axis=1)
    slice_rows = top // dp_size
    far_half = jnp.concatenate(
        [
            lax.dynamic_slice_in_dim(wq, top + dp_place * slice_rows, slice_rows, 0),
            lax.dynamic_slice_in_dim(
                w_mix[mid:].reshape(top, cols), dp_place * slice_rows, slice_rows, 0
            ),
        ],
        axis=1,
    )
    piece = swap(far_half, 2)
    low = lax.all_gather(piece, "dp", axis=0, tiled=True)
    near_half = after(near_half, piece)
    high = swap(near_half, 2)
    qb_far = swap(qv_bias, 2)
    wq_far = jnp.concatenate([high[:, : 3 * cols], low[:, : 3 * cols]], axis=0)
    wm_far = jnp.concatenate(
        [high[:, 3 * cols :].reshape(mid, width), low[:, 3 * cols :].reshape(mid, width)], axis=0
    )

    x = block_in.astype(F32)
    norm1, scale1 = norm_stats(x)
    n1 = (norm1 * first_gain + first_shift).astype(BF)
    rows1 = in_order(n1, swap(n1, 1))

    def project(w, b):
        bias = jnp.concatenate([b[0], jnp.zeros_like(b[0]), b[1]])
        return (dot(rows1, w) + bias).astype(BF)

    qkv_a = project(wq, qv_bias)
    att_a = attn_fwd(qkv_a, segc, seg)
    wq_far, att_a, wm_far = lax.optimization_barrier((wq_far, att_a, wm_far))
    qkv_b = project(wq_far, qb_far)
    att_b = attn_fwd(qkv_b, segc, seg)

    part = dot(other_rows(att_a), w_mix) + dot(other_rows(att_b), wm_far)
    got = swap(part.astype(BF), 1)
    mixed = dot(own_rows(att_a), w_mix) + dot(own_rows(att_b), wm_far) + got.astype(F32) + mix_bias
    resid = x + mixed
    norm2, scale2 = norm_stats(resid)
    n2 = (norm2 * second_gain + second_shift).astype(BF)

    og_s = swap(out_grad, 1)
    og_y = swap(after(out_grad, high), 2)
    og_d = swap(og_y, 1)

    n2_y = swap(n2, 2)
    n2_s = swap(n2, 1)

    be = expand_bias.reshape(1, units)
    act = jnp.zeros((4 * rows, units), BF)
    pg = jnp.zeros((4 * rows, units), BF)
    act, pg, br0, ng0, sum0 = ff_part(0, n2, n2_s, out_grad, og_s, w_expand, w_reduce, be, act, pg)
    n2_y, og_y, og_d, act = lax.optimization_barrier((n2_y, og_y, og_d, act))
    n2_d = swap(n2_y, 1)
    act, pg, br1, ng1, sum1 = ff_part(1, n2_y, n2_d, og_y, og_d, w_expand, w_reduce, be, act, pg)

    def across(far):
        return (far[:rows].astype(F32) + swap(far[rows:], 1).astype(F32)).astype(BF)

    def near_sum(near):
        return near[:rows].astype(F32) + swap(near[rows:], 1).astype(F32)

    ng_got = swap(across(ng1), 2)
    br_got = swap(after(across(br1), ng_got), 2)

    grads_all = jnp.concatenate([out_grad, og_s, og_y, og_d], axis=0)
    n2_all = jnp.concatenate([n2, n2_s, n2_y, n2_d], axis=0)
    reduce_grad = dot(act, grads_all, TN).astype(BF)
    reduce_own = lax.psum_scatter(reduce_grad, "dp", scatter_dimension=0, tiled=True)
    expand_grad = dot(n2_all, pg, TN).astype(BF)
    expand_own = lax.psum_scatter(expand_grad, "dp", scatter_dimension=0, tiled=True)
    expand_bias_grad = (sum0 + sum1)[0]

    ng_got, reduce_grad, expand_grad = lax.optimization_barrier((ng_got, reduce_grad, expand_grad))
    ng = near_sum(ng0) + ng_got.astype(F32)
    grad = out_grad.astype(F32)
    reduce_bias_grad = jnp.sum(grad, axis=0)
    back2, second_gain_grad, second_shift_grad = norm_back(ng, second_gain, norm2, scale2)
    resid_grad = grad + back2
    mg = resid_grad.astype(BF)
    mix_bias_grad = jnp.sum(mg.astype(F32), axis=0)

    mg_all = in_order(mg, swap(mg, 1))
    ag_b = dot(mg_all, wm_far, NT).astype(BF)
    dqkv_b, sums_b = attn_bwd(qkv_b, ag_b, segc, seg)
    qkv_grad_b = dot(rows1, dqkv_b, TN).astype(BF)
    mix_grad_b = dot(att_b, mg_all, TN).astype(BF)
    mix_back = swap(mix_grad_b, 2)
    qkv_back = swap(qkv_grad_b, 2)
    sums_back = swap(sums_b, 2)
    ag_a = dot(after(mg_all, qkv_grad_b), w_mix, NT).astype(BF)
    dqkv_a, sums_a = attn_bwd(qkv_a, ag_a, segc, seg)
    qkv_back, mix_back, dqkv_a, br_got = lax.optimization_barrier((qkv_back, mix_back, dqkv_a, br_got))

    branch = near_sum(br0) + br_got.astype(F32)
    block_out = (resid + branch + reduce_bias).astype(BF)

    n1g_other = dot(other_rows(dqkv_b), wq_far, NT) + dot(other_rows(dqkv_a), wq, NT)
    n1g_got = swap(n1g_other.astype(BF), 1)
    n1g = dot(own_rows(dqkv_b), wq_far, NT) + dot(own_rows(dqkv_a), wq, NT) + n1g_got.astype(F32)
    back1, first_gain_grad, first_shift_grad = norm_back(n1g, first_gain, norm1, scale1)
    in_grad = resid_grad + back1

    def over_tensor(parts):
        a = jnp.stack(parts)
        a = a + swap(a, 1)
        return a + swap(a, 2)

    early = over_tensor([mix_bias_grad, second_gain_grad, second_shift_grad, reduce_bias_grad])
    late = over_tensor([first_gain_grad, first_shift_grad])

    mix_grad = (dot(att_a, mg_all, TN) + mix_back.astype(F32)).astype(BF)
    qkv_grad = (dot(rows1, dqkv_a, TN) + qkv_back.astype(F32)).astype(BF)
    packed = jnp.concatenate([qkv_grad, mix_grad.reshape(width, cols)], axis=1)
    qv_bias_grad = (sums_a + sums_back).reshape(1, 2 * cols)
    small = jnp.concatenate(
        [
            late,
            early,
            expand_bias_grad.reshape(1, units),
            jnp.pad(qv_bias_grad, ((0, 0), (0, width - 2 * cols))),
        ],
        axis=0,
    )
    packed, small, reduce_all, expand_all = ring_sum(packed, small, reduce_own, expand_own, dp_size)
    return (
        block_out,
        in_grad,
        small[0],
        small[1],
        packed[:, : 3 * cols].astype(F32).reshape(width, 3, cols),
        small[7, : 2 * cols].reshape(2, cols),
        packed[:, 3 * cols :].astype(F32).reshape(cols, width),
        small[2],
        small[3],
        small[4],
        expand_all.astype(F32),
        small[6],
        reduce_all.astype(F32),
        small[5],
    )


def solution(mesh):
    both = P(("dp", "tensor"), None)
    return jax.shard_map(
        body,
        mesh=mesh,
        in_specs=(
            both,
            P("dp", None),
            P(),
            P(),
            P(None, None, "tensor"),
            P(None, "tensor"),
            P("tensor", None),
            P(),
            P(),
            P(),
            P(None, "tensor"),
            P("tensor"),
            P("tensor", None),
            P(),
            both,
        ),
        out_specs=(
            both,
            both,
            P(),
            P(),
            P(None, None, "tensor"),
            P(None, "tensor"),
            P("tensor", None),
            P(),
            P(),
            P(),
            P(None, "tensor"),
            P("tensor"),
            P("tensor", None),
            P(),
        ),
        check_vma=False,
    )
```

```python
import functools

import jax
import jax.numpy as jnp
from jax import lax
from jax.experimental import pallas as pl
from jax.experimental.pallas import tpu as pltpu
from jax.sharding import PartitionSpec as P

HD = 64
PAIR = 2 * HD
QB = 256
EPS = 1e-5
BF = jnp.bfloat16
F32 = jnp.float32
SCALE = HD ** (-0.5)
MESH_ID = pl.DeviceIdType.MESH
NT = (((1,), (1,)), ((), ()))
TN = (((0,), (0,)), ((), ()))


def dot(a, b, dims=(((1,), (0,)), ((), ()))):
    return lax.dot_general(a, b, dims, preferred_element_type=F32)


def after(a, other):
    return lax.optimization_barrier((a, other))[0]


def swap(a, bit):
    return lax.ppermute(a, "tensor", [(i, i ^ bit) for i in range(4)])


def fill_bias(segc_ref, segr_ref, bias_ref, blocks):
    off = 0
    for i in range(blocks):
        keys = (i + 1) * QB
        kpos = lax.broadcasted_iota(jnp.int32, (keys, QB), 0)
        qpos = lax.broadcasted_iota(jnp.int32, (keys, QB), 1) + i * QB
        same = segc_ref[:keys, :] == segr_ref[:, i * QB : (i + 1) * QB]
        allowed = jnp.logical_and(kpos <= qpos, same)
        bias_ref[off : off + keys, :] = jnp.where(allowed, 0.0, -1e30)
        off += keys


def half_masks():
    lane = lax.broadcasted_iota(jnp.int32, (1, PAIR), 1)
    return (lane < HD, lane >= HD)


def attn_fwd_kernel(blocks, segc_ref, segr_ref, q_ref, k_ref, v_ref, o_ref, bias_ref):
    @pl.when(pl.program_id(0) == 0)
    def _():
        fill_bias(segc_ref, segr_ref, bias_ref, blocks)

    masks = half_masks()
    vt = v_ref[...].T
    off = 0
    for i in range(blocks):
        keys = (i + 1) * QB
        qi = q_ref[i * QB : (i + 1) * QB, :] * jnp.asarray(SCALE, BF)
        outs = []
        for h in range(2):
            qm = jnp.where(masks[h], qi, jnp.zeros_like(qi))
            s = dot(k_ref[:keys, :], qm, NT) + bias_ref[off : off + keys, :]
            e = jnp.exp(s - jnp.max(s, axis=0, keepdims=True))
            total = jnp.sum(e, axis=0, keepdims=True)
            o = dot(vt[h * HD : (h + 1) * HD, :keys], e.astype(BF))
            outs.append(o * (1.0 / total))
        o_ref[i * QB : (i + 1) * QB, :] = jnp.concatenate(outs, axis=0).T.astype(BF)
        off += keys


def attn_fwd(qkv, segc, segr):
    rows, cols = qkv.shape
    pairs = cols // 3 // PAIR
    blocks = rows // QB

    def col(base):
        return pl.BlockSpec((rows, PAIR), lambda p: (0, base * pairs + p))

    return pl.pallas_call(
        functools.partial(attn_fwd_kernel, blocks),
        grid=(pairs,),
        in_specs=[
            pl.BlockSpec((rows, 1), lambda p: (0, 0)),
            pl.BlockSpec((1, rows), lambda p: (0, 0)),
            col(0),
            col(1),
            col(2),
        ],
        out_specs=pl.BlockSpec((rows, PAIR), lambda p: (0, p)),
        out_shape=jax.ShapeDtypeStruct((rows, cols // 3), BF),
        scratch_shapes=[pltpu.VMEM((QB * blocks * (blocks + 1) // 2, QB), F32)],
        compiler_params=pltpu.CompilerParams(vmem_limit_bytes=48 << 20),
        cost_estimate=pl.CostEstimate(
            flops=8 * pairs * rows * rows * HD,
            bytes_accessed=qkv.size * 4,
            transcendentals=pairs * rows * rows,
        ),
        name="attn_fwd",
    )(segc, segr, qkv, qkv, qkv)


def attn_bwd_kernel(
    blocks, pairs, segc_ref, segr_ref, q_ref, k_ref, v_ref, g_ref, d_ref, sum_ref, bias_ref, dk_ref, dv_ref
):
    p_id = pl.program_id(0)

    @pl.when(p_id == 0)
    def _():
        fill_bias(segc_ref, segr_ref, bias_ref, blocks)

    def place(base):
        return pl.ds(pl.multiple_of((base * pairs + p_id) * PAIR, PAIR), PAIR)

    masks = half_masks()
    kt = k_ref[...].T
    dk_ref[...] = jnp.zeros_like(dk_ref)
    dv_ref[...] = jnp.zeros_like(dv_ref)
    off = 0
    qsum = jnp.zeros((1, PAIR), F32)
    for i in range(blocks):
        keys = (i + 1) * QB
        rows = slice(i * QB, (i + 1) * QB)
        qi = q_ref[rows, :] * jnp.asarray(SCALE, BF)
        gi = g_ref[rows, :]
        outs = []
        for h in range(2):
            qm = jnp.where(masks[h], qi, jnp.zeros_like(qi))
            gm = jnp.where(masks[h], gi, jnp.zeros_like(gi))
            s = dot(k_ref[:keys, :], qm, NT) + bias_ref[off : off + keys, :]
            e = jnp.exp(s - jnp.max(s, axis=0, keepdims=True))
            prob = e * (1.0 / jnp.sum(e, axis=0, keepdims=True))
            weighted = prob * dot(v_ref[:keys, :], gm, NT)
            ds = (weighted - prob * jnp.sum(weighted, axis=0, keepdims=True)).astype(BF)
            dv_ref[:keys, :] += dot(prob.astype(BF), gm)
            dk_ref[:keys, :] += dot(ds, qm)
            outs.append(dot(kt[h * HD : (h + 1) * HD, :keys], ds))
        dq = (jnp.concatenate(outs, axis=0).T * SCALE).astype(BF)
        d_ref[rows, place(0)] = dq
        qsum += jnp.sum(dq.astype(F32), axis=0, keepdims=True)
        off += keys
    dv = dv_ref[...].astype(BF)
    d_ref[:, place(1)] = dk_ref[...].astype(BF)
    d_ref[:, place(2)] = dv
    at = pl.ds(pl.multiple_of(p_id * PAIR, PAIR), PAIR)
    sum_ref[0:1, at] = qsum
    sum_ref[1:2, at] = jnp.sum(dv.astype(F32), axis=0, keepdims=True)


def attn_bwd(qkv, grad, segc, segr):
    rows, cols = qkv.shape
    pairs = cols // 3 // PAIR
    blocks = rows // QB

    def col(base):
        return pl.BlockSpec((rows, PAIR), lambda p: (0, base * pairs + p))

    return pl.pallas_call(
        functools.partial(attn_bwd_kernel, blocks, pairs),
        grid=(pairs,),
        in_specs=[
            pl.BlockSpec((rows, 1), lambda p: (0, 0)),
            pl.BlockSpec((1, rows), lambda p: (0, 0)),
            col(0),
            col(1),
            col(2),
            col(0),
        ],
        out_specs=[
            pl.BlockSpec((rows, cols), lambda p: (0, 0)),
            pl.BlockSpec((2, cols // 3), lambda p: (0, 0)),
        ],
        out_shape=[
            jax.ShapeDtypeStruct((rows, cols), BF),
            jax.ShapeDtypeStruct((2, cols // 3), F32),
        ],
        scratch_shapes=[
            pltpu.VMEM((QB * blocks * (blocks + 1) // 2, QB), F32),
            pltpu.VMEM((rows, PAIR), F32),
            pltpu.VMEM((rows, PAIR), F32),
        ],
        compiler_params=pltpu.CompilerParams(vmem_limit_bytes=48 << 20),
        cost_estimate=pl.CostEstimate(
            flops=24 * pairs * rows * rows * HD,
            bytes_accessed=qkv.size * 6,
            transcendentals=pairs * rows * rows,
        ),
        name="attn_bwd",
    )(segc, segr, qkv, qkv, qkv, grad)


GA = 0.7978845608028654
GB = 0.044715


def ff_kernel(
    n2_ref, og_ref, we_ref, wr_ref, be_ref, resid_ref, gain_ref,
    rgrad_ref, mg_ref, rg_ref, eg_ref, brn_ref, brf_ref, usum_ref, dsum_ref,
    n2b, act, pg, ng, br, ng_d, br_d, ng_s, br_s, ng_far, ng_out,
    send, recv,
):
    rows, width = n2_ref.shape
    units = we_ref.shape[1]
    part = rows // 2
    nb = 256
    me = lax.axis_index("tensor")
    core = me % 2
    sib = me + 1 - 2 * core
    far = (me + 2) % 4

    barrier = pltpu.get_barrier_semaphore()
    for other in (sib, far):
        pl.semaphore_signal(barrier, inc=1, device_id={"tensor": other}, device_id_type=MESH_ID)
    pl.semaphore_wait(barrier, 2)

    def remote(src, dst, k, other):
        return pltpu.make_async_remote_copy(
            src_ref=src,
            dst_ref=dst,
            send_sem=send.at[k],
            recv_sem=recv.at[k],
            device_id={"tensor": other},
            device_id_type=MESH_ID,
        )

    def y_at(c):
        return pl.ds((2 + c) * rows, part)

    def d_at(c):
        return pl.ds((2 + c) * rows + part, part)

    def rows_across(c):
        return remote(n2_ref.at[pl.ds(c * part, part)], n2b.at[y_at(c)], c, far)

    def rows_beside():
        return remote(n2_ref, n2b.at[pl.ds(rows, rows)], 2, sib)

    def rows_forward(c):
        return remote(n2b.at[y_at(c)], n2b.at[d_at(c)], 3 + c, sib)

    def ng_beside():
        return remote(ng.at[pl.ds(rows, rows)], ng_s, 5, sib)

    def br_beside():
        return remote(br.at[pl.ds(rows, rows)], br_s, 6, sib)

    def ng_combine(c):
        return remote(ng.at[d_at(c)], ng_d.at[c], 7 + c, sib)

    def br_combine(c):
        return remote(br.at[d_at(c)], br_d.at[c], 9 + c, sib)

    def ng_across(c):
        return remote(ng_out.at[c], ng_far.at[c], 11 + c, far)

    def mg_beside(c):
        at = pl.ds(pl.multiple_of(core * rows + c * part, part), part)
        return remote(mg_ref.at[at], mg_ref.at[at], 13 + c, sib)

    for c in range(2):
        rows_across(c).start()
    rows_beside().start()
    n2b[0:rows, :] = n2_ref[...]
    usum_ref[...] = jnp.zeros_like(usum_ref)

    @pl.loop(0, 4)
    def _(b):
        at = pl.ds(pl.multiple_of(b * rows, rows), rows)
        c = b - 2

        @pl.when(b == 1)
        def _():
            rows_beside().wait()

        @pl.when(b >= 2)
        def _():
            rows_across(c).wait()
            rows_forward(c).start()
            rows_forward(c).wait()

        for k in range(units // nb):
            cols = slice(k * nb, (k + 1) * nb)
            u = dot(n2b[at, :], we_ref[:, cols]) + be_ref[:, cols]
            act_grad = dot(og_ref[at, :], wr_ref[cols, :], NT)
            sq = u * u
            th = jnp.tanh(u * (GA + (GA * GB) * sq))
            cdf = 0.5 * (1.0 + th)
            slope = cdf + (0.5 * u) * (1.0 - th * th) * (GA + (3.0 * GA * GB) * sq)
            pre = (act_grad * slope).astype(BF)
            act[at, cols] = (u * cdf).astype(BF)
            pg[at, cols] = pre
            usum_ref[:, cols] += jnp.sum(pre.astype(F32), axis=0, keepdims=True)
        for k in range(width // nb):
            cols = slice(k * nb, (k + 1) * nb)
            ng[at, cols] = dot(pg[at, :], we_ref[cols, :], NT).astype(BF)

        @pl.when(b == 1)
        def _():
            ng_beside().start()

        @pl.when(b >= 2)
        def _():
            ng_combine(c).start()

        for k in range(width // nb):
            cols = slice(k * nb, (k + 1) * nb)
            br[at, cols] = dot(act[at, :], wr_ref[:, cols]).astype(BF)

        @pl.when(b == 1)
        def _():
            br_beside().start()

        @pl.when(b >= 2)
        def _():
            br_combine(c).start()
            ng_combine(c).wait()
            ng_out[c] = (ng[y_at(c), :].astype(F32) + ng_d[c].astype(F32)).astype(BF)
            ng_across(c).start()

    @pl.loop(0, width // nb)
    def _(k):
        cols = pl.ds(pl.multiple_of(k * nb, nb), nb)
        rg_ref[:, cols] = dot(act[...], og_ref[:, cols], TN).astype(BF)
        eg_ref[:, cols] = dot(n2b[...], pg[:, cols], TN).astype(BF)

    br_beside().wait()
    brn_ref[...] = (br[0:rows, :].astype(F32) + br_s[...].astype(F32)).astype(BF)
    for c in range(2):
        br_combine(c).wait()
        brf_ref[c * part : (c + 1) * part, :] = (
            br[y_at(c), :].astype(F32) + br_d[c].astype(F32)
        ).astype(BF)
    ng_beside().wait()
    dsum_ref[...] = jnp.zeros_like(dsum_ref)
    step = 64
    for c in range(2):
        ng_across(c).wait()

        @pl.loop(0, part // step)
        def _(r):
            inner = pl.ds(pl.multiple_of(r * step, step), step)
            at = pl.ds(pl.multiple_of(c * part + r * step, step), step)
            grad = ng[at, :].astype(F32) + ng_s[at, :].astype(F32) + ng_far[c, inner, :].astype(F32)
            normed, scale = norm_stats(resid_ref[at, :])
            g = grad * gain_ref[...]
            gn = g * normed
            mean_g = jnp.mean(g, axis=-1, keepdims=True)
            mean_gn = jnp.mean(gn, axis=-1, keepdims=True)
            og = og_ref[at, :].astype(F32)
            rgrad = og + scale * (g - mean_g - normed * mean_gn)
            rgrad_ref[at, :] = rgrad
            mg = rgrad.astype(BF)
            mg_ref[pl.ds(pl.multiple_of(core * rows + c * part + r * step, step), step), :] = mg
            dsum_ref[0:1, :] += jnp.sum(mg.astype(F32), axis=0, keepdims=True)
            dsum_ref[1:2, :] += jnp.sum(grad * normed, axis=0, keepdims=True)
            dsum_ref[2:3, :] += jnp.sum(grad, axis=0, keepdims=True)
            dsum_ref[3:4, :] += jnp.sum(og, axis=0, keepdims=True)

        mg_beside(c).start()
    for c in range(2):
        mg_beside(c).wait()


def ff(n2, og_all, we, wr, be, resid, gain):
    rows, width = n2.shape
    units = we.shape[1]
    part = rows // 2
    vmem = pl.BlockSpec(memory_space=pltpu.VMEM)
    return pl.pallas_call(
        ff_kernel,
        in_specs=[vmem] * 7,
        out_specs=[vmem] * 8,
        out_shape=[
            jax.ShapeDtypeStruct((rows, width), F32),
            jax.ShapeDtypeStruct((2 * rows, width), BF),
            jax.ShapeDtypeStruct((units, width), BF),
            jax.ShapeDtypeStruct((width, units), BF),
            jax.ShapeDtypeStruct((rows, width), BF),
            jax.ShapeDtypeStruct((rows, width), BF),
            jax.ShapeDtypeStruct((1, units), F32),
            jax.ShapeDtypeStruct((4, width), F32),
        ],
        scratch_shapes=[
            pltpu.VMEM((4 * rows, width), BF),
            pltpu.VMEM((4 * rows, units), BF),
            pltpu.VMEM((4 * rows, units), BF),
            pltpu.VMEM((4 * rows, width), BF),
            pltpu.VMEM((4 * rows, width), BF),
            pltpu.VMEM((2, part, width), BF),
            pltpu.VMEM((2, part, width), BF),
            pltpu.VMEM((rows, width), BF),
            pltpu.VMEM((rows, width), BF),
            pltpu.VMEM((2, part, width), BF),
            pltpu.VMEM((2, part, width), BF),
            pltpu.SemaphoreType.DMA((15,)),
            pltpu.SemaphoreType.DMA((15,)),
        ],
        compiler_params=pltpu.CompilerParams(
            collective_id=2, has_side_effects=True, vmem_limit_bytes=60 << 20
        ),
        name="ff",
    )(n2, og_all, we, wr, be, resid, gain)


def ring_kernel(
    n, x_ref, small_ref, r_ref, e_ref, xo_ref, so_ref, ro_ref, eo_ref, xbuf, sbuf, send, recv, local
):
    half = n // 2
    mine = lax.axis_index("dp")
    odd = mine % 2
    pos = (1 - odd) * (mine // 2) + odd * (n - 1 - mine // 2)

    def index_of(at):
        at = (at + 2 * n) % n
        far = at // half
        return (1 - far) * 2 * at + far * (2 * (n - 1 - at) + 1)

    sides = (index_of(pos + 1), index_of(pos - 1))
    barrier = pltpu.get_barrier_semaphore()
    for side in sides:
        pl.semaphore_signal(barrier, inc=1, device_id={"dp": side}, device_id_type=MESH_ID)
    pl.semaphore_wait(barrier, 2)

    def remote(src, dst, kind, d, s):
        return pltpu.make_async_remote_copy(
            src_ref=src,
            dst_ref=dst,
            send_sem=send.at[kind, d],
            recv_sem=recv.at[kind, d, s],
            device_id={"dp": sides[d]},
            device_id_type=MESH_ID,
        )

    def gather(out, kind, d, s):
        chunk = index_of(pos - s if d == 0 else pos + s)
        return remote(out.at[chunk, d], out.at[chunk, d], kind, d, s)

    def gather_small(s):
        chunk = index_of(pos - s)
        return remote(so_ref.at[chunk], so_ref.at[chunk], 5, 0, s)

    def part(d, s):
        return index_of(pos - 1 - s if d == 0 else pos + 1 + s)

    def reduce_first(d):
        return remote(x_ref.at[part(d, 0), d], xbuf.at[0, d], 0, d, 0)

    def reduce_next(d, s):
        return remote(xbuf.at[s - 1, d], xbuf.at[s, d], 0, d, s)

    def small_first():
        return remote(small_ref.at[part(0, 0)], sbuf.at[0], 4, 0, 0)

    def small_next(s):
        return remote(sbuf.at[s - 1], sbuf.at[s], 4, 0, s)

    def add(d, s):
        chunk = part(d, s + 1)
        xbuf[s, d] = (xbuf[s, d].astype(F32) + x_ref[chunk, d].astype(F32)).astype(BF)

    def add_small(s):
        sbuf[s] = sbuf[s] + small_ref[part(0, s + 1)]

    own_r = pltpu.make_async_copy(r_ref, ro_ref.at[mine], local.at[0])
    own_e = pltpu.make_async_copy(e_ref, eo_ref.at[mine], local.at[1])
    own_r.start()
    own_e.start()
    for d in range(2):
        reduce_first(d).start()
    small_first().start()
    own_r.wait()
    own_e.wait()
    for d in range(2):
        gather(ro_ref, 1, d, 0).start()

    @pl.loop(1, n - 1)
    def _(s):
        for d in range(2):
            reduce_first(d).wait_send()
            remote(xbuf.at[s - 1, d], xbuf.at[s - 1, d], 0, d, s - 1).wait_recv()
            add(d, s - 1)
            reduce_next(d, s).start()
        small_first().wait_send()
        remote(sbuf.at[s - 1], sbuf.at[s - 1], 4, 0, s - 1).wait_recv()
        add_small(s - 1)
        small_next(s).start()
        for d in range(2):
            gather(ro_ref, 1, d, s - 1).wait()
            gather(ro_ref, 1, d, s).start()

    last = n - 2
    for d in range(2):
        reduce_first(d).wait_send()
        remote(xbuf.at[last, d], xbuf.at[last, d], 0, d, last).wait_recv()
        add(d, last)
    small_first().wait_send()
    remote(sbuf.at[last], sbuf.at[last], 4, 0, last).wait_recv()
    add_small(last)
    own_x = pltpu.make_async_copy(xbuf.at[last], xo_ref.at[mine], local.at[0])
    own_s = pltpu.make_async_copy(sbuf.at[last], so_ref.at[mine], local.at[1])
    own_x.start()
    own_s.start()
    for d in range(2):
        gather(ro_ref, 1, d, last).wait()
        gather(eo_ref, 2, d, 0).start()
    own_x.wait()
    own_s.wait()
    for d in range(2):
        gather(xo_ref, 3, d, 0).start()
    gather_small(0).start()

    @pl.loop(1, n - 1)
    def _(s):
        for d in range(2):
            gather(eo_ref, 2, d, s - 1).wait()
            gather(eo_ref, 2, d, s).start()
        for d in range(2):
            gather(xo_ref, 3, d, s - 1).wait()
            gather(xo_ref, 3, d, s).start()
        gather_small(s - 1).wait()
        gather_small(s).start()

    for d in range(2):
        gather(eo_ref, 2, d, last).wait()
        gather(xo_ref, 3, d, last).wait()
    gather_small(last).wait()


def ring_sum(x, small, r_own, e_own, n):
    rows, width = x.shape
    h = rows // (2 * n)
    m = small.size // n
    full = jax.ShapeDtypeStruct((n, 2, h, width), BF)
    vmem = pl.BlockSpec(memory_space=pltpu.VMEM)
    anyspace = pl.BlockSpec(memory_space=pl.ANY)
    xo, so, ro, eo = pl.pallas_call(
        functools.partial(ring_kernel, n),
        in_specs=[vmem, vmem, anyspace, anyspace],
        out_specs=[anyspace] * 4,
        out_shape=[full, jax.ShapeDtypeStruct((n, 1, m), F32), full, full],
        scratch_shapes=[
            pltpu.VMEM((n - 1, 2, h, width), BF),
            pltpu.VMEM((n - 1, 1, m), F32),
            pltpu.SemaphoreType.DMA((6, 2)),
            pltpu.SemaphoreType.DMA((6, 2, n - 1)),
            pltpu.SemaphoreType.DMA((2,)),
        ],
        compiler_params=pltpu.CompilerParams(
            collective_id=1, has_side_effects=True, vmem_limit_bytes=32 << 20
        ),
        name="ring_sum",
    )(
        x.reshape(n, 2, h, width),
        small.reshape(n, 1, m),
        r_own.reshape(2, h, width),
        e_own.reshape(2, h, width),
    )
    flat = (rows, width)
    return xo.reshape(flat), so.reshape(small.shape), ro.reshape(flat), eo.reshape(flat)


def norm_stats(values):
    mean = jnp.mean(values, axis=-1, keepdims=True)
    centered = values - mean
    variance = jnp.mean(centered * centered, axis=-1, keepdims=True)
    scale = lax.rsqrt(variance + EPS)
    return centered * scale, scale


def norm_back(grad, gain, normed, scale):
    g = grad * gain
    inner = g - jnp.mean(g, axis=-1, keepdims=True)
    inner = inner - normed * jnp.mean(g * normed, axis=-1, keepdims=True)
    return scale * inner, jnp.sum(grad * normed, axis=0), jnp.sum(grad, axis=0)


def body(
    block_in,
    segments,
    first_gain,
    first_shift,
    w_qkv,
    qv_bias,
    w_mix,
    mix_bias,
    second_gain,
    second_shift,
    w_expand,
    expand_bias,
    w_reduce,
    reduce_bias,
    out_grad,
):
    rows, width = block_in.shape
    cols = w_qkv.shape[2]
    units = w_expand.shape[1]
    place = lax.axis_index("tensor")
    core = place % 2
    seg = lax.dynamic_slice_in_dim(segments, place // 2, 1, 0)
    segc = seg.reshape(-1, 1)

    def in_order(own, other):
        return jnp.where(
            core == 0,
            jnp.concatenate([own, other], axis=0),
            jnp.concatenate([other, own], axis=0),
        )

    def own_rows(a):
        return lax.dynamic_slice_in_dim(a, core * rows, rows, 0)

    def other_rows(a):
        return lax.dynamic_slice_in_dim(a, (1 - core) * rows, rows, 0)

    dp_size = lax.axis_size("dp")
    dp_place = lax.axis_index("dp")

    half = rows // 2
    og_y = swap(out_grad, 2)
    og_s = swap(out_grad, 1)
    og_d = swap(og_y, 1)
    og_all = jnp.concatenate(
        [out_grad, og_s, og_y[:half], og_d[:half], og_y[half:], og_d[half:]], axis=0
    )

    wq = w_qkv.reshape(width, 3 * cols)
    top = width // 2
    mid = cols // 2
    near_half = jnp.concatenate([wq[:top], w_mix[:mid].reshape(top, cols)], axis=1)
    slice_rows = top // dp_size
    far_half = jnp.concatenate(
        [
            lax.dynamic_slice_in_dim(wq, top + dp_place * slice_rows, slice_rows, 0),
            lax.dynamic_slice_in_dim(
                w_mix[mid:].reshape(top, cols), dp_place * slice_rows, slice_rows, 0
            ),
        ],
        axis=1,
    )
    piece = swap(far_half, 2)
    low = lax.all_gather(piece, "dp", axis=0, tiled=True)
    near_half = after(near_half, og_y)
    high = swap(near_half, 2)
    qb_far = swap(qv_bias, 2)
    wq_far = jnp.concatenate([high[:, : 3 * cols], low[:, : 3 * cols]], axis=0)
    wm_far = jnp.concatenate(
        [high[:, 3 * cols :].reshape(mid, width), low[:, 3 * cols :].reshape(mid, width)], axis=0
    )

    x = block_in.astype(F32)
    norm1, scale1 = norm_stats(x)
    n1 = (norm1 * first_gain + first_shift).astype(BF)
    rows1 = in_order(n1, swap(n1, 1))

    def project(w, b):
        bias = jnp.concatenate([b[0], jnp.zeros_like(b[0]), b[1]])
        return (dot(rows1, w) + bias).astype(BF)

    qkv_a = project(wq, qv_bias)
    att_a = attn_fwd(qkv_a, segc, seg)
    wq_far, att_a, wm_far = lax.optimization_barrier((wq_far, att_a, wm_far))
    qkv_b = project(wq_far, qb_far)
    att_b = attn_fwd(qkv_b, segc, seg)

    part = dot(other_rows(att_a), w_mix) + dot(other_rows(att_b), wm_far)
    got = swap(part.astype(BF), 1)
    mixed = dot(own_rows(att_a), w_mix) + dot(own_rows(att_b), wm_far) + got.astype(F32) + mix_bias
    resid = x + mixed
    norm2 = norm_stats(resid)[0]
    n2 = (norm2 * second_gain + second_shift).astype(BF)

    flat = (1, width)
    resid_grad, mg_all, reduce_grad, expand_grad, br_near, br_far, unit_sums, sums2 = ff(
        n2, og_all, w_expand, w_reduce, expand_bias.reshape(1, units), resid, second_gain.reshape(flat)
    )
    br_got = swap(br_far, 2)
    reduce_own = lax.psum_scatter(reduce_grad, "dp", scatter_dimension=0, tiled=True)
    expand_own = lax.psum_scatter(expand_grad, "dp", scatter_dimension=0, tiled=True)

    ag_b = dot(mg_all, wm_far, NT).astype(BF)
    dqkv_b, sums_b = attn_bwd(qkv_b, ag_b, segc, seg)
    qkv_grad_b = dot(rows1, dqkv_b, TN).astype(BF)
    mix_grad_b = dot(att_b, mg_all, TN).astype(BF)
    mix_back = swap(mix_grad_b, 2)
    qkv_back = swap(qkv_grad_b, 2)
    sums_back = swap(sums_b, 2)
    ag_a = dot(after(mg_all, qkv_grad_b), w_mix, NT).astype(BF)
    dqkv_a, sums_a = attn_bwd(qkv_a, ag_a, segc, seg)
    qkv_back, mix_back, dqkv_a, br_got = lax.optimization_barrier((qkv_back, mix_back, dqkv_a, br_got))

    branch = br_near.astype(F32) + br_got.astype(F32)
    block_out = (resid + branch + reduce_bias).astype(BF)

    n1g_other = dot(other_rows(dqkv_b), wq_far, NT) + dot(other_rows(dqkv_a), wq, NT)
    n1g_got = swap(n1g_other.astype(BF), 1)
    n1g = dot(own_rows(dqkv_b), wq_far, NT) + dot(own_rows(dqkv_a), wq, NT) + n1g_got.astype(F32)
    back1, first_gain_grad, first_shift_grad = norm_back(n1g, first_gain, norm1, scale1)
    in_grad = resid_grad + back1

    def over_tensor(a):
        a = a + swap(a, 1)
        return a + swap(a, 2)

    early = over_tensor(sums2)
    late = over_tensor(jnp.stack([first_gain_grad, first_shift_grad]))

    mix_grad = (dot(att_a, mg_all, TN) + mix_back.astype(F32)).astype(BF)
    qkv_grad = (dot(rows1, dqkv_a, TN) + qkv_back.astype(F32)).astype(BF)
    packed = jnp.concatenate([qkv_grad, mix_grad.reshape(width, cols)], axis=1)
    qv_bias_grad = (sums_a + sums_back).reshape(1, 2 * cols)
    small = jnp.concatenate(
        [
            late,
            early,
            unit_sums,
            jnp.pad(qv_bias_grad, ((0, 0), (0, width - 2 * cols))),
        ],
        axis=0,
    )
    packed, small, reduce_all, expand_all = ring_sum(packed, small, reduce_own, expand_own, dp_size)
    return (
        block_out,
        in_grad,
        small[0],
        small[1],
        packed[:, : 3 * cols].astype(F32).reshape(width, 3, cols),
        small[7, : 2 * cols].reshape(2, cols),
        packed[:, 3 * cols :].astype(F32).reshape(cols, width),
        small[2],
        small[3],
        small[4],
        expand_all.astype(F32),
        small[6],
        reduce_all.astype(F32),
        small[5],
    )


def solution(mesh):
    both = P(("dp", "tensor"), None)
    return jax.shard_map(
        body,
        mesh=mesh,
        in_specs=(
            both,
            P("dp", None),
            P(),
            P(),
            P(None, None, "tensor"),
            P(None, "tensor"),
            P("tensor", None),
            P(),
            P(),
            P(),
            P(None, "tensor"),
            P("tensor"),
            P("tensor", None),
            P(),
            both,
        ),
        out_specs=(
            both,
            both,
            P(),
            P(),
            P(None, None, "tensor"),
            P(None, "tensor"),
            P("tensor", None),
            P(),
            P(),
            P(),
            P(None, "tensor"),
            P("tensor"),
            P("tensor", None),
            P(),
        ),
        check_vma=False,
    )
```

```python
import functools

import jax
import jax.numpy as jnp
from jax import lax
from jax.experimental import pallas as pl
from jax.experimental.pallas import tpu as pltpu
from jax.sharding import PartitionSpec as P

HD = 64
PAIR = 2 * HD
QB = 256
EPS = 1e-5
BF = jnp.bfloat16
F32 = jnp.float32
SCALE = HD ** (-0.5)
MESH_ID = pl.DeviceIdType.MESH
NT = (((1,), (1,)), ((), ()))
TN = (((0,), (0,)), ((), ()))


def dot(a, b, dims=(((1,), (0,)), ((), ()))):
    return lax.dot_general(a, b, dims, preferred_element_type=F32)


def norm_stats(values):
    mean = jnp.mean(values, axis=-1, keepdims=True)
    centered = values - mean
    variance = jnp.mean(centered * centered, axis=-1, keepdims=True)
    scale = lax.rsqrt(variance + EPS)
    return centered * scale, scale


def fill_bias(segc_ref, segr_ref, bias_ref, blocks):
    off = 0
    for i in range(blocks):
        keys = (i + 1) * QB
        kpos = lax.broadcasted_iota(jnp.int32, (keys, QB), 0)
        qpos = lax.broadcasted_iota(jnp.int32, (keys, QB), 1) + i * QB
        same = segc_ref[:keys, :] == segr_ref[:, i * QB : (i + 1) * QB]
        allowed = jnp.logical_and(kpos <= qpos, same)
        bias_ref[off : off + keys, :] = jnp.where(allowed, 0.0, -1e30)
        off += keys


def half_masks():
    lane = lax.broadcasted_iota(jnp.int32, (1, PAIR), 1)
    return (lane < HD, lane >= HD)


def ring_index(at, n):
    at = (at + 2 * n) % n
    far = at // (n // 2)
    return (1 - far) * 2 * at + far * (2 * (n - 1 - at) + 1)


def ring_place(n):
    mine = lax.axis_index("dp")
    odd = mine % 2
    pos = (1 - odd) * (mine // 2) + odd * (n - 1 - mine // 2)
    return mine, pos, (ring_index(pos + 1, n), ring_index(pos - 1, n))


def meet(tensor_peers, dp_peers):
    barrier = pltpu.get_barrier_semaphore()
    for other in tensor_peers:
        pl.semaphore_signal(barrier, inc=1, device_id={"tensor": other}, device_id_type=MESH_ID)
    for other in dp_peers:
        pl.semaphore_signal(barrier, inc=1, device_id={"dp": other}, device_id_type=MESH_ID)
    pl.semaphore_wait(barrier, len(tensor_peers) + len(dp_peers))


def fwd_kernel(
    n,
    x_ref, segc_ref, segr_ref, g1_ref, s1_ref, wq_ref, bq_ref, wm_ref, mixb_ref, g2_ref, s2_ref, og_ref,
    rows1_ref, qkv_ref, att_ref, resid_ref, n2_ref, wqf_ref, wmf_ref, oga_ref,
    bqf, bias_ref, psend, pgot, send, recv, ring_send, ring_recv, local,
):
    rows, width = x_ref.shape
    seq = rows1_ref.shape[0]
    cols3 = wq_ref.shape[1]
    cols = cols3 // 3
    half = rows // 2
    blocks = seq // QB
    me = lax.axis_index("tensor")
    core = me % 2
    sib = me + 1 - 2 * core
    far = (me + 2) % 4
    mine, pos, sides = ring_place(n)
    meet((sib, far), sides)

    def remote(src, dst, k, other):
        return pltpu.make_async_remote_copy(
            src_ref=src,
            dst_ref=dst,
            send_sem=send.at[k],
            recv_sem=recv.at[k],
            device_id={"tensor": other},
            device_id_type=MESH_ID,
        )

    slab = width // n
    wide = cols3 // 2

    def slab_rows(chunk):
        return pl.ds(pl.multiple_of(chunk * slab, slab), slab)

    def piece():
        return remote(wq_ref.at[slab_rows(mine)], wqf_ref.at[slab_rows(mine)], 0, far)

    def bias_across():
        return remote(bq_ref, bqf, 1, far)

    def own_half(c):
        return pl.ds(pl.multiple_of(core * rows + c * half, half), half)

    def rows_beside(c):
        return remote(rows1_ref.at[own_half(c)], rows1_ref.at[own_half(c)], 2 + c, sib)

    def mix_across():
        return remote(wm_ref, wmf_ref, 4, far)

    def og_across(c):
        return remote(
            og_ref.at[pl.ds(c * half, half)], oga_ref.at[pl.ds((2 + c) * rows, half)], 5 + c, far
        )

    def og_beside():
        return remote(og_ref, oga_ref.at[pl.ds(rows, rows)], 7, sib)

    def og_forward(c):
        return remote(
            oga_ref.at[pl.ds((2 + c) * rows, half)],
            oga_ref.at[pl.ds((2 + c) * rows + half, half)],
            8 + c,
            sib,
        )

    def part_beside():
        return remote(psend, pgot, 10, sib)

    def og_own():
        return pltpu.make_async_copy(og_ref, oga_ref.at[pl.ds(0, rows)], local.at[0])

    def hop(d, s):
        chunk = ring_index(pos - s if d == 0 else pos + s, n)
        ref = wqf_ref.at[slab_rows(chunk), d * wide : (d + 1) * wide]
        return pltpu.make_async_remote_copy(
            src_ref=ref,
            dst_ref=ref,
            send_sem=ring_send.at[d],
            recv_sem=ring_recv.at[d, s],
            device_id={"dp": sides[d]},
            device_id_type=MESH_ID,
        )

    def tick(s):
        for d in range(2):
            hop(d, s).wait()

        @pl.when(s < n - 2)
        def _():
            for d in range(2):
                hop(d, s + 1).start()

    piece().start()
    bias_across().start()
    step = 64
    for c in range(2):

        @pl.loop(0, half // step)
        def _(r):
            normed = norm_stats(x_ref[pl.ds(pl.multiple_of(c * half + r * step, step), step), :].astype(F32))[0]
            to = pl.ds(pl.multiple_of(core * rows + c * half + r * step, step), step)
            rows1_ref[to, :] = (normed * g1_ref[...] + s1_ref[...]).astype(BF)

        rows_beside(c).start()
    piece().wait()
    for d in range(2):
        hop(d, 0).start()
    mix_across().start()
    for c in range(2):
        og_across(c).start()
    og_beside().start()
    og_own().start()
    fill_bias(segc_ref, segr_ref, bias_ref, blocks)

    def project(g, w_ref, b_ref):
        for k in range(3):
            at = slice(k * cols, (k + 1) * cols)
            to = slice(g * cols3 + k * cols, g * cols3 + (k + 1) * cols)
            qkv_ref[:, to] = (dot(rows1_ref[...], w_ref[:, at]) + b_ref[:, at]).astype(BF)

    for c in range(2):
        rows_beside(c).wait()
    project(0, wq_ref, bq_ref)
    masks = half_masks()
    pairs = cols // PAIR
    ticks = 2 * pairs

    @pl.loop(0, 2 * pairs)
    def _(p):
        @pl.when(p == pairs)
        def _():
            @pl.loop(ticks, n - 1)
            def _(s):
                tick(s)

            bias_across().wait()
            project(1, wqf_ref, bqf)

        base = (p // pairs) * cols3 + (p % pairs) * PAIR

        def lanes(k):
            return pl.ds(pl.multiple_of(base + k * cols, PAIR), PAIR)

        vt = qkv_ref[:, lanes(2)].T
        off = 0
        for i in range(blocks):
            keys = (i + 1) * QB
            at = slice(i * QB, (i + 1) * QB)
            qi = qkv_ref[at, lanes(0)] * jnp.asarray(SCALE, BF)
            kk = qkv_ref[:keys, lanes(1)]
            outs = []
            for h in range(2):
                qm = jnp.where(masks[h], qi, jnp.zeros_like(qi))
                s = dot(kk, qm, NT) + bias_ref[off : off + keys, :]
                e = jnp.exp(s - jnp.max(s, axis=0, keepdims=True))
                total = jnp.sum(e, axis=0, keepdims=True)
                o = dot(vt[h * HD : (h + 1) * HD, :keys], e.astype(BF))
                outs.append(o * (1.0 / total))
            out = jnp.concatenate(outs, axis=0).T.astype(BF)
            att_ref[at, pl.ds(pl.multiple_of(p * PAIR, PAIR), PAIR)] = out
            off += keys
            if i % 2 == 1:

                @pl.when(p < pairs)
                def _():
                    tick(2 * p + i // 2)

    mix_across().wait()
    nb = 256

    def mixed(start, at):
        sel = pl.ds(pl.multiple_of(start, rows), rows)
        return dot(att_ref[sel, 0:cols], wm_ref[:, at]) + dot(att_ref[sel, cols : 2 * cols], wmf_ref[:, at])

    for k in range(width // nb):
        at = slice(k * nb, (k + 1) * nb)
        psend[:, at] = mixed((1 - core) * rows, at).astype(BF)
    part_beside().start()
    for k in range(width // nb):
        at = slice(k * nb, (k + 1) * nb)
        resid_ref[:, at] = x_ref[:, at].astype(F32) + mixed(core * rows, at) + mixb_ref[:, at]
    for c in range(2):
        og_across(c).wait()
        og_forward(c).start()
    part_beside().wait()

    @pl.loop(0, rows // step)
    def _(r):
        at = pl.ds(pl.multiple_of(r * step, step), step)
        full = resid_ref[at, :] + pgot[at, :].astype(F32)
        resid_ref[at, :] = full
        n2_ref[at, :] = (norm_stats(full)[0] * g2_ref[...] + s2_ref[...]).astype(BF)

    og_own().wait()
    og_beside().wait()
    for c in range(2):
        og_forward(c).wait()


def forward(x, segc, segr, g1, s1, wq, bq, wm, mixb, g2, s2, og, n):
    rows, width = x.shape
    seq = segr.shape[1]
    cols3 = wq.shape[1]
    blocks = seq // QB
    vmem = pl.BlockSpec(memory_space=pltpu.VMEM)
    anyspace = pl.BlockSpec(memory_space=pl.ANY)
    return pl.pallas_call(
        functools.partial(fwd_kernel, n),
        in_specs=[vmem] * 11 + [anyspace],
        out_specs=[vmem] * 7 + [anyspace],
        out_shape=[
            jax.ShapeDtypeStruct((seq, width), BF),
            jax.ShapeDtypeStruct((seq, 2 * cols3), BF),
            jax.ShapeDtypeStruct((seq, 2 * cols3 // 3), BF),
            jax.ShapeDtypeStruct((rows, width), F32),
            jax.ShapeDtypeStruct((rows, width), BF),
            jax.ShapeDtypeStruct(wq.shape, BF),
            jax.ShapeDtypeStruct(wm.shape, BF),
            jax.ShapeDtypeStruct((4 * rows, width), BF),
        ],
        scratch_shapes=[
            pltpu.VMEM((1, cols3), F32),
            pltpu.VMEM((QB * blocks * (blocks + 1) // 2, QB), F32),
            pltpu.VMEM((rows, width), BF),
            pltpu.VMEM((rows, width), BF),
            pltpu.SemaphoreType.DMA((11,)),
            pltpu.SemaphoreType.DMA((11,)),
            pltpu.SemaphoreType.DMA((2,)),
            pltpu.SemaphoreType.DMA((2, n - 1)),
            pltpu.SemaphoreType.DMA((1,)),
        ],
        compiler_params=pltpu.CompilerParams(
            collective_id=3, has_side_effects=True, vmem_limit_bytes=56 << 20
        ),
        name="forward",
    )(x, segc, segr, g1, s1, wq, bq, wm, mixb, g2, s2, og)


def bwd_kernel(
    n,
    mg_hbm, qkv_hbm, att_hbm, rows1_hbm, wq_hbm, wqf_hbm, wm_hbm, wmf_hbm, x_hbm, rgrad_hbm, rg_hbm, eg_hbm,
    segc_ref, segr_ref, g1_ref,
    in_ref, qg_ref, mixg_ref, owns_ref, qsum_ref, nsum_ref,
    mg, qkv, att, rows1, wq, wqf, wm, wmf, x, rgrad, ffg,
    rbuf, dqkv, ag, bias_ref, dk_ref, dv_ref, q_send, q_got, m_send, m_got, s_got, s_send, psend, pgot, n1g,
    send, recv, ring_send, ring_recv, local,
):
    rows, width = in_ref.shape
    seq = mg.shape[0]
    cols3 = wq.shape[1]
    cols = cols3 // 3
    pairs = cols // PAIR
    blocks = seq // QB
    me = lax.axis_index("tensor")
    core = me % 2
    sib = me + 1 - 2 * core
    far = (me + 2) % 4
    mine, pos, sides = ring_place(n)

    pairs_in = (
        (mg_hbm, mg), (wmf_hbm, wmf), (qkv_hbm, qkv), (att_hbm, att), (rows1_hbm, rows1), (wqf_hbm, wqf),
        (wm_hbm, wm), (rg_hbm, ffg.at[0]), (eg_hbm, ffg.at[1]), (wq_hbm, wq), (x_hbm, x), (rgrad_hbm, rgrad),
    )

    def load(k):
        return pltpu.make_async_copy(pairs_in[k][0], pairs_in[k][1], local.at[k])

    for k in range(len(pairs_in)):
        load(k).start()
    meet((sib, far), sides)

    def remote(src, dst, k, other):
        return pltpu.make_async_remote_copy(
            src_ref=src,
            dst_ref=dst,
            send_sem=send.at[k],
            recv_sem=recv.at[k],
            device_id={"tensor": other},
            device_id_type=MESH_ID,
        )

    def q_across(k):
        return remote(q_send.at[k], q_got.at[k], k, far)

    def m_across():
        return remote(m_send, m_got, 3, far)

    def s_across():
        return remote(s_send, s_got, 4, far)

    def part_beside():
        return remote(psend, pgot, 5, sib)

    def ring_copy(src, kind, d, s):
        return pltpu.make_async_remote_copy(
            src_ref=src,
            dst_ref=rbuf.at[s, kind, d],
            send_sem=ring_send.at[kind, d],
            recv_sem=ring_recv.at[kind, d, s],
            device_id={"dp": sides[d]},
            device_id_type=MESH_ID,
        )

    def part(d, s):
        return ring_index(pos - 1 - s if d == 0 else pos + 1 + s, n)

    def tick(s):
        for kind in range(2):
            for d in range(2):
                ring_copy(rbuf.at[s, kind, d], kind, d, s).wait()
                mixed = rbuf[s, kind, d].astype(F32) + ffg[kind, part(d, s + 1), d].astype(F32)
                rbuf[s, kind, d] = mixed.astype(BF)

                @pl.when(s < n - 2)
                def _():
                    ring_copy(rbuf.at[s, kind, d], kind, d, s + 1).start()

    for k in (7, 8):
        load(k).wait()
    for kind in range(2):
        for d in range(2):
            ring_copy(ffg.at[kind, part(d, 0), d], kind, d, 0).start()

    fill_bias(segc_ref, segr_ref, bias_ref, blocks)
    masks = half_masks()
    for k in (0, 1, 2, 3):
        load(k).wait()
    m_send[...] = dot(att[:, cols : 2 * cols], mg[...], TN).astype(BF)
    m_across().start()
    ag[...] = dot(mg[...], wmf[...], NT).astype(BF)

    @pl.loop(0, 2 * pairs)
    def _(q):
        first = q < pairs
        group = 1 - q // pairs
        slot = q % pairs
        base = group * cols3 + slot * PAIR

        @pl.when(q == pairs)
        def _():
            ag[...] = dot(mg[...], wm[...], NT).astype(BF)

        def lanes(k):
            return pl.ds(pl.multiple_of(base + k * cols, PAIR), PAIR)

        own = pl.ds(pl.multiple_of(slot * PAIR, PAIR), PAIR)
        kt = qkv[:, lanes(1)].T
        dk_ref[...] = jnp.zeros_like(dk_ref)
        dv_ref[...] = jnp.zeros_like(dv_ref)
        off = 0
        qsum = jnp.zeros((1, PAIR), F32)
        for i in range(blocks):
            keys = (i + 1) * QB
            at = slice(i * QB, (i + 1) * QB)
            qi = qkv[at, lanes(0)] * jnp.asarray(SCALE, BF)
            gi = ag[at, own]
            kk = qkv[:keys, lanes(1)]
            vv = qkv[:keys, lanes(2)]
            outs = []
            for h in range(2):
                qm = jnp.where(masks[h], qi, jnp.zeros_like(qi))
                gm = jnp.where(masks[h], gi, jnp.zeros_like(gi))
                s = dot(kk, qm, NT) + bias_ref[off : off + keys, :]
                e = jnp.exp(s - jnp.max(s, axis=0, keepdims=True))
                prob = e * (1.0 / jnp.sum(e, axis=0, keepdims=True))
                weighted = prob * dot(vv, gm, NT)
                ds = (weighted - prob * jnp.sum(weighted, axis=0, keepdims=True)).astype(BF)
                dv_ref[:keys, :] += dot(prob.astype(BF), gm)
                dk_ref[:keys, :] += dot(ds, qm)
                outs.append(dot(kt[h * HD : (h + 1) * HD, :keys], ds))
            dq = (jnp.concatenate(outs, axis=0).T * SCALE).astype(BF)
            dqkv[at, lanes(0)] = dq
            qsum += jnp.sum(dq.astype(F32), axis=0, keepdims=True)
            off += keys
            if i == 1:

                @pl.when(q == 2 * pairs - 1)
                def _():
                    tick(4)
            if i == 2:

                @pl.when(jnp.logical_and(q > 0, q < 2 * pairs - 1))
                def _():
                    tick(2 * q - 1)
            if i == 3:

                @pl.when(q == 0)
                def _():
                    tick(0)
        dv = dv_ref[...].astype(BF)
        dqkv[:, lanes(1)] = dk_ref[...].astype(BF)
        dqkv[:, lanes(2)] = dv
        vsum = jnp.sum(dv.astype(F32), axis=0, keepdims=True)
        for (name, sel) in ((s_send, first), (qsum_ref, jnp.logical_not(first))):

            @pl.when(sel)
            def _():
                name[0:1, own] = qsum
                name[1:2, own] = vsum

        @pl.when(q == pairs - 1)
        def _():
            s_across().start()
            load(4).wait()
            for k in range(3):
                to = slice(cols3 + k * cols, cols3 + (k + 1) * cols)
                q_send[k] = dot(rows1[...], dqkv[:, to], TN).astype(BF)
                q_across(k).start()
            tick(2)
            load(6).wait()

    for k in (5, 9):
        load(k).wait()
    nb = 256

    def back(start, at):
        sel = pl.ds(pl.multiple_of(start, rows), rows)
        return dot(dqkv[sel, 0:cols3], wq[at, :], NT) + dot(dqkv[sel, cols3 : 2 * cols3], wqf[at, :], NT)

    for k in range(width // nb):
        at = slice(k * nb, (k + 1) * nb)
        psend[:, at] = back((1 - core) * rows, at).astype(BF)
    part_beside().start()
    tick(5)
    for k in range(width // nb):
        at = slice(k * nb, (k + 1) * nb)
        n1g[:, at] = back(core * rows, at)
    part_beside().wait()
    load(10).wait()
    load(11).wait()
    nsum_ref[...] = jnp.zeros_like(nsum_ref)
    step = 64

    @pl.loop(0, rows // step)
    def _(r):
        at = pl.ds(pl.multiple_of(r * step, step), step)
        grad = n1g[at, :] + pgot[at, :].astype(F32)
        normed, scale = norm_stats(x[at, :].astype(F32))
        g = grad * g1_ref[...]
        mean_g = jnp.mean(g, axis=-1, keepdims=True)
        mean_gn = jnp.mean(g * normed, axis=-1, keepdims=True)
        in_ref[at, :] = rgrad[at, :] + scale * (g - mean_g - normed * mean_gn)
        nsum_ref[0:1, :] += jnp.sum(grad * normed, axis=0, keepdims=True)
        nsum_ref[1:2, :] += jnp.sum(grad, axis=0, keepdims=True)

    @pl.loop(6, n - 1)
    def _(s):
        tick(s)

    owns_ref[...] = rbuf[n - 2]
    m_across().wait()
    mixg_ref[...] = (dot(att[:, 0:cols], mg[...], TN) + m_got[...].astype(F32)).astype(BF)
    s_across().wait()
    qsum_ref[...] += s_got[...]
    for k in range(3):
        to = slice(k * cols, (k + 1) * cols)
        qg = dot(rows1[...], dqkv[:, to], TN)
        q_across(k).wait()
        qg_ref[:, to] = (qg + q_got[k].astype(F32)).astype(BF)


def backward(mg, qkv, att, rows1, wq, wqf, wm, wmf, x, rgrad, rg, eg, segc, segr, g1, n):
    rows, width = x.shape
    seq = mg.shape[0]
    cols3 = wq.shape[1]
    cols = cols3 // 3
    blocks = seq // QB
    vmem = pl.BlockSpec(memory_space=pltpu.VMEM)
    anyspace = pl.BlockSpec(memory_space=pl.ANY)
    split = (n, 2, rg.shape[0] // (2 * n), width)
    chunk = split[2:]
    return pl.pallas_call(
        functools.partial(bwd_kernel, n),
        in_specs=[anyspace] * 12 + [vmem] * 3,
        out_specs=[vmem] * 6,
        out_shape=[
            jax.ShapeDtypeStruct((rows, width), F32),
            jax.ShapeDtypeStruct((width, cols3), BF),
            jax.ShapeDtypeStruct((cols, width), BF),
            jax.ShapeDtypeStruct((2, 2) + chunk, BF),
            jax.ShapeDtypeStruct((2, cols), F32),
            jax.ShapeDtypeStruct((2, width), F32),
        ],
        scratch_shapes=[
            pltpu.VMEM(mg.shape, BF),
            pltpu.VMEM(qkv.shape, BF),
            pltpu.VMEM(att.shape, BF),
            pltpu.VMEM(rows1.shape, BF),
            pltpu.VMEM(wq.shape, BF),
            pltpu.VMEM(wq.shape, BF),
            pltpu.VMEM(wm.shape, BF),
            pltpu.VMEM(wm.shape, BF),
            pltpu.VMEM(x.shape, BF),
            pltpu.VMEM(rgrad.shape, F32),
            pltpu.VMEM((2,) + split, BF),
            pltpu.VMEM((n - 1, 2, 2) + chunk, BF),
            pltpu.VMEM(qkv.shape, BF),
            pltpu.VMEM((seq, cols), BF),
            pltpu.VMEM((QB * blocks * (blocks + 1) // 2, QB), F32),
            pltpu.VMEM((seq, PAIR), F32),
            pltpu.VMEM((seq, PAIR), F32),
            pltpu.VMEM((3, width, cols), BF),
            pltpu.VMEM((3, width, cols), BF),
            pltpu.VMEM((cols, width), BF),
            pltpu.VMEM((cols, width), BF),
            pltpu.VMEM((2, cols), F32),
            pltpu.VMEM((2, cols), F32),
            pltpu.VMEM((rows, width), BF),
            pltpu.VMEM((rows, width), BF),
            pltpu.VMEM((rows, width), F32),
            pltpu.SemaphoreType.DMA((6,)),
            pltpu.SemaphoreType.DMA((6,)),
            pltpu.SemaphoreType.DMA((2, 2)),
            pltpu.SemaphoreType.DMA((2, 2, n - 1)),
            pltpu.SemaphoreType.DMA((12,)),
        ],
        compiler_params=pltpu.CompilerParams(
            collective_id=4, has_side_effects=True, vmem_limit_bytes=60 << 20
        ),
        name="backward",
    )(mg, qkv, att, rows1, wq, wqf, wm, wmf, x, rgrad, rg.reshape(split), eg.reshape(split), segc, segr, g1)


GA = 0.7978845608028654
GB = 0.044715


def ff_kernel(
    n2_ref, og_ref, we_ref, wr_ref, be_ref, resid_ref, gain_ref,
    rgrad_ref, mg_ref, rg_ref, eg_ref, brn_ref, brf_ref, usum_ref, dsum_ref,
    n2b, act, pg, ng, br, ng_d, br_d, ng_s, br_s, ng_far, ng_out,
    send, recv,
):
    rows, width = n2_ref.shape
    units = we_ref.shape[1]
    part = rows // 2
    nb = 256
    me = lax.axis_index("tensor")
    core = me % 2
    sib = me + 1 - 2 * core
    far = (me + 2) % 4

    barrier = pltpu.get_barrier_semaphore()
    for other in (sib, far):
        pl.semaphore_signal(barrier, inc=1, device_id={"tensor": other}, device_id_type=MESH_ID)
    pl.semaphore_wait(barrier, 2)

    def remote(src, dst, k, other):
        return pltpu.make_async_remote_copy(
            src_ref=src,
            dst_ref=dst,
            send_sem=send.at[k],
            recv_sem=recv.at[k],
            device_id={"tensor": other},
            device_id_type=MESH_ID,
        )

    def y_at(c):
        return pl.ds((2 + c) * rows, part)

    def d_at(c):
        return pl.ds((2 + c) * rows + part, part)

    def rows_across(c):
        return remote(n2_ref.at[pl.ds(c * part, part)], n2b.at[y_at(c)], c, far)

    def rows_beside():
        return remote(n2_ref, n2b.at[pl.ds(rows, rows)], 2, sib)

    def rows_forward(c):
        return remote(n2b.at[y_at(c)], n2b.at[d_at(c)], 3 + c, sib)

    def ng_beside():
        return remote(ng.at[pl.ds(rows, rows)], ng_s, 5, sib)

    def br_beside():
        return remote(br.at[pl.ds(rows, rows)], br_s, 6, sib)

    def ng_combine(c):
        return remote(ng.at[d_at(c)], ng_d.at[c], 7 + c, sib)

    def br_combine(c):
        return remote(br.at[d_at(c)], br_d.at[c], 9 + c, sib)

    def ng_across(c):
        return remote(ng_out.at[c], ng_far.at[c], 11 + c, far)

    def mg_beside(c):
        at = pl.ds(pl.multiple_of(core * rows + c * part, part), part)
        return remote(mg_ref.at[at], mg_ref.at[at], 13 + c, sib)

    for c in range(2):
        rows_across(c).start()
    rows_beside().start()
    n2b[0:rows, :] = n2_ref[...]
    usum_ref[...] = jnp.zeros_like(usum_ref)

    @pl.loop(0, 4)
    def _(b):
        at = pl.ds(pl.multiple_of(b * rows, rows), rows)
        c = b - 2

        @pl.when(b == 1)
        def _():
            rows_beside().wait()

        @pl.when(b >= 2)
        def _():
            rows_across(c).wait()
            rows_forward(c).start()
            rows_forward(c).wait()

        for k in range(units // nb):
            cols = slice(k * nb, (k + 1) * nb)
            u = dot(n2b[at, :], we_ref[:, cols]) + be_ref[:, cols]
            act_grad = dot(og_ref[at, :], wr_ref[cols, :], NT)
            sq = u * u
            th = jnp.tanh(u * (GA + (GA * GB) * sq))
            cdf = 0.5 * (1.0 + th)
            slope = cdf + (0.5 * u) * (1.0 - th * th) * (GA + (3.0 * GA * GB) * sq)
            pre = (act_grad * slope).astype(BF)
            act[at, cols] = (u * cdf).astype(BF)
            pg[at, cols] = pre
            usum_ref[:, cols] += jnp.sum(pre.astype(F32), axis=0, keepdims=True)
        for k in range(width // nb):
            cols = slice(k * nb, (k + 1) * nb)
            ng[at, cols] = dot(pg[at, :], we_ref[cols, :], NT).astype(BF)

        @pl.when(b == 1)
        def _():
            ng_beside().start()

        @pl.when(b >= 2)
        def _():
            ng_combine(c).start()

        for k in range(width // nb):
            cols = slice(k * nb, (k + 1) * nb)
            br[at, cols] = dot(act[at, :], wr_ref[:, cols]).astype(BF)

        @pl.when(b == 1)
        def _():
            br_beside().start()

        @pl.when(b >= 2)
        def _():
            br_combine(c).start()
            ng_combine(c).wait()
            ng_out[c] = (ng[y_at(c), :].astype(F32) + ng_d[c].astype(F32)).astype(BF)
            ng_across(c).start()

    @pl.loop(0, width // nb)
    def _(k):
        cols = pl.ds(pl.multiple_of(k * nb, nb), nb)
        rg_ref[:, cols] = dot(act[...], og_ref[:, cols], TN).astype(BF)
        eg_ref[:, cols] = dot(n2b[...], pg[:, cols], TN).astype(BF)

    br_beside().wait()
    brn_ref[...] = (br[0:rows, :].astype(F32) + br_s[...].astype(F32)).astype(BF)
    for c in range(2):
        br_combine(c).wait()
        brf_ref[c * part : (c + 1) * part, :] = (
            br[y_at(c), :].astype(F32) + br_d[c].astype(F32)
        ).astype(BF)
    ng_beside().wait()
    dsum_ref[...] = jnp.zeros_like(dsum_ref)
    step = 64
    for c in range(2):
        ng_across(c).wait()

        @pl.loop(0, part // step)
        def _(r):
            inner = pl.ds(pl.multiple_of(r * step, step), step)
            at = pl.ds(pl.multiple_of(c * part + r * step, step), step)
            grad = ng[at, :].astype(F32) + ng_s[at, :].astype(F32) + ng_far[c, inner, :].astype(F32)
            normed, scale = norm_stats(resid_ref[at, :])
            g = grad * gain_ref[...]
            gn = g * normed
            mean_g = jnp.mean(g, axis=-1, keepdims=True)
            mean_gn = jnp.mean(gn, axis=-1, keepdims=True)
            og = og_ref[at, :].astype(F32)
            rgrad = og + scale * (g - mean_g - normed * mean_gn)
            rgrad_ref[at, :] = rgrad
            mg = rgrad.astype(BF)
            mg_ref[pl.ds(pl.multiple_of(core * rows + c * part + r * step, step), step), :] = mg
            dsum_ref[0:1, :] += jnp.sum(mg.astype(F32), axis=0, keepdims=True)
            dsum_ref[1:2, :] += jnp.sum(grad * normed, axis=0, keepdims=True)
            dsum_ref[2:3, :] += jnp.sum(grad, axis=0, keepdims=True)
            dsum_ref[3:4, :] += jnp.sum(og, axis=0, keepdims=True)

        mg_beside(c).start()
    for c in range(2):
        mg_beside(c).wait()


def ff(n2, og_all, we, wr, be, resid, gain):
    rows, width = n2.shape
    units = we.shape[1]
    part = rows // 2
    vmem = pl.BlockSpec(memory_space=pltpu.VMEM)
    return pl.pallas_call(
        ff_kernel,
        in_specs=[vmem] * 7,
        out_specs=[vmem] * 8,
        out_shape=[
            jax.ShapeDtypeStruct((rows, width), F32),
            jax.ShapeDtypeStruct((2 * rows, width), BF),
            jax.ShapeDtypeStruct((units, width), BF),
            jax.ShapeDtypeStruct((width, units), BF),
            jax.ShapeDtypeStruct((rows, width), BF),
            jax.ShapeDtypeStruct((rows, width), BF),
            jax.ShapeDtypeStruct((1, units), F32),
            jax.ShapeDtypeStruct((4, width), F32),
        ],
        scratch_shapes=[
            pltpu.VMEM((4 * rows, width), BF),
            pltpu.VMEM((4 * rows, units), BF),
            pltpu.VMEM((4 * rows, units), BF),
            pltpu.VMEM((4 * rows, width), BF),
            pltpu.VMEM((4 * rows, width), BF),
            pltpu.VMEM((2, part, width), BF),
            pltpu.VMEM((2, part, width), BF),
            pltpu.VMEM((rows, width), BF),
            pltpu.VMEM((rows, width), BF),
            pltpu.VMEM((2, part, width), BF),
            pltpu.VMEM((2, part, width), BF),
            pltpu.SemaphoreType.DMA((15,)),
            pltpu.SemaphoreType.DMA((15,)),
        ],
        compiler_params=pltpu.CompilerParams(
            collective_id=2, has_side_effects=True, vmem_limit_bytes=60 << 20
        ),
        name="ff",
    )(n2, og_all, we, wr, be, resid, gain)


def ring_kernel(
    n, q_ref, m_ref, small_ref, owns_ref, brf_ref,
    qo_ref, mo_ref, so_ref, ro_ref, eo_ref, bro_ref,
    qbuf, mbuf, sbuf, speer, ssum, send, recv, tsend, trecv, local,
):
    mine, pos, sides = ring_place(n)
    me = lax.axis_index("tensor")
    far = (me + 2) % 4
    peers = [(me + k) % 4 for k in range(1, 4)]
    meet(peers, sides)

    def remote(src, dst, kind, d, s):
        return pltpu.make_async_remote_copy(
            src_ref=src,
            dst_ref=dst,
            send_sem=send.at[kind, d],
            recv_sem=recv.at[kind, d, s],
            device_id={"dp": sides[d]},
            device_id_type=MESH_ID,
        )

    def beside(src, dst, k, other):
        return pltpu.make_async_remote_copy(
            src_ref=src,
            dst_ref=dst,
            send_sem=tsend.at[k],
            recv_sem=trecv.at[k],
            device_id={"tensor": other},
            device_id_type=MESH_ID,
        )

    def share(k):
        return beside(small_ref, speer.at[k], k, peers[k])

    def branch():
        return beside(brf_ref, bro_ref, 3, far)

    def gather(out, kind, d, s):
        chunk = ring_index(pos - s if d == 0 else pos + s, n)
        return remote(out.at[chunk, d], out.at[chunk, d], kind, d, s)

    def gather_small(s):
        chunk = ring_index(pos - s, n)
        return remote(so_ref.at[chunk], so_ref.at[chunk], 7, 0, s)

    def part(d, s):
        return ring_index(pos - 1 - s if d == 0 else pos + 1 + s, n)

    parts = ((q_ref, qbuf, 0), (m_ref, mbuf, 1))

    def begin(ref, buf, kind, d):
        remote(ref.at[part(d, 0), d], buf.at[0, d], kind, d, 0).start()

    def take(ref, buf, kind, d, s):
        remote(buf.at[s, d], buf.at[s, d], kind, d, s).wait()
        total = buf[s, d].astype(F32) + ref[part(d, s + 1), d].astype(F32)
        buf[s, d] = total.astype(BF)

    def pass_on(buf, kind, d, s):
        remote(buf.at[s, d], buf.at[s + 1, d], kind, d, s + 1).start()

    def take_small(s):
        remote(sbuf.at[s], sbuf.at[s], 6, 0, s).wait()
        sbuf[s] = sbuf[s] + ssum[part(0, s + 1)]

    for k in range(3):
        share(k).start()
    own = [pltpu.make_async_copy(owns_ref.at[k], (ro_ref, eo_ref)[k].at[mine], local.at[k]) for k in range(2)]
    for copy in own:
        copy.start()
    for d in range(2):
        for ref, buf, kind in parts:
            begin(ref, buf, kind, d)
    for copy in own:
        copy.wait()
    for d in range(2):
        gather(ro_ref, 2, d, 0).start()
    branch().start()
    for k in range(3):
        share(k).wait()
    ssum[...] = small_ref[...]
    shared = n * 6 // 8
    ssum[0:shared] = ssum[0:shared] + speer[0, 0:shared] + speer[1, 0:shared] + speer[2, 0:shared]
    remote(ssum.at[part(0, 0)], sbuf.at[0], 6, 0, 0).start()

    @pl.loop(0, n - 2)
    def _(s):
        for d in range(2):
            for ref, buf, kind in parts:
                take(ref, buf, kind, d, s)
                pass_on(buf, kind, d, s)
        take_small(s)
        remote(sbuf.at[s], sbuf.at[s + 1], 6, 0, s + 1).start()
        for d in range(2):
            gather(ro_ref, 2, d, s).wait()
            gather(ro_ref, 2, d, s + 1).start()

    last = n - 2
    for d in range(2):
        for ref, buf, kind in parts:
            take(ref, buf, kind, d, last)
    take_small(last)
    own = [
        pltpu.make_async_copy(qbuf.at[last], qo_ref.at[mine], local.at[0]),
        pltpu.make_async_copy(mbuf.at[last], mo_ref.at[mine], local.at[1]),
        pltpu.make_async_copy(sbuf.at[last], so_ref.at[mine], local.at[2]),
    ]
    for copy in own:
        copy.start()
    for d in range(2):
        gather(ro_ref, 2, d, last).wait()
        gather(eo_ref, 3, d, 0).start()
    for copy in own:
        copy.wait()
    for d in range(2):
        gather(qo_ref, 4, d, 0).start()
        gather(mo_ref, 5, d, 0).start()
    gather_small(0).start()

    @pl.loop(0, n - 2)
    def _(s):
        for out, kind in ((eo_ref, 3), (qo_ref, 4), (mo_ref, 5)):
            for d in range(2):
                gather(out, kind, d, s).wait()
                gather(out, kind, d, s + 1).start()
        gather_small(s).wait()
        gather_small(s + 1).start()

    for out, kind in ((eo_ref, 3), (qo_ref, 4), (mo_ref, 5)):
        for d in range(2):
            gather(out, kind, d, last).wait()
    gather_small(last).wait()
    branch().wait()


def ring_sum(q, m, small, owns, brf, n):
    def split(a):
        return a.reshape(n, 2, a.shape[0] // (2 * n), a.shape[1])

    q4, m4, s3 = split(q), split(m), small.reshape(n, 1, small.size // n)
    chunk = owns.shape[1:]
    full = jax.ShapeDtypeStruct((n,) + chunk, BF)
    vmem = pl.BlockSpec(memory_space=pltpu.VMEM)
    anyspace = pl.BlockSpec(memory_space=pl.ANY)
    qo, mo, so, ro, eo, bro = pl.pallas_call(
        functools.partial(ring_kernel, n),
        in_specs=[vmem, vmem, vmem, anyspace, anyspace],
        out_specs=[anyspace] * 6,
        out_shape=[
            jax.ShapeDtypeStruct(q4.shape, BF),
            jax.ShapeDtypeStruct(m4.shape, BF),
            jax.ShapeDtypeStruct(s3.shape, F32),
            full,
            full,
            jax.ShapeDtypeStruct(brf.shape, BF),
        ],
        scratch_shapes=[
            pltpu.VMEM((n - 1,) + q4.shape[1:], BF),
            pltpu.VMEM((n - 1,) + m4.shape[1:], BF),
            pltpu.VMEM((n - 1,) + s3.shape[1:], F32),
            pltpu.VMEM((3,) + s3.shape, F32),
            pltpu.VMEM(s3.shape, F32),
            pltpu.SemaphoreType.DMA((8, 2)),
            pltpu.SemaphoreType.DMA((8, 2, n - 1)),
            pltpu.SemaphoreType.DMA((4,)),
            pltpu.SemaphoreType.DMA((4,)),
            pltpu.SemaphoreType.DMA((3,)),
        ],
        compiler_params=pltpu.CompilerParams(
            collective_id=1, has_side_effects=True, vmem_limit_bytes=32 << 20
        ),
        name="ring_sum",
    )(q4, m4, s3, owns, brf)
    wide = (2 * n * chunk[1], chunk[2])
    return qo.reshape(q.shape), mo.reshape(m.shape), so.reshape(small.shape), ro.reshape(wide), eo.reshape(wide), bro


def body(
    block_in,
    segments,
    first_gain,
    first_shift,
    w_qkv,
    qv_bias,
    w_mix,
    mix_bias,
    second_gain,
    second_shift,
    w_expand,
    expand_bias,
    w_reduce,
    reduce_bias,
    out_grad,
):
    rows, width = block_in.shape
    cols = w_qkv.shape[2]
    units = w_expand.shape[1]
    place = lax.axis_index("tensor")
    seg = lax.dynamic_slice_in_dim(segments, place // 2, 1, 0)
    segc = seg.reshape(-1, 1)

    dp_size = lax.axis_size("dp")

    flat = (1, width)
    wq = w_qkv.reshape(width, 3 * cols)
    bq = jnp.concatenate([qv_bias[0], jnp.zeros_like(qv_bias[0]), qv_bias[1]]).reshape(1, 3 * cols)
    rows1, qkv, att, resid, n2, wq_far, wm_far, og_all = forward(
        block_in,
        segc,
        seg,
        first_gain.reshape(flat),
        first_shift.reshape(flat),
        wq,
        bq,
        w_mix,
        mix_bias.reshape(flat),
        second_gain.reshape(flat),
        second_shift.reshape(flat),
        out_grad,
        dp_size,
    )
    resid_grad, mg_all, reduce_grad, expand_grad, br_near, br_far, unit_sums, sums2 = ff(
        n2, og_all, w_expand, w_reduce, expand_bias.reshape(1, units), resid, second_gain.reshape(flat)
    )
    in_grad, qkv_grad, mix_grad, owns, qv_sums, norm_sums = backward(
        mg_all,
        qkv,
        att,
        rows1,
        wq,
        wq_far,
        w_mix,
        wm_far,
        block_in,
        resid_grad,
        reduce_grad,
        expand_grad,
        segc,
        seg,
        first_gain.reshape(flat),
        dp_size,
    )
    small = jnp.concatenate(
        [
            norm_sums,
            sums2,
            unit_sums,
            jnp.pad(qv_sums.reshape(1, 2 * cols), ((0, 0), (0, width - 2 * cols))),
        ],
        axis=0,
    )
    qkv_grad, mix_grad, small, reduce_all, expand_all, br_got = ring_sum(
        qkv_grad, mix_grad, small, owns, br_far, dp_size
    )
    block_out = (resid + br_near.astype(F32) + br_got.astype(F32) + reduce_bias).astype(BF)
    return (
        block_out,
        in_grad,
        small[0],
        small[1],
        qkv_grad.astype(F32).reshape(width, 3, cols),
        small[7, : 2 * cols].reshape(2, cols),
        mix_grad.astype(F32),
        small[2],
        small[3],
        small[4],
        expand_all.astype(F32),
        small[6],
        reduce_all.astype(F32),
        small[5],
    )


def solution(mesh):
    both = P(("dp", "tensor"), None)
    return jax.shard_map(
        body,
        mesh=mesh,
        in_specs=(
            both,
            P("dp", None),
            P(),
            P(),
            P(None, None, "tensor"),
            P(None, "tensor"),
            P("tensor", None),
            P(),
            P(),
            P(),
            P(None, "tensor"),
            P("tensor"),
            P("tensor", None),
            P(),
            both,
        ),
        out_specs=(
            both,
            both,
            P(),
            P(),
            P(None, None, "tensor"),
            P(None, "tensor"),
            P("tensor", None),
            P(),
            P(),
            P(),
            P(None, "tensor"),
            P("tensor"),
            P("tensor", None),
            P(),
        ),
        check_vma=False,
    )
```

```python
import functools

import jax
import jax.numpy as jnp
from jax import lax
from jax.experimental import pallas as pl
from jax.experimental.pallas import tpu as pltpu
from jax.sharding import PartitionSpec as P

HD = 64
PAIR = 2 * HD
QB = 256
EPS = 1e-5
BF = jnp.bfloat16
F32 = jnp.float32
SCALE = HD ** (-0.5)
MESH_ID = pl.DeviceIdType.MESH
EARLY = 1
AHEAD = 4
NT = (((1,), (1,)), ((), ()))
TN = (((0,), (0,)), ((), ()))


def dot(a, b, dims=(((1,), (0,)), ((), ()))):
    return lax.dot_general(a, b, dims, preferred_element_type=F32)


def norm_stats(values):
    mean = jnp.mean(values, axis=-1, keepdims=True)
    centered = values - mean
    variance = jnp.mean(centered * centered, axis=-1, keepdims=True)
    scale = lax.rsqrt(variance + EPS)
    return centered * scale, scale


def fill_bias(seg_ref, row, bias_ref, blocks):
    segr = seg_ref[pl.ds(row, 1), :].astype(F32)
    segc = jnp.broadcast_to(segr, (8, segr.shape[1])).T[:, 0:1]
    off = 0
    for i in range(blocks):
        keys = (i + 1) * QB
        kpos = lax.broadcasted_iota(jnp.int32, (keys, QB), 0)
        qpos = lax.broadcasted_iota(jnp.int32, (keys, QB), 1) + i * QB
        same = segc[:keys, :] == segr[:, i * QB : (i + 1) * QB]
        allowed = jnp.logical_and(kpos <= qpos, same)
        bias_ref[off : off + keys, :] = jnp.where(allowed, 0.0, -1e30)
        off += keys


def half_masks():
    lane = lax.broadcasted_iota(jnp.int32, (1, PAIR), 1)
    return (lane < HD, lane >= HD)


def ring_index(at, n):
    at = (at + 2 * n) % n
    far = at // (n // 2)
    return (1 - far) * 2 * at + far * (2 * (n - 1 - at) + 1)


def ring_place(n):
    mine = lax.axis_index("dp")
    odd = mine % 2
    pos = (1 - odd) * (mine // 2) + odd * (n - 1 - mine // 2)
    return mine, pos, (ring_index(pos + 1, n), ring_index(pos - 1, n))


def meet(tensor_peers, dp_peers):
    barrier = pltpu.get_barrier_semaphore()
    for other in tensor_peers:
        pl.semaphore_signal(barrier, inc=1, device_id={"tensor": other}, device_id_type=MESH_ID)
    for other in dp_peers:
        pl.semaphore_signal(barrier, inc=1, device_id={"dp": other}, device_id_type=MESH_ID)
    pl.semaphore_wait(barrier, len(tensor_peers) + len(dp_peers))


def fwd_kernel(
    n,
    x_ref, seg_ref, g1_ref, s1_ref, bq_ref, mixb_ref, g2_ref, s2_ref, wq_hbm, wm_hbm, og_ref,
    rows1_ref, qkv_ref, att_ref, resid_ref, n2_ref, wqf_ref, wmf_ref, oga_ref,
    wq_ref, wm_ref, bqf, bias_ref, psend, pgot, send, recv, ring_send, ring_recv, local,
):
    rows, width = x_ref.shape
    seq = rows1_ref.shape[0]
    cols = wq_ref.shape[2]
    cols3 = 3 * cols
    half = rows // 2
    blocks = seq // QB
    me = lax.axis_index("tensor")
    core = me % 2
    sib = me + 1 - 2 * core
    far = (me + 2) % 4
    mine, pos, sides = ring_place(n)
    meet((sib, far), sides)

    def remote(src, dst, k, other):
        return pltpu.make_async_remote_copy(
            src_ref=src,
            dst_ref=dst,
            send_sem=send.at[k],
            recv_sem=recv.at[k],
            device_id={"tensor": other},
            device_id_type=MESH_ID,
        )

    slab = width // n
    wide = cols // 2

    def slab_rows(chunk):
        return pl.ds(pl.multiple_of(chunk * slab, slab), slab)

    def piece():
        return remote(wq_hbm.at[:, slab_rows(mine)], wqf_ref.at[:, slab_rows(mine)], 0, far)

    def bias_across():
        return remote(bq_ref, bqf, 1, far)

    def own_half(c):
        return pl.ds(pl.multiple_of(core * rows + c * half, half), half)

    def rows_beside(c):
        return remote(rows1_ref.at[own_half(c)], rows1_ref.at[own_half(c)], 2 + c, sib)

    def mix_across():
        return remote(wm_hbm, wmf_ref, 4, far)

    def og_across(c):
        return remote(
            og_ref.at[pl.ds(c * half, half)], oga_ref.at[pl.ds((2 + c) * rows, half)], 5 + c, far
        )

    def og_beside():
        return remote(og_ref, oga_ref.at[pl.ds(rows, rows)], 7, sib)

    def og_forward(c):
        return remote(
            oga_ref.at[pl.ds((2 + c) * rows, half)],
            oga_ref.at[pl.ds((2 + c) * rows + half, half)],
            8 + c,
            sib,
        )

    def part_beside():
        return remote(psend, pgot, 10, sib)

    def og_own():
        return pltpu.make_async_copy(og_ref, oga_ref.at[pl.ds(0, rows)], local.at[0])

    def hop(k, d, s):
        chunk = ring_index(pos - s if d == 0 else pos + s, n)
        ref = wqf_ref.at[k, slab_rows(chunk), d * wide : (d + 1) * wide]
        return pltpu.make_async_remote_copy(
            src_ref=ref,
            dst_ref=ref,
            send_sem=ring_send.at[k, d],
            recv_sem=ring_recv.at[k, d, s],
            device_id={"dp": sides[d]},
            device_id_type=MESH_ID,
        )

    def tick(s):
        for k in range(3):
            for d in range(2):
                hop(k, d, s).wait()

                @pl.when(s < n - 2)
                def _():
                    hop(k, d, s + 1).start()

    piece().start()
    bias_across().start()
    loads = (
        pltpu.make_async_copy(wq_hbm, wq_ref, local.at[1]),
        pltpu.make_async_copy(wm_hbm, wm_ref, local.at[2]),
    )
    for load in loads:
        load.start()
    step = 64
    for c in range(2):

        @pl.loop(0, half // step)
        def _(r):
            normed = norm_stats(x_ref[pl.ds(pl.multiple_of(c * half + r * step, step), step), :].astype(F32))[0]
            to = pl.ds(pl.multiple_of(core * rows + c * half + r * step, step), step)
            rows1_ref[to, :] = (normed * g1_ref[...] + s1_ref[...]).astype(BF)

        rows_beside(c).start()
    piece().wait()
    for k in range(3):
        for d in range(2):
            hop(k, d, 0).start()
    mix_across().start()
    for c in range(2):
        og_across(c).start()
    og_beside().start()
    og_own().start()
    fill_bias(seg_ref, me // 2, bias_ref, blocks)

    def project(g, w_ref, b_ref):
        for k in range(3):
            to = slice(g * cols3 + k * cols, g * cols3 + (k + 1) * cols)
            part = dot(rows1_ref[...], w_ref[k])
            if k != 1:
                part = part + b_ref[k // 2 : k // 2 + 1, :]
            qkv_ref[:, to] = part.astype(BF)

    for c in range(2):
        rows_beside(c).wait()
    for load in loads:
        load.wait()
    project(0, wq_ref, bq_ref)
    tick(0)
    masks = half_masks()
    pairs = cols // PAIR
    ticks = 1 + 2 * pairs

    @pl.loop(0, 2 * pairs)
    def _(p):
        @pl.when(p == pairs)
        def _():
            @pl.loop(ticks, n - 1)
            def _(s):
                tick(s)

            bias_across().wait()
            project(1, wqf_ref, bqf)

        base = (p // pairs) * cols3 + (p % pairs) * PAIR

        def lanes(k):
            return pl.ds(pl.multiple_of(base + k * cols, PAIR), PAIR)

        vt = qkv_ref[:, lanes(2)].T
        off = 0
        for i in range(blocks):
            keys = (i + 1) * QB
            at = slice(i * QB, (i + 1) * QB)
            qi = qkv_ref[at, lanes(0)] * jnp.asarray(SCALE, BF)
            kk = qkv_ref[:keys, lanes(1)]
            outs = []
            for h in range(2):
                qm = jnp.where(masks[h], qi, jnp.zeros_like(qi))
                s = dot(kk, qm, NT) + bias_ref[off : off + keys, :]
                e = jnp.exp(s - jnp.max(s, axis=0, keepdims=True))
                total = jnp.sum(e, axis=0, keepdims=True)
                o = dot(vt[h * HD : (h + 1) * HD, :keys], e.astype(BF))
                outs.append(o * (1.0 / total))
            out = jnp.concatenate(outs, axis=0).T.astype(BF)
            att_ref[at, pl.ds(pl.multiple_of(p * PAIR, PAIR), PAIR)] = out
            off += keys
            if i % 2 == 1:

                @pl.when(p < pairs)
                def _():
                    tick(1 + 2 * p + i // 2)

    mix_across().wait()
    nb = 256

    def mixed(start, at):
        sel = pl.ds(pl.multiple_of(start, rows), rows)
        return dot(att_ref[sel, 0:cols], wm_ref[:, at]) + dot(att_ref[sel, cols : 2 * cols], wmf_ref[:, at])

    for k in range(width // nb):
        at = slice(k * nb, (k + 1) * nb)
        psend[:, at] = mixed((1 - core) * rows, at).astype(BF)
    part_beside().start()
    for k in range(width // nb):
        at = slice(k * nb, (k + 1) * nb)
        resid_ref[:, at] = x_ref[:, at].astype(F32) + mixed(core * rows, at) + mixb_ref[:, at]
    for c in range(2):
        og_across(c).wait()
        og_forward(c).start()
    part_beside().wait()

    @pl.loop(0, rows // step)
    def _(r):
        at = pl.ds(pl.multiple_of(r * step, step), step)
        full = resid_ref[at, :] + pgot[at, :].astype(F32)
        resid_ref[at, :] = full
        n2_ref[at, :] = (norm_stats(full)[0] * g2_ref[...] + s2_ref[...]).astype(BF)

    og_own().wait()
    og_beside().wait()
    for c in range(2):
        og_forward(c).wait()


def forward(x, segments, g1, s1, bq, mixb, g2, s2, wq, wm, og, n):
    rows, width = x.shape
    seq = segments.shape[1]
    cols = wq.shape[2]
    blocks = seq // QB
    vmem = pl.BlockSpec(memory_space=pltpu.VMEM)
    anyspace = pl.BlockSpec(memory_space=pl.ANY)
    return pl.pallas_call(
        functools.partial(fwd_kernel, n),
        in_specs=[vmem] * 8 + [anyspace] * 3,
        out_specs=[vmem] * 7 + [anyspace],
        out_shape=[
            jax.ShapeDtypeStruct((seq, width), BF),
            jax.ShapeDtypeStruct((seq, 6 * cols), BF),
            jax.ShapeDtypeStruct((seq, 2 * cols), BF),
            jax.ShapeDtypeStruct((rows, width), F32),
            jax.ShapeDtypeStruct((rows, width), BF),
            jax.ShapeDtypeStruct(wq.shape, BF),
            jax.ShapeDtypeStruct(wm.shape, BF),
            jax.ShapeDtypeStruct((4 * rows, width), BF),
        ],
        scratch_shapes=[
            pltpu.VMEM(wq.shape, BF),
            pltpu.VMEM(wm.shape, BF),
            pltpu.VMEM((2, cols), F32),
            pltpu.VMEM((QB * blocks * (blocks + 1) // 2, QB), F32),
            pltpu.VMEM((rows, width), BF),
            pltpu.VMEM((rows, width), BF),
            pltpu.SemaphoreType.DMA((11,)),
            pltpu.SemaphoreType.DMA((11,)),
            pltpu.SemaphoreType.DMA((3, 2)),
            pltpu.SemaphoreType.DMA((3, 2, n - 1)),
            pltpu.SemaphoreType.DMA((3,)),
        ],
        compiler_params=pltpu.CompilerParams(
            collective_id=3, has_side_effects=True, vmem_limit_bytes=56 << 20
        ),
        name="forward",
    )(x, segments, g1, s1, bq, mixb, g2, s2, wq, wm, og)


def bwd_kernel(
    n,
    mg_hbm, qkv_hbm, att_hbm, rows1_hbm, wq_hbm, wqf_hbm, wm_hbm, wmf_hbm, x_hbm, rgrad_hbm, rg_hbm, eg_hbm, carry_hbm,
    seg_ref, g1_ref,
    in_ref, qg_ref, qsum_ref, nsum_ref, ro_ref, eo_ref,
    mg, qkv, att, rows1, wq, wqf, wm, wmf, x, rgrad, ffg,
    rbuf, dqkv, ag, bias_ref, dk_ref, dv_ref, q_send, q_got, m_send, m_got, s_got, s_send, psend, pgot, n1g,
    send, recv, ring_send, ring_recv, gather_send, gather_recv, local,
):
    rows, width = in_ref.shape
    seq = mg.shape[0]
    cols = wq.shape[2]
    cols3 = 3 * cols
    pairs = cols // PAIR
    blocks = seq // QB
    me = lax.axis_index("tensor")
    core = me % 2
    sib = me + 1 - 2 * core
    far = (me + 2) % 4
    mine, pos, sides = ring_place(n)

    pairs_in = (
        (mg_hbm, mg), (wmf_hbm, wmf), (att_hbm, att), (qkv_hbm, qkv), (rg_hbm, ffg.at[0]), (eg_hbm, ffg.at[1]),
        (rows1_hbm, rows1), (wm_hbm, wm), (wqf_hbm, wqf), (wq_hbm, wq), (x_hbm, x), (rgrad_hbm, rgrad),
    )

    def load(k):
        return pltpu.make_async_copy(pairs_in[k][0], pairs_in[k][1], local.at[k])

    for k in range(len(pairs_in)):
        load(k).start()
    meet((sib, far), sides)

    def remote(src, dst, k, other):
        return pltpu.make_async_remote_copy(
            src_ref=src,
            dst_ref=dst,
            send_sem=send.at[k],
            recv_sem=recv.at[k],
            device_id={"tensor": other},
            device_id_type=MESH_ID,
        )

    def q_across(k):
        return remote(q_send.at[k], q_got.at[k], k, far)

    def m_across():
        return remote(m_send, m_got, 3, far)

    def s_across():
        return remote(s_send, s_got, 4, far)

    def part_beside():
        return remote(psend, pgot, 5, sib)

    def ring_copy(src, kind, d, s):
        return pltpu.make_async_remote_copy(
            src_ref=src,
            dst_ref=rbuf.at[s, kind, d],
            send_sem=ring_send.at[kind, d],
            recv_sem=ring_recv.at[kind, d, s],
            device_id={"dp": sides[d]},
            device_id_type=MESH_ID,
        )

    def part(d, s):
        return ring_index(pos - 1 - s if d == 0 else pos + 1 + s, n)

    def tick(kind, s):
        for d in range(2):
            ring_copy(rbuf.at[s, kind, d], kind, d, s).wait()
            mixed = rbuf[s, kind, d].astype(F32) + ffg[kind, part(d, s + 1), d].astype(F32)
            rbuf[s, kind, d] = mixed.astype(BF)

            @pl.when(s < n - 2)
            def _():
                ring_copy(rbuf.at[s, kind, d], kind, d, s + 1).start()

    outs_hbm = (ro_ref, eo_ref)

    def gather(kind, d, s):
        chunk = ring_index(pos - s if d == 0 else pos + s, n)
        ref = outs_hbm[kind].at[chunk, d]
        return pltpu.make_async_remote_copy(
            src_ref=ref,
            dst_ref=ref,
            send_sem=gather_send.at[kind, d],
            recv_sem=gather_recv.at[kind, d, s],
            device_id={"dp": sides[d]},
            device_id_type=MESH_ID,
        )

    def gather_tick(kind, s):
        for d in range(2):
            gather(kind, d, s).wait()
            if s + 1 < AHEAD:
                gather(kind, d, s + 1).start()

    for kind in range(2):
        for d in range(2):
            ring_copy(carry_hbm.at[kind, d], kind, d, EARLY).start()

    fill_bias(seg_ref, me // 2, bias_ref, blocks)
    masks = half_masks()
    for k in range(6):
        load(k).wait()
    m_send[...] = dot(mg[...], att[:, cols : 2 * cols], TN).astype(BF)
    m_across().start()
    ag[...] = dot(mg[...], wmf[...], NT).astype(BF)

    @pl.loop(0, 2 * pairs)
    def _(q):
        first = q < pairs
        group = 1 - q // pairs
        slot = q % pairs
        base = group * cols3 + slot * PAIR

        @pl.when(q == pairs)
        def _():
            ag[...] = dot(mg[...], wm[...], NT).astype(BF)

        def lanes(k):
            return pl.ds(pl.multiple_of(base + k * cols, PAIR), PAIR)

        own = pl.ds(pl.multiple_of(slot * PAIR, PAIR), PAIR)
        kt = qkv[:, lanes(1)].T
        dk_ref[...] = jnp.zeros_like(dk_ref)
        dv_ref[...] = jnp.zeros_like(dv_ref)
        off = 0
        qsum = jnp.zeros((1, PAIR), F32)
        for i in range(blocks):
            keys = (i + 1) * QB
            at = slice(i * QB, (i + 1) * QB)
            qi = qkv[at, lanes(0)] * jnp.asarray(SCALE, BF)
            gi = ag[at, own]
            kk = qkv[:keys, lanes(1)]
            vv = qkv[:keys, lanes(2)]
            outs = []
            for h in range(2):
                qm = jnp.where(masks[h], qi, jnp.zeros_like(qi))
                gm = jnp.where(masks[h], gi, jnp.zeros_like(gi))
                s = dot(kk, qm, NT) + bias_ref[off : off + keys, :]
                e = jnp.exp(s - jnp.max(s, axis=0, keepdims=True))
                prob = e * (1.0 / jnp.sum(e, axis=0, keepdims=True))
                weighted = prob * dot(vv, gm, NT)
                ds = (weighted - prob * jnp.sum(weighted, axis=0, keepdims=True)).astype(BF)
                dv_ref[:keys, :] += dot(prob.astype(BF), gm)
                dk_ref[:keys, :] += dot(ds, qm)
                outs.append(dot(kt[h * HD : (h + 1) * HD, :keys], ds))
            dq = (jnp.concatenate(outs, axis=0).T * SCALE).astype(BF)
            dqkv[at, lanes(0)] = dq
            qsum += jnp.sum(dq.astype(F32), axis=0, keepdims=True)
            off += keys
            turn = blocks * q + i

            @pl.when(turn < 2 * (n - 1 - EARLY))
            def _():
                tick(turn % 2, EARLY + turn // 2)
        dv = dv_ref[...].astype(BF)
        dqkv[:, lanes(1)] = dk_ref[...].astype(BF)
        dqkv[:, lanes(2)] = dv
        vsum = jnp.sum(dv.astype(F32), axis=0, keepdims=True)
        for (name, sel) in ((s_send, first), (qsum_ref, jnp.logical_not(first))):

            @pl.when(sel)
            def _():
                name[0:1, own] = qsum
                name[1:2, own] = vsum

        @pl.when(q == pairs - 1)
        def _():
            s_across().start()
            load(6).wait()
            load(7).wait()
            for k in range(3):
                to = slice(cols3 + k * cols, cols3 + (k + 1) * cols)
                q_send[k] = dot(rows1[...], dqkv[:, to], TN).astype(BF)
                q_across(k).start()

    @pl.loop(EARLY + blocks * pairs, n - 1)
    def _(s):
        for kind in range(2):
            tick(kind, s)

    puts = [
        pltpu.make_async_copy(rbuf.at[n - 2, kind], outs_hbm[kind].at[mine], local.at[12 + kind])
        for kind in range(2)
    ]
    for put in puts:
        put.start()
    for k in (8, 9):
        load(k).wait()
    for put in puts:
        put.wait()
    for kind in range(2):
        for d in range(2):
            gather(kind, d, 0).start()
    nb = 256

    def back(start, at):
        sel = pl.ds(pl.multiple_of(start, rows), rows)
        total = dot(dqkv[sel, 0:cols], wq[0, at, :], NT)
        for k in range(1, 6):
            w = wq if k < 3 else wqf
            total += dot(dqkv[sel, k * cols : (k + 1) * cols], w[k % 3, at, :], NT)
        return total

    for k in range(width // nb):
        at = slice(k * nb, (k + 1) * nb)
        psend[:, at] = back((1 - core) * rows, at).astype(BF)
        if k % 2 == 1:
            gather_tick(k // 2, 0)
    part_beside().start()
    for k in range(width // nb):
        at = slice(k * nb, (k + 1) * nb)
        n1g[:, at] = back(core * rows, at)
        if k % 2 == 1:
            gather_tick(k // 2, 1)
    part_beside().wait()
    load(10).wait()
    load(11).wait()
    nsum_ref[...] = jnp.zeros_like(nsum_ref)
    step = 64

    @pl.loop(0, rows // step)
    def _(r):
        at = pl.ds(pl.multiple_of(r * step, step), step)
        grad = n1g[at, :] + pgot[at, :].astype(F32)
        normed, scale = norm_stats(x[at, :].astype(F32))
        g = grad * g1_ref[...]
        mean_g = jnp.mean(g, axis=-1, keepdims=True)
        mean_gn = jnp.mean(g * normed, axis=-1, keepdims=True)
        in_ref[at, :] = rgrad[at, :] + scale * (g - mean_g - normed * mean_gn)
        nsum_ref[0:1, :] += jnp.sum(grad * normed, axis=0, keepdims=True)
        nsum_ref[1:2, :] += jnp.sum(grad, axis=0, keepdims=True)

    for kind in range(2):
        gather_tick(kind, 2)
    mixed = dot(mg[...], att[:, 0:cols], TN)
    m_across().wait()
    qg_ref[3] = (mixed + m_got[...].astype(F32)).astype(BF)
    s_across().wait()
    qsum_ref[...] += s_got[...]
    for k in range(3):
        qg = dot(rows1[...], dqkv[:, k * cols : (k + 1) * cols], TN)
        q_across(k).wait()
        qg_ref[k] = (qg + q_got[k].astype(F32)).astype(BF)
    for kind in range(2):
        for s in range(3, AHEAD):
            gather_tick(kind, s)


def backward(mg, qkv, att, rows1, wq, wqf, wm, wmf, x, rgrad, rg, eg, carry, segments, g1, n):
    rows, width = x.shape
    seq = mg.shape[0]
    cols = wq.shape[2]
    blocks = seq // QB
    vmem = pl.BlockSpec(memory_space=pltpu.VMEM)
    anyspace = pl.BlockSpec(memory_space=pl.ANY)
    split = rg.shape
    chunk = split[2:]
    return pl.pallas_call(
        functools.partial(bwd_kernel, n),
        in_specs=[anyspace] * 13 + [vmem] * 2,
        out_specs=[vmem] * 4 + [anyspace] * 2,
        out_shape=[
            jax.ShapeDtypeStruct((rows, width), F32),
            jax.ShapeDtypeStruct((4, width, cols), BF),
            jax.ShapeDtypeStruct((2, cols), F32),
            jax.ShapeDtypeStruct((2, width), F32),
            jax.ShapeDtypeStruct(split, BF),
            jax.ShapeDtypeStruct(split, BF),
        ],
        scratch_shapes=[
            pltpu.VMEM(mg.shape, BF),
            pltpu.VMEM(qkv.shape, BF),
            pltpu.VMEM(att.shape, BF),
            pltpu.VMEM(rows1.shape, BF),
            pltpu.VMEM(wq.shape, BF),
            pltpu.VMEM(wq.shape, BF),
            pltpu.VMEM(wm.shape, BF),
            pltpu.VMEM(wm.shape, BF),
            pltpu.VMEM(x.shape, BF),
            pltpu.VMEM(rgrad.shape, F32),
            pltpu.VMEM((2,) + split, BF),
            pltpu.VMEM((n - 1, 2, 2) + chunk, BF),
            pltpu.VMEM(qkv.shape, BF),
            pltpu.VMEM((seq, cols), BF),
            pltpu.VMEM((QB * blocks * (blocks + 1) // 2, QB), F32),
            pltpu.VMEM((seq, PAIR), F32),
            pltpu.VMEM((seq, PAIR), F32),
            pltpu.VMEM((3, width, cols), BF),
            pltpu.VMEM((3, width, cols), BF),
            pltpu.VMEM((width, cols), BF),
            pltpu.VMEM((width, cols), BF),
            pltpu.VMEM((2, cols), F32),
            pltpu.VMEM((2, cols), F32),
            pltpu.VMEM((rows, width), BF),
            pltpu.VMEM((rows, width), BF),
            pltpu.VMEM((rows, width), F32),
            pltpu.SemaphoreType.DMA((6,)),
            pltpu.SemaphoreType.DMA((6,)),
            pltpu.SemaphoreType.DMA((2, 2)),
            pltpu.SemaphoreType.DMA((2, 2, n - 1)),
            pltpu.SemaphoreType.DMA((2, 2)),
            pltpu.SemaphoreType.DMA((2, 2, n - 1)),
            pltpu.SemaphoreType.DMA((14,)),
        ],
        compiler_params=pltpu.CompilerParams(
            collective_id=4, has_side_effects=True, vmem_limit_bytes=60 << 20
        ),
        name="backward",
    )(mg, qkv, att, rows1, wq, wqf, wm, wmf, x, rgrad, rg, eg, carry, segments, g1)


GA = 0.7978845608028654
GB = 0.044715


def ff_kernel(
    n,
    n2_ref, og_hbm, we_hbm, wr_hbm, resid_hbm, be_ref, gain_ref,
    rgrad_ref, mg_ref, rg_ref, eg_ref, brn_ref, brf_ref, usum_ref, dsum_ref, carry_ref,
    og_ref, we_ref, wr_ref, resid_ref, n2b, act, pg, ng, br, ng_d, br_d, ng_s, br_s, ng_far, ng_out,
    rbuf, send, recv, ring_send, ring_recv, local,
):
    rows, width = n2_ref.shape
    units = we_ref.shape[1]
    part = rows // 2
    nb = 256
    me = lax.axis_index("tensor")
    core = me % 2
    sib = me + 1 - 2 * core
    far = (me + 2) % 4

    mine, pos, sides = ring_place(n)
    meet((sib, far), sides)
    h = rg_ref.shape[2]

    def remote(src, dst, k, other):
        return pltpu.make_async_remote_copy(
            src_ref=src,
            dst_ref=dst,
            send_sem=send.at[k],
            recv_sem=recv.at[k],
            device_id={"tensor": other},
            device_id_type=MESH_ID,
        )

    def y_at(c):
        return pl.ds((2 + c) * rows, part)

    def d_at(c):
        return pl.ds((2 + c) * rows + part, part)

    def rows_across(c):
        return remote(n2_ref.at[pl.ds(c * part, part)], n2b.at[y_at(c)], c, far)

    def rows_beside():
        return remote(n2_ref, n2b.at[pl.ds(rows, rows)], 2, sib)

    def rows_forward(c):
        return remote(n2b.at[y_at(c)], n2b.at[d_at(c)], 3 + c, sib)

    def ng_beside():
        return remote(ng.at[pl.ds(rows, rows)], ng_s, 5, sib)

    def br_beside():
        return remote(br.at[pl.ds(rows, rows)], br_s, 6, sib)

    def ng_combine(c):
        return remote(ng.at[d_at(c)], ng_d.at[c], 7 + c, sib)

    def br_combine(c):
        return remote(br.at[d_at(c)], br_d.at[c], 9 + c, sib)

    def ng_across(c):
        return remote(ng_out.at[c], ng_far.at[c], 11 + c, far)

    def mg_beside(c):
        at = pl.ds(pl.multiple_of(core * rows + c * part, part), part)
        return remote(mg_ref.at[at], mg_ref.at[at], 13 + c, sib)

    for c in range(2):
        rows_across(c).start()
    rows_beside().start()
    first = pl.ds(0, rows)
    rest = pl.ds(rows, 3 * rows)
    loads = [
        pltpu.make_async_copy(n2_ref, n2b.at[first], local.at[0]),
        pltpu.make_async_copy(we_hbm, we_ref, local.at[1]),
        pltpu.make_async_copy(og_hbm.at[first], og_ref.at[first], local.at[2]),
        pltpu.make_async_copy(wr_hbm, wr_ref, local.at[3]),
        pltpu.make_async_copy(og_hbm.at[rest], og_ref.at[rest], local.at[4]),
        pltpu.make_async_copy(resid_hbm, resid_ref, local.at[5]),
    ]
    for load in loads:
        load.start()
    usum_ref[...] = jnp.zeros_like(usum_ref)
    for load in loads[:4]:
        load.wait()

    @pl.loop(0, 4)
    def _(b):
        at = pl.ds(pl.multiple_of(b * rows, rows), rows)
        c = b - 2

        @pl.when(b == 1)
        def _():
            rows_beside().wait()
            loads[4].wait()

        @pl.when(b >= 2)
        def _():
            rows_across(c).wait()
            rows_forward(c).start()
            rows_forward(c).wait()

        for k in range(units // nb):
            cols = slice(k * nb, (k + 1) * nb)
            u = dot(n2b[at, :], we_ref[:, cols]) + be_ref[:, cols]
            act_grad = dot(og_ref[at, :], wr_ref[cols, :], NT)
            sq = u * u
            th = jnp.tanh(u * (GA + (GA * GB) * sq))
            cdf = 0.5 * (1.0 + th)
            slope = cdf + (0.5 * u) * (1.0 - th * th) * (GA + (3.0 * GA * GB) * sq)
            pre = (act_grad * slope).astype(BF)
            act[at, cols] = (u * cdf).astype(BF)
            pg[at, cols] = pre
            usum_ref[:, cols] += jnp.sum(pre.astype(F32), axis=0, keepdims=True)
        for k in range(width // nb):
            cols = slice(k * nb, (k + 1) * nb)
            ng[at, cols] = dot(pg[at, :], we_ref[cols, :], NT).astype(BF)

        @pl.when(b == 1)
        def _():
            ng_beside().start()

        @pl.when(b >= 2)
        def _():
            ng_combine(c).start()

        for k in range(width // nb):
            cols = slice(k * nb, (k + 1) * nb)
            br[at, cols] = dot(act[at, :], wr_ref[:, cols]).astype(BF)

        @pl.when(b == 1)
        def _():
            br_beside().start()

        @pl.when(b >= 2)
        def _():
            br_combine(c).start()
            ng_combine(c).wait()
            ng_out[c] = (ng[y_at(c), :].astype(F32) + ng_d[c].astype(F32)).astype(BF)
            ng_across(c).start()

    def part_of(d, s):
        return ring_index(pos - 1 - s if d == 0 else pos + 1 + s, n)

    def ring_copy(src, kind, d, s):
        return pltpu.make_async_remote_copy(
            src_ref=src,
            dst_ref=rbuf.at[s, kind, d],
            send_sem=ring_send.at[kind, d],
            recv_sem=ring_recv.at[kind, d, s],
            device_id={"dp": sides[d]},
            device_id_type=MESH_ID,
        )

    ffg = (rg_ref, eg_ref)

    def ring_start(kind):
        for d in range(2):
            ring_copy(ffg[kind].at[part_of(d, 0), d], kind, d, 0).start()

    def tick(kind, s):
        for d in range(2):
            ring_copy(rbuf.at[s, kind, d], kind, d, s).wait()
            total = rbuf[s, kind, d].astype(F32) + ffg[kind][part_of(d, s + 1), d].astype(F32)
            rbuf[s, kind, d] = total.astype(BF)
            if s + 1 < EARLY:
                ring_copy(rbuf.at[s, kind, d], kind, d, s + 1).start()

    @pl.loop(0, width // nb)
    def _(k):
        cols = pl.ds(pl.multiple_of(k * nb, nb), nb)
        grad = dot(act[...], og_ref[:, cols], TN).astype(BF)
        rg_ref[:, :, :, cols] = grad.reshape(n, 2, h, nb)

    ring_start(0)

    @pl.loop(0, width // nb)
    def _(k):
        cols = pl.ds(pl.multiple_of(k * nb, nb), nb)
        grad = dot(n2b[...], pg[:, cols], TN).astype(BF)
        eg_ref[:, :, :, cols] = grad.reshape(n, 2, h, nb)

    ring_start(1)
    br_beside().wait()
    brn_ref[...] = (br[0:rows, :].astype(F32) + br_s[...].astype(F32)).astype(BF)
    for c in range(2):
        br_combine(c).wait()
        brf_ref[c * part : (c + 1) * part, :] = (
            br[y_at(c), :].astype(F32) + br_d[c].astype(F32)
        ).astype(BF)
    ng_beside().wait()
    loads[5].wait()
    dsum_ref[...] = jnp.zeros_like(dsum_ref)
    step = 64
    for c in range(2):
        ng_across(c).wait()

        @pl.loop(0, part // step)
        def _(r):
            inner = pl.ds(pl.multiple_of(r * step, step), step)
            at = pl.ds(pl.multiple_of(c * part + r * step, step), step)
            grad = ng[at, :].astype(F32) + ng_s[at, :].astype(F32) + ng_far[c, inner, :].astype(F32)
            normed, scale = norm_stats(resid_ref[at, :])
            g = grad * gain_ref[...]
            gn = g * normed
            mean_g = jnp.mean(g, axis=-1, keepdims=True)
            mean_gn = jnp.mean(gn, axis=-1, keepdims=True)
            og = og_ref[at, :].astype(F32)
            rgrad = og + scale * (g - mean_g - normed * mean_gn)
            rgrad_ref[at, :] = rgrad
            mg = rgrad.astype(BF)
            mg_ref[pl.ds(pl.multiple_of(core * rows + c * part + r * step, step), step), :] = mg
            dsum_ref[0:1, :] += jnp.sum(mg.astype(F32), axis=0, keepdims=True)
            dsum_ref[1:2, :] += jnp.sum(grad * normed, axis=0, keepdims=True)
            dsum_ref[2:3, :] += jnp.sum(grad, axis=0, keepdims=True)
            dsum_ref[3:4, :] += jnp.sum(og, axis=0, keepdims=True)

        mg_beside(c).start()
        if c == 0:
            for s in range(EARLY):
                tick(0, s)
    for s in range(EARLY):
        tick(1, s)
    carry_ref[...] = rbuf[EARLY - 1]
    for c in range(2):
        mg_beside(c).wait()


def ff(n2, og_all, we, wr, be, resid, gain, n):
    rows, width = n2.shape
    units = we.shape[1]
    part = rows // 2
    vmem = pl.BlockSpec(memory_space=pltpu.VMEM)
    anyspace = pl.BlockSpec(memory_space=pl.ANY)
    return pl.pallas_call(
        functools.partial(ff_kernel, n),
        in_specs=[anyspace] * 5 + [vmem] * 2,
        out_specs=[vmem] * 9,
        out_shape=[
            jax.ShapeDtypeStruct((rows, width), F32),
            jax.ShapeDtypeStruct((2 * rows, width), BF),
            jax.ShapeDtypeStruct((n, 2, units // (2 * n), width), BF),
            jax.ShapeDtypeStruct((n, 2, width // (2 * n), units), BF),
            jax.ShapeDtypeStruct((rows, width), BF),
            jax.ShapeDtypeStruct((rows, width), BF),
            jax.ShapeDtypeStruct((1, units), F32),
            jax.ShapeDtypeStruct((4, width), F32),
            jax.ShapeDtypeStruct((2, 2, units // (2 * n), width), BF),
        ],
        scratch_shapes=[
            pltpu.VMEM((4 * rows, width), BF),
            pltpu.VMEM(we.shape, BF),
            pltpu.VMEM(wr.shape, BF),
            pltpu.VMEM((rows, width), F32),
            pltpu.VMEM((4 * rows, width), BF),
            pltpu.VMEM((4 * rows, units), BF),
            pltpu.VMEM((4 * rows, units), BF),
            pltpu.VMEM((4 * rows, width), BF),
            pltpu.VMEM((4 * rows, width), BF),
            pltpu.VMEM((2, part, width), BF),
            pltpu.VMEM((2, part, width), BF),
            pltpu.VMEM((rows, width), BF),
            pltpu.VMEM((rows, width), BF),
            pltpu.VMEM((2, part, width), BF),
            pltpu.VMEM((2, part, width), BF),
            pltpu.VMEM((EARLY, 2, 2, units // (2 * n), width), BF),
            pltpu.SemaphoreType.DMA((15,)),
            pltpu.SemaphoreType.DMA((15,)),
            pltpu.SemaphoreType.DMA((2, 2)),
            pltpu.SemaphoreType.DMA((2, 2, EARLY)),
            pltpu.SemaphoreType.DMA((6,)),
        ],
        compiler_params=pltpu.CompilerParams(
            collective_id=2, has_side_effects=True, vmem_limit_bytes=60 << 20
        ),
        name="ff",
    )(n2, og_all, we, wr, resid, be, gain)


def ring_kernel(
    n, g_ref, small_ref, rbias_ref, resid_hbm, brn_hbm, brf_hbm, _r, _e,
    qo_ref, mo_ref, ro_ref, eo_ref, so_ref, bo_ref,
    buf, sbuf, sall, speer, ssum, resid, brn, bro,
    send, recv, fsend, frecv, ssend, srecv, tsend, trecv, local,
):
    mine, pos, sides = ring_place(n)
    me = lax.axis_index("tensor")
    far = (me + 2) % 4
    peers = [(me + k) % 4 for k in range(1, 4)]
    loads = (
        pltpu.make_async_copy(resid_hbm, resid, local.at[0]),
        pltpu.make_async_copy(brn_hbm, brn, local.at[1]),
    )
    for load in loads:
        load.start()
    meet(peers, sides)

    def remote(src, dst, kind, d, s):
        return pltpu.make_async_remote_copy(
            src_ref=src,
            dst_ref=dst,
            send_sem=send.at[kind, d],
            recv_sem=recv.at[kind, d, s],
            device_id={"dp": sides[d]},
            device_id_type=MESH_ID,
        )

    def little(src, dst, kind, s):
        return pltpu.make_async_remote_copy(
            src_ref=src,
            dst_ref=dst,
            send_sem=ssend.at[kind],
            recv_sem=srecv.at[kind, s],
            device_id={"dp": sides[0]},
            device_id_type=MESH_ID,
        )

    def beside(src, dst, k, other):
        return pltpu.make_async_remote_copy(
            src_ref=src,
            dst_ref=dst,
            send_sem=tsend.at[k],
            recv_sem=trecv.at[k],
            device_id={"tensor": other},
            device_id_type=MESH_ID,
        )

    def share(k):
        return beside(small_ref, speer.at[k], k, peers[k])

    def branch():
        return beside(brf_hbm, bro, 3, far)

    def part(d, s):
        return ring_index(pos - 1 - s if d == 0 else pos + 1 + s, n)

    def held(d, s):
        return ring_index(pos - s if d == 0 else pos + s, n)

    streams = [(k, d) for k in range(3) for d in range(2)]
    spans = ((0, 2), (2, 1), (3, 1))

    def source(k, chunk, d):
        return g_ref.at[pl.ds(*spans[k]), chunk, d]

    def slot(k, s, d):
        return buf.at[s, d, pl.ds(*spans[k])]

    def put_at(k, chunk, d):
        return qo_ref.at[pl.ds(*spans[k]), chunk, d] if k < 2 else mo_ref.at[pl.ds(0, 1), chunk, d]

    def add(k, d, s):
        ref = slot(k, s, d)
        total = ref[...].astype(F32) + source(k, part(d, s + 1), d)[...].astype(F32)
        ref[...] = total.astype(BF)

    def gather(k, d, s):
        ref = put_at(k, held(d, s), d)
        return remote(ref, ref, 3 + k, d, s)

    left = n - 1 - AHEAD
    half = ro_ref.shape[3] // 2

    def ff_hop(kind, c, d, s):
        ref = (ro_ref, eo_ref)[kind].at[held(d, s), d, :, pl.ds(c * half, half)]
        k = 2 * kind + c
        return pltpu.make_async_remote_copy(
            src_ref=ref,
            dst_ref=ref,
            send_sem=fsend.at[k, d],
            recv_sem=frecv.at[k, d, s - AHEAD],
            device_id={"dp": sides[d]},
            device_id_type=MESH_ID,
        )

    def beside_step(kind, s, act):
        @pl.when(s < left)
        def _():
            for d in range(2):
                act(ff_hop(kind, 0, d, AHEAD + s))

        @pl.when(s >= n - 1 - left)
        def _():
            for d in range(2):
                act(ff_hop(kind, 1, d, AHEAD + s - (n - 1 - left)))

    def start(copy):
        copy.start()

    def finish(copy):
        copy.wait()

    def gather_small(s):
        ref = sall.at[held(0, s)]
        return little(ref, ref, 1, s)

    for k, d in streams:
        remote(source(k, part(d, 0), d), slot(k, 0, d), k, d, 0).start()
    for k in range(3):
        share(k).start()
    branch().start()
    for k in range(3):
        share(k).wait()
    ssum[...] = small_ref[...]
    shared = n * 6 // 8
    ssum[0:shared] = ssum[0:shared] + speer[0, 0:shared] + speer[1, 0:shared] + speer[2, 0:shared]
    little(ssum.at[part(0, 0)], sbuf.at[0], 0, 0).start()

    @pl.loop(0, n - 2)
    def _(s):
        beside_step(0, s, start)
        for k, d in streams:
            remote(slot(k, s, d), slot(k, s, d), k, d, s).wait()
            add(k, d, s)
            remote(slot(k, s, d), slot(k, s + 1, d), k, d, s + 1).start()
        little(sbuf.at[s], sbuf.at[s], 0, s).wait()
        sbuf[s] = sbuf[s] + ssum[part(0, s + 1)]
        little(sbuf.at[s], sbuf.at[s + 1], 0, s + 1).start()
        beside_step(0, s, finish)

    last = n - 2
    beside_step(0, last, start)
    puts = []
    for k, d in streams:
        remote(slot(k, last, d), slot(k, last, d), k, d, last).wait()
        add(k, d, last)
        put = pltpu.make_async_copy(slot(k, last, d), put_at(k, mine, d), local.at[2 + 2 * k + d])
        put.start()
        puts.append(put)
    for (k, d), put in zip(streams, puts):
        put.wait()
        gather(k, d, 0).start()
    little(sbuf.at[last], sbuf.at[last], 0, last).wait()
    sall[mine] = sbuf[last] + ssum[mine]
    gather_small(0).start()
    beside_step(0, last, finish)

    @pl.loop(0, n - 2)
    def _(s):
        beside_step(1, s, start)
        for k, d in streams:
            gather(k, d, s).wait()
            gather(k, d, s + 1).start()
        gather_small(s).wait()
        gather_small(s + 1).start()
        beside_step(1, s, finish)

    beside_step(1, last, start)

    branch().wait()
    for load in loads:
        load.wait()
    step = 64

    @pl.loop(0, bo_ref.shape[0] // step)
    def _(r):
        at = pl.ds(pl.multiple_of(r * step, step), step)
        total = resid[at, :] + brn[at, :].astype(F32) + bro[at, :].astype(F32) + rbias_ref[...]
        bo_ref[at, :] = total.astype(BF)

    for k, d in streams:
        gather(k, d, last).wait()
    gather_small(last).wait()
    so_ref[...] = sall[...]
    beside_step(1, last, finish)


def ring_sum(g, small, resid, brn, brf, r, e, rbias, n):
    split = (4, n, 2, g.shape[1] // (2 * n), g.shape[2])
    s3 = small.reshape(n, 1, small.size // n)
    vmem = pl.BlockSpec(memory_space=pltpu.VMEM)
    anyspace = pl.BlockSpec(memory_space=pl.ANY)
    qo, mo, ro, eo, so, bo = pl.pallas_call(
        functools.partial(ring_kernel, n),
        in_specs=[vmem] * 3 + [anyspace] * 5,
        out_specs=[anyspace] * 4 + [vmem] * 2,
        input_output_aliases={6: 2, 7: 3},
        out_shape=[
            jax.ShapeDtypeStruct((3,) + split[1:], BF),
            jax.ShapeDtypeStruct((1,) + split[1:], BF),
            jax.ShapeDtypeStruct(r.shape, BF),
            jax.ShapeDtypeStruct(e.shape, BF),
            jax.ShapeDtypeStruct(s3.shape, F32),
            jax.ShapeDtypeStruct(brf.shape, BF),
        ],
        scratch_shapes=[
            pltpu.VMEM((n - 1, 2, 4) + split[3:], BF),
            pltpu.VMEM((n - 1,) + s3.shape[1:], F32),
            pltpu.VMEM(s3.shape, F32),
            pltpu.VMEM((3,) + s3.shape, F32),
            pltpu.VMEM(s3.shape, F32),
            pltpu.VMEM(resid.shape, F32),
            pltpu.VMEM(brn.shape, BF),
            pltpu.VMEM(brf.shape, BF),
            pltpu.SemaphoreType.DMA((6, 2)),
            pltpu.SemaphoreType.DMA((6, 2, n - 1)),
            pltpu.SemaphoreType.DMA((4, 2)),
            pltpu.SemaphoreType.DMA((4, 2, n - 1 - AHEAD)),
            pltpu.SemaphoreType.DMA((2,)),
            pltpu.SemaphoreType.DMA((2, n - 1)),
            pltpu.SemaphoreType.DMA((4,)),
            pltpu.SemaphoreType.DMA((4,)),
            pltpu.SemaphoreType.DMA((8,)),
        ],
        compiler_params=pltpu.CompilerParams(
            collective_id=1, has_side_effects=True, vmem_limit_bytes=60 << 20
        ),
        name="ring_sum",
    )(g.reshape(split), s3, rbias, resid, brn, brf, r, e)
    wide = (-1, r.shape[-1])
    return (
        qo.reshape((3,) + g.shape[1:]),
        mo.reshape(g.shape[1:]),
        ro.reshape(wide),
        eo.reshape(wide),
        so.reshape(small.shape),
        bo,
    )


def body(
    block_in,
    segments,
    first_gain,
    first_shift,
    w_qkv,
    qv_bias,
    w_mix,
    mix_bias,
    second_gain,
    second_shift,
    w_expand,
    expand_bias,
    w_reduce,
    reduce_bias,
    out_grad,
):
    width = block_in.shape[1]
    cols = w_qkv.shape[2]
    units = w_expand.shape[1]
    dp_size = lax.axis_size("dp")
    flat = (1, width)
    wq = w_qkv.transpose(1, 0, 2)
    rows1, qkv, att, resid, n2, wq_far, wm_far, og_all = forward(
        block_in,
        segments,
        first_gain.reshape(flat),
        first_shift.reshape(flat),
        qv_bias,
        mix_bias.reshape(flat),
        second_gain.reshape(flat),
        second_shift.reshape(flat),
        wq,
        w_mix,
        out_grad,
        dp_size,
    )
    resid_grad, mg_all, reduce_grad, expand_grad, br_near, br_far, unit_sums, sums2, carry = ff(
        n2, og_all, w_expand, w_reduce, expand_bias.reshape(1, units), resid, second_gain.reshape(flat), dp_size
    )
    in_grad, grads, qv_sums, norm_sums, reduce_all, expand_all = backward(
        mg_all,
        qkv,
        att,
        rows1,
        wq,
        wq_far,
        w_mix,
        wm_far,
        block_in,
        resid_grad,
        reduce_grad,
        expand_grad,
        carry,
        segments,
        first_gain.reshape(flat),
        dp_size,
    )
    small = jnp.concatenate(
        [
            norm_sums,
            sums2,
            unit_sums,
            jnp.pad(qv_sums.reshape(1, 2 * cols), ((0, 0), (0, width - 2 * cols))),
        ],
        axis=0,
    )
    qkv_grad, mix_grad, reduce_all, expand_all, small, block_out = ring_sum(
        grads,
        small,
        resid,
        br_near,
        br_far,
        reduce_all,
        expand_all,
        reduce_bias.reshape(flat),
        dp_size,
    )
    return (
        block_out,
        in_grad,
        small[0],
        small[1],
        qkv_grad.astype(F32).transpose(1, 0, 2),
        small[7, : 2 * cols].reshape(2, cols),
        mix_grad.astype(F32).T,
        small[2],
        small[3],
        small[4],
        expand_all.astype(F32),
        small[6],
        reduce_all.astype(F32),
        small[5],
    )


def solution(mesh):
    both = P(("dp", "tensor"), None)
    return jax.shard_map(
        body,
        mesh=mesh,
        in_specs=(
            both,
            P("dp", None),
            P(),
            P(),
            P(None, None, "tensor"),
            P(None, "tensor"),
            P("tensor", None),
            P(),
            P(),
            P(),
            P(None, "tensor"),
            P("tensor"),
            P("tensor", None),
            P(),
            both,
        ),
        out_specs=(
            both,
            both,
            P(),
            P(),
            P(None, None, "tensor"),
            P(None, "tensor"),
            P("tensor", None),
            P(),
            P(),
            P(),
            P(None, "tensor"),
            P("tensor"),
            P("tensor", None),
            P(),
        ),
        check_vma=False,
    )
```

```python
import functools

import jax
import jax.numpy as jnp
from jax import lax
from jax.experimental import pallas as pl
from jax.experimental.pallas import tpu as pltpu
from jax.sharding import PartitionSpec as P

HD = 64
PAIR = 2 * HD
QB = 256
EPS = 1e-5
BF = jnp.bfloat16
F32 = jnp.float32
SCALE = HD ** (-0.5)
MESH_ID = pl.DeviceIdType.MESH
EARLY = 1
AHEAD = 4
NT = (((1,), (1,)), ((), ()))
TN = (((0,), (0,)), ((), ()))


def dot(a, b, dims=(((1,), (0,)), ((), ()))):
    return lax.dot_general(a, b, dims, preferred_element_type=F32)


def norm_stats(values):
    mean = jnp.mean(values, axis=-1, keepdims=True)
    centered = values - mean
    variance = jnp.mean(centered * centered, axis=-1, keepdims=True)
    scale = lax.rsqrt(variance + EPS)
    return centered * scale, scale


def fill_bias(seg_ref, row, bias_ref, blocks):
    segr = seg_ref[pl.ds(row, 1), :].astype(F32)
    segc = jnp.broadcast_to(segr, (8, segr.shape[1])).T[:, 0:1]
    off = 0
    for i in range(blocks):
        keys = (i + 1) * QB
        kpos = lax.broadcasted_iota(jnp.int32, (keys, QB), 0)
        qpos = lax.broadcasted_iota(jnp.int32, (keys, QB), 1) + i * QB
        same = segc[:keys, :] == segr[:, i * QB : (i + 1) * QB]
        allowed = jnp.logical_and(kpos <= qpos, same)
        bias_ref[off : off + keys, :] = jnp.where(allowed, 0.0, -1e30)
        off += keys


def half_masks():
    lane = lax.broadcasted_iota(jnp.int32, (1, PAIR), 1)
    return (lane < HD, lane >= HD)


def ring_index(at, n):
    at = (at + 2 * n) % n
    far = at // (n // 2)
    return (1 - far) * 2 * at + far * (2 * (n - 1 - at) + 1)


def ring_place(n):
    mine = lax.axis_index("dp")
    odd = mine % 2
    pos = (1 - odd) * (mine // 2) + odd * (n - 1 - mine // 2)
    return mine, pos, (ring_index(pos + 1, n), ring_index(pos - 1, n))


def meet(tensor_peers, dp_peers):
    barrier = pltpu.get_barrier_semaphore()
    for other in tensor_peers:
        pl.semaphore_signal(barrier, inc=1, device_id={"tensor": other}, device_id_type=MESH_ID)
    for other in dp_peers:
        pl.semaphore_signal(barrier, inc=1, device_id={"dp": other}, device_id_type=MESH_ID)
    pl.semaphore_wait(barrier, len(tensor_peers) + len(dp_peers))


def both_heads(a, masks):
    zero = jnp.zeros_like(a)
    return jnp.concatenate([jnp.where(masks[0], a, zero), jnp.where(masks[1], a, zero)], axis=0)


def twice(a):
    return jnp.concatenate([a, a], axis=1)


def fwd_kernel(
    n,
    x_ref, seg_ref, g1_ref, s1_ref, bq_ref, mixb_ref, g2_ref, s2_ref, wq_hbm, wm_hbm, og_ref,
    rows1_out, qkv_out, att_out, resid_out, n2_out, wqf_out, wmf_out, oga_ref,
    rows1_ref, qkv_ref, att_ref, resid_ref, n2_ref, w_all, wm_all,
    b_all, bqf, bias_ref, psend, pgot, send, recv, ring_send, ring_recv, local, out,
):
    rows, width = x_ref.shape
    seq = rows1_ref.shape[0]
    cols = w_all.shape[3]
    wqf_ref = w_all.at[1]
    wmf_ref = wm_all.at[1]
    cols3 = 3 * cols
    half = rows // 2
    blocks = seq // QB
    me = lax.axis_index("tensor")
    core = me % 2
    sib = me + 1 - 2 * core
    far = (me + 2) % 4
    mine, pos, sides = ring_place(n)
    meet((sib, far), sides)

    def remote(src, dst, k, other):
        return pltpu.make_async_remote_copy(
            src_ref=src,
            dst_ref=dst,
            send_sem=send.at[k],
            recv_sem=recv.at[k],
            device_id={"tensor": other},
            device_id_type=MESH_ID,
        )

    slab = width // n
    wide = cols // 2

    def slab_rows(chunk):
        return pl.ds(pl.multiple_of(chunk * slab, slab), slab)

    def piece():
        return remote(wq_hbm.at[:, slab_rows(mine)], wqf_ref.at[:, slab_rows(mine)], 0, far)

    def bias_across():
        return remote(bq_ref, bqf, 1, far)

    def own_half(c):
        return pl.ds(pl.multiple_of(core * rows + c * half, half), half)

    def rows_beside(c):
        return remote(rows1_ref.at[own_half(c)], rows1_ref.at[own_half(c)], 2 + c, sib)

    def mix_across():
        return remote(wm_hbm, wmf_ref, 4, far)

    def og_across(c):
        return remote(
            og_ref.at[pl.ds(c * half, half)], oga_ref.at[pl.ds((2 + c) * rows, half)], 5 + c, far
        )

    def og_beside():
        return remote(og_ref, oga_ref.at[pl.ds(rows, rows)], 7, sib)

    def og_forward(c):
        return remote(
            oga_ref.at[pl.ds((2 + c) * rows, half)],
            oga_ref.at[pl.ds((2 + c) * rows + half, half)],
            8 + c,
            sib,
        )

    def part_beside():
        return remote(psend, pgot, 10, sib)

    def og_own():
        return pltpu.make_async_copy(og_ref, oga_ref.at[pl.ds(0, rows)], local.at[0])

    def hop(k, d, s):
        chunk = ring_index(pos - s if d == 0 else pos + s, n)
        ref = wqf_ref.at[k, slab_rows(chunk), d * wide : (d + 1) * wide]
        return pltpu.make_async_remote_copy(
            src_ref=ref,
            dst_ref=ref,
            send_sem=ring_send.at[k, d],
            recv_sem=ring_recv.at[k, d, s],
            device_id={"dp": sides[d]},
            device_id_type=MESH_ID,
        )

    def tick(s):
        for k in range(3):
            for d in range(2):
                hop(k, d, s).wait()

                @pl.when(s < n - 2)
                def _():
                    hop(k, d, s + 1).start()

    def put(k):
        near = pl.ds(0, cols3)
        far_part = pl.ds(cols3, cols3)
        low, high = pl.ds(0, half), pl.ds(half, half)
        src, dst = (
            (rows1_ref, rows1_out),
            (qkv_ref.at[:, near], qkv_out.at[:, near]),
            (qkv_ref.at[:, far_part], qkv_out.at[:, far_part]),
            (wqf_ref, wqf_out),
            (wmf_ref, wmf_out),
            (att_ref, att_out),
            (resid_ref.at[low], resid_out.at[low]),
            (resid_ref.at[high], resid_out.at[high]),
            (n2_ref.at[low], n2_out.at[low]),
            (n2_ref.at[high], n2_out.at[high]),
        )[k]
        return pltpu.make_async_copy(src, dst, out.at[k])

    piece().start()
    bias_across().start()
    loads = (
        pltpu.make_async_copy(wq_hbm, w_all.at[0], local.at[1]),
        pltpu.make_async_copy(wm_hbm, wm_all.at[0], local.at[2]),
    )
    for load in loads:
        load.start()
    step = 64
    for c in range(2):

        @pl.loop(0, half // step)
        def _(r):
            normed = norm_stats(x_ref[pl.ds(pl.multiple_of(c * half + r * step, step), step), :].astype(F32))[0]
            to = pl.ds(pl.multiple_of(core * rows + c * half + r * step, step), step)
            rows1_ref[to, :] = (normed * g1_ref[...] + s1_ref[...]).astype(BF)

        rows_beside(c).start()
    piece().wait()
    for k in range(3):
        for d in range(2):
            hop(k, d, 0).start()
    mix_across().start()
    for c in range(2):
        og_across(c).start()
    og_beside().start()
    og_own().start()
    fill_bias(seg_ref, me // 2, bias_ref, blocks)

    def fill_shift(g, ref):
        b_all[g, 0:1] = ref[0:1]
        b_all[g, 1:2] = jnp.zeros_like(ref[0:1])
        b_all[g, 2:3] = ref[1:2]

    fill_shift(0, bq_ref)
    for c in range(2):
        rows_beside(c).wait()
    for load in loads:
        load.wait()
    put(0).start()
    masks = half_masks()
    pairs = cols // PAIR
    ticks = 1 + 2 * pairs

    @pl.loop(0, 2 * pairs)
    def _(p):
        group = p // pairs

        @pl.when(p == pairs)
        def _():
            @pl.loop(ticks, n - 1)
            def _(s):
                tick(s)

            bias_across().wait()
            fill_shift(1, bqf)
            put(3).start()

        @pl.when(p % pairs == 0)
        def _():
            @pl.loop(0, 3)
            def _(k):
                to = pl.ds(pl.multiple_of(group * cols3 + k * cols, cols), cols)
                part = dot(rows1_ref[...], w_all[group, k]) + b_all[group, pl.ds(k, 1)]
                qkv_ref[:, to] = part.astype(BF)

        @pl.when(p == 0)
        def _():
            put(1).start()
            tick(0)

        @pl.when(p == pairs)
        def _():
            put(2).start()

        base = group * cols3 + (p % pairs) * PAIR

        def lanes(k):
            return pl.ds(pl.multiple_of(base + k * cols, PAIR), PAIR)

        vt = qkv_ref[:, lanes(2)].T
        off = 0
        for i in range(blocks):
            keys = (i + 1) * QB
            at = slice(i * QB, (i + 1) * QB)
            qi = qkv_ref[at, lanes(0)] * jnp.asarray(SCALE, BF)
            kk = qkv_ref[:keys, lanes(1)]
            s = dot(kk, both_heads(qi, masks), NT) + twice(bias_ref[off : off + keys, :])
            e = jnp.exp(s - jnp.max(s, axis=0, keepdims=True))
            inverse = 1.0 / jnp.sum(e, axis=0, keepdims=True)
            e = e.astype(BF)
            outs = []
            for h in range(2):
                side = slice(h * QB, (h + 1) * QB)
                outs.append(dot(vt[h * HD : (h + 1) * HD, :keys], e[:, side]) * inverse[:, side])
            att_ref[at, pl.ds(pl.multiple_of(p * PAIR, PAIR), PAIR)] = jnp.concatenate(outs, axis=0).T.astype(BF)
            off += keys
            if i % 2 == 1:

                @pl.when(p < pairs)
                def _():
                    tick(1 + 2 * p + i // 2)

    mix_across().wait()
    put(4).start()
    put(5).start()
    nb = 256

    def mixed(start, at):
        sel = pl.ds(pl.multiple_of(start, rows), rows)
        total = dot(att_ref[sel, 0:cols], wm_all[0, :, at])
        return total + dot(att_ref[sel, cols : 2 * cols], wm_all[1, :, at])

    @pl.loop(0, width // nb)
    def _(k):
        at = pl.ds(pl.multiple_of(k * nb, nb), nb)
        psend[:, at] = mixed((1 - core) * rows, at).astype(BF)

    part_beside().start()

    @pl.loop(0, width // nb)
    def _(k):
        at = pl.ds(pl.multiple_of(k * nb, nb), nb)
        resid_ref[:, at] = x_ref[:, at].astype(F32) + mixed(core * rows, at) + mixb_ref[:, at]

    for c in range(2):
        og_across(c).wait()
        og_forward(c).start()
    part_beside().wait()

    for c in range(2):

        @pl.loop(0, half // step)
        def _(r):
            at = pl.ds(pl.multiple_of(c * half + r * step, step), step)
            full = resid_ref[at, :] + pgot[at, :].astype(F32)
            resid_ref[at, :] = full
            n2_ref[at, :] = (norm_stats(full)[0] * g2_ref[...] + s2_ref[...]).astype(BF)

        put(6 + c).start()
        put(8 + c).start()

    for k in range(10):
        put(k).wait()
    og_own().wait()
    og_beside().wait()
    for c in range(2):
        og_forward(c).wait()


def forward(x, segments, g1, s1, bq, mixb, g2, s2, wq, wm, og, n):
    rows, width = x.shape
    seq = segments.shape[1]
    cols = wq.shape[2]
    blocks = seq // QB
    vmem = pl.BlockSpec(memory_space=pltpu.VMEM)
    anyspace = pl.BlockSpec(memory_space=pl.ANY)
    return pl.pallas_call(
        functools.partial(fwd_kernel, n),
        in_specs=[vmem] * 8 + [anyspace] * 3,
        out_specs=[anyspace] * 8,
        out_shape=[
            jax.ShapeDtypeStruct((seq, width), BF),
            jax.ShapeDtypeStruct((seq, 6 * cols), BF),
            jax.ShapeDtypeStruct((seq, 2 * cols), BF),
            jax.ShapeDtypeStruct((rows, width), F32),
            jax.ShapeDtypeStruct((rows, width), BF),
            jax.ShapeDtypeStruct(wq.shape, BF),
            jax.ShapeDtypeStruct(wm.shape, BF),
            jax.ShapeDtypeStruct((4 * rows, width), BF),
        ],
        scratch_shapes=[
            pltpu.VMEM((seq, width), BF),
            pltpu.VMEM((seq, 6 * cols), BF),
            pltpu.VMEM((seq, 2 * cols), BF),
            pltpu.VMEM((rows, width), F32),
            pltpu.VMEM((rows, width), BF),
            pltpu.VMEM((2,) + wq.shape, BF),
            pltpu.VMEM((2,) + wm.shape, BF),
            pltpu.VMEM((2, 3, cols), F32),
            pltpu.VMEM((2, cols), F32),
            pltpu.VMEM((QB * blocks * (blocks + 1) // 2, QB), F32),
            pltpu.VMEM((rows, width), BF),
            pltpu.VMEM((rows, width), BF),
            pltpu.SemaphoreType.DMA((11,)),
            pltpu.SemaphoreType.DMA((11,)),
            pltpu.SemaphoreType.DMA((3, 2)),
            pltpu.SemaphoreType.DMA((3, 2, n - 1)),
            pltpu.SemaphoreType.DMA((3,)),
            pltpu.SemaphoreType.DMA((10,)),
        ],
        compiler_params=pltpu.CompilerParams(
            collective_id=3, has_side_effects=True, vmem_limit_bytes=56 << 20
        ),
        name="forward",
    )(x, segments, g1, s1, bq, mixb, g2, s2, wq, wm, og)


def bwd_kernel(
    n,
    mg_hbm, qkv_hbm, att_hbm, rows1_hbm, wq_hbm, wqf_hbm, wm_hbm, wmf_hbm, x_hbm, rgrad_hbm, rg_hbm, eg_hbm, carry_hbm,
    seg_ref, g1_ref,
    in_out, qg_out, qsum_ref, nsum_ref, ro_ref, eo_ref,
    in_ref, qg_ref,
    mg, qkv, att, rows1, wq, wqf, wm, wmf, x, rgrad, ffg,
    rbuf, dqkv, ag, bias_ref, dk_ref, dv_ref, q_send, q_got, m_send, m_got, s_got, s_send, psend, pgot, n1g,
    send, recv, ring_send, ring_recv, gather_send, gather_recv, local, out,
):
    rows, width = in_ref.shape
    seq = mg.shape[0]
    cols = wq.shape[2]
    cols3 = 3 * cols
    pairs = cols // PAIR
    blocks = seq // QB
    me = lax.axis_index("tensor")
    core = me % 2
    sib = me + 1 - 2 * core
    far = (me + 2) % 4
    mine, pos, sides = ring_place(n)

    pairs_in = (
        (mg_hbm, mg), (wmf_hbm, wmf), (att_hbm, att), (qkv_hbm, qkv), (rg_hbm, ffg.at[0]), (eg_hbm, ffg.at[1]),
        (rows1_hbm, rows1), (wm_hbm, wm), (wqf_hbm, wqf), (wq_hbm, wq), (x_hbm, x), (rgrad_hbm, rgrad),
    )

    def load(k):
        return pltpu.make_async_copy(pairs_in[k][0], pairs_in[k][1], local.at[k])

    for k in range(len(pairs_in)):
        load(k).start()
    meet((sib, far), sides)

    def remote(src, dst, k, other):
        return pltpu.make_async_remote_copy(
            src_ref=src,
            dst_ref=dst,
            send_sem=send.at[k],
            recv_sem=recv.at[k],
            device_id={"tensor": other},
            device_id_type=MESH_ID,
        )

    def q_across(k):
        return remote(q_send.at[k], q_got.at[k], k, far)

    def m_across():
        return remote(m_send, m_got, 3, far)

    def s_across():
        return remote(s_send, s_got, 4, far)

    def part_beside():
        return remote(psend, pgot, 5, sib)

    def ring_copy(src, kind, d, s):
        return pltpu.make_async_remote_copy(
            src_ref=src,
            dst_ref=rbuf.at[s, kind, d],
            send_sem=ring_send.at[kind, d],
            recv_sem=ring_recv.at[kind, d, s],
            device_id={"dp": sides[d]},
            device_id_type=MESH_ID,
        )

    def part(d, s):
        return ring_index(pos - 1 - s if d == 0 else pos + 1 + s, n)

    def tick(kind, s):
        for d in range(2):
            ring_copy(rbuf.at[s, kind, d], kind, d, s).wait()
            mixed = rbuf[s, kind, d].astype(F32) + ffg[kind, part(d, s + 1), d].astype(F32)
            rbuf[s, kind, d] = mixed.astype(BF)

            @pl.when(s < n - 2)
            def _():
                ring_copy(rbuf.at[s, kind, d], kind, d, s + 1).start()

    outs_hbm = (ro_ref, eo_ref)

    def put(k):
        if isinstance(k, int) and k == 4:
            return pltpu.make_async_copy(in_ref, in_out, out.at[4])
        return pltpu.make_async_copy(qg_ref.at[k], qg_out.at[k], out.at[k])

    def gather(kind, d, s):
        chunk = ring_index(pos - s if d == 0 else pos + s, n)
        ref = outs_hbm[kind].at[chunk, d]
        return pltpu.make_async_remote_copy(
            src_ref=ref,
            dst_ref=ref,
            send_sem=gather_send.at[kind, d],
            recv_sem=gather_recv.at[kind, d, s],
            device_id={"dp": sides[d]},
            device_id_type=MESH_ID,
        )

    def gather_tick(kind, s):
        for d in range(2):
            gather(kind, d, s).wait()

            @pl.when(s + 1 < AHEAD)
            def _():
                gather(kind, d, s + 1).start()

    def gather_begin():
        owns = [
            pltpu.make_async_copy(rbuf.at[n - 2, kind], outs_hbm[kind].at[mine], local.at[12 + kind])
            for kind in range(2)
        ]
        for item in owns:
            item.start()
        for kind in range(2):
            owns[kind].wait()
            for d in range(2):
                gather(kind, d, 0).start()

    for kind in range(2):
        for d in range(2):
            ring_copy(carry_hbm.at[kind, d], kind, d, EARLY).start()

    fill_bias(seg_ref, me // 2, bias_ref, blocks)
    masks = half_masks()
    for k in range(6):
        load(k).wait()
    m_send[...] = dot(mg[...], att[:, cols : 2 * cols], TN).astype(BF)
    m_across().start()
    ag[...] = dot(mg[...], wmf[...], NT).astype(BF)

    turns = 2 * pairs * blocks
    reduce_turns = 2 * (n - 1 - EARLY)
    inside = reduce_turns < turns
    hops = [(h % 2, h // 2) for h in range(max(turns - reduce_turns - 1, 0), 2 * AHEAD)]
    if not inside:
        hops = [(h % 2, h // 2) for h in range(2 * AHEAD)]

    def next_hop():
        if hops:
            gather_tick(*hops.pop(0))

    @pl.loop(0, 2 * pairs)
    def _(q):
        first = q < pairs
        group = 1 - q // pairs
        slot = q % pairs
        base = group * cols3 + slot * PAIR

        @pl.when(q == pairs)
        def _():
            ag[...] = dot(mg[...], wm[...], NT).astype(BF)

        def lanes(k):
            return pl.ds(pl.multiple_of(base + k * cols, PAIR), PAIR)

        own = pl.ds(pl.multiple_of(slot * PAIR, PAIR), PAIR)
        kt = qkv[:, lanes(1)].T
        dk_ref[...] = jnp.zeros_like(dk_ref)
        dv_ref[...] = jnp.zeros_like(dv_ref)
        off = 0
        qsum = jnp.zeros((1, PAIR), F32)
        for i in range(blocks):
            keys = (i + 1) * QB
            at = slice(i * QB, (i + 1) * QB)
            qi = qkv[at, lanes(0)] * jnp.asarray(SCALE, BF)
            gi = ag[at, own]
            kk = qkv[:keys, lanes(1)]
            vv = qkv[:keys, lanes(2)]
            q2 = both_heads(qi, masks)
            g2 = both_heads(gi, masks)
            s = dot(kk, q2, NT) + twice(bias_ref[off : off + keys, :])
            e = jnp.exp(s - jnp.max(s, axis=0, keepdims=True))
            prob = e * (1.0 / jnp.sum(e, axis=0, keepdims=True))
            weighted = prob * dot(vv, g2, NT)
            ds = (weighted - prob * jnp.sum(weighted, axis=0, keepdims=True)).astype(BF)
            dv_ref[:keys, :] += dot(prob.astype(BF), g2)
            dk_ref[:keys, :] += dot(ds, q2)
            outs = []
            for h in range(2):
                outs.append(dot(kt[h * HD : (h + 1) * HD, :keys], ds[:, h * QB : (h + 1) * QB]))
            dq = (jnp.concatenate(outs, axis=0).T * SCALE).astype(BF)
            dqkv[at, lanes(0)] = dq
            qsum += jnp.sum(dq.astype(F32), axis=0, keepdims=True)
            off += keys
            turn = blocks * q + i

            @pl.when(turn < reduce_turns)
            def _():
                tick(i % 2, EARLY + turn // 2)

            if inside and i == reduce_turns % blocks:

                @pl.when(turn == reduce_turns)
                def _():
                    gather_begin()

            if inside:
                hop = turn - reduce_turns - 1

                @pl.when(jnp.logical_and(hop >= 0, hop < 2 * AHEAD))
                def _():
                    gather_tick((i + 1) % 2, hop // 2)
        dv = dv_ref[...].astype(BF)
        dqkv[:, lanes(1)] = dk_ref[...].astype(BF)
        dqkv[:, lanes(2)] = dv
        vsum = jnp.sum(dv.astype(F32), axis=0, keepdims=True)
        for (name, sel) in ((s_send, first), (qsum_ref, jnp.logical_not(first))):

            @pl.when(sel)
            def _():
                name[0:1, own] = qsum
                name[1:2, own] = vsum

        @pl.when(q == pairs - 1)
        def _():
            s_across().start()
            load(6).wait()
            load(7).wait()

            @pl.loop(0, 3)
            def _(k):
                to = pl.ds(pl.multiple_of(cols3 + k * cols, cols), cols)
                q_send[k] = dot(rows1[...], dqkv[:, to], TN).astype(BF)
                q_across(k).start()

    @pl.loop(EARLY + blocks * pairs, n - 1)
    def _(s):
        for kind in range(2):
            tick(kind, s)

    if not inside:
        gather_begin()
    for k in (8, 9):
        load(k).wait()
    nb = 256

    def back(start, at):
        sel = pl.ds(pl.multiple_of(start, rows), rows)
        total = dot(dqkv[sel, 0:cols], wq[0, at, :], NT)
        for k in range(1, 6):
            w = wq if k < 3 else wqf
            total += dot(dqkv[sel, k * cols : (k + 1) * cols], w[k % 3, at, :], NT)
        return total

    @pl.loop(0, width // nb)
    def _(k):
        at = pl.ds(pl.multiple_of(k * nb, nb), nb)
        psend[:, at] = back((1 - core) * rows, at).astype(BF)

    part_beside().start()
    next_hop()

    @pl.loop(0, width // nb)
    def _(k):
        at = pl.ds(pl.multiple_of(k * nb, nb), nb)
        n1g[:, at] = back(core * rows, at)

    next_hop()
    part_beside().wait()
    load(10).wait()
    load(11).wait()
    nsum_ref[...] = jnp.zeros_like(nsum_ref)
    step = 64

    @pl.loop(0, rows // step)
    def _(r):
        at = pl.ds(pl.multiple_of(r * step, step), step)
        grad = n1g[at, :] + pgot[at, :].astype(F32)
        normed, scale = norm_stats(x[at, :].astype(F32))
        g = grad * g1_ref[...]
        mean_g = jnp.mean(g, axis=-1, keepdims=True)
        mean_gn = jnp.mean(g * normed, axis=-1, keepdims=True)
        in_ref[at, :] = rgrad[at, :] + scale * (g - mean_g - normed * mean_gn)
        nsum_ref[0:1, :] += jnp.sum(grad * normed, axis=0, keepdims=True)
        nsum_ref[1:2, :] += jnp.sum(grad, axis=0, keepdims=True)

    put(4).start()
    next_hop()
    mixed = dot(mg[...], att[:, 0:cols], TN)
    m_across().wait()
    qg_ref[3] = (mixed + m_got[...].astype(F32)).astype(BF)
    put(3).start()
    s_across().wait()
    qsum_ref[...] += s_got[...]
    next_hop()

    @pl.loop(0, 3)
    def _(k):
        to = pl.ds(pl.multiple_of(k * cols, cols), cols)
        qg = dot(rows1[...], dqkv[:, to], TN)
        q_across(k).wait()
        qg_ref[k] = (qg + q_got[k].astype(F32)).astype(BF)
        put(k).start()

    while hops:
        next_hop()
    for k in range(5):
        put(k).wait()


def backward(mg, qkv, att, rows1, wq, wqf, wm, wmf, x, rgrad, rg, eg, carry, segments, g1, n):
    rows, width = x.shape
    seq = mg.shape[0]
    cols = wq.shape[2]
    blocks = seq // QB
    vmem = pl.BlockSpec(memory_space=pltpu.VMEM)
    anyspace = pl.BlockSpec(memory_space=pl.ANY)
    split = rg.shape
    chunk = split[2:]
    return pl.pallas_call(
        functools.partial(bwd_kernel, n),
        in_specs=[anyspace] * 13 + [vmem] * 2,
        out_specs=[anyspace] * 2 + [vmem] * 2 + [anyspace] * 2,
        out_shape=[
            jax.ShapeDtypeStruct((rows, width), F32),
            jax.ShapeDtypeStruct((4, width, cols), BF),
            jax.ShapeDtypeStruct((2, cols), F32),
            jax.ShapeDtypeStruct((2, width), F32),
            jax.ShapeDtypeStruct(split, BF),
            jax.ShapeDtypeStruct(split, BF),
        ],
        scratch_shapes=[
            pltpu.VMEM((rows, width), F32),
            pltpu.VMEM((4, width, cols), BF),
            pltpu.VMEM(mg.shape, BF),
            pltpu.VMEM(qkv.shape, BF),
            pltpu.VMEM(att.shape, BF),
            pltpu.VMEM(rows1.shape, BF),
            pltpu.VMEM(wq.shape, BF),
            pltpu.VMEM(wq.shape, BF),
            pltpu.VMEM(wm.shape, BF),
            pltpu.VMEM(wm.shape, BF),
            pltpu.VMEM(x.shape, BF),
            pltpu.VMEM(rgrad.shape, F32),
            pltpu.VMEM((2,) + split, BF),
            pltpu.VMEM((n - 1, 2, 2) + chunk, BF),
            pltpu.VMEM(qkv.shape, BF),
            pltpu.VMEM((seq, cols), BF),
            pltpu.VMEM((QB * blocks * (blocks + 1) // 2, QB), F32),
            pltpu.VMEM((seq, PAIR), F32),
            pltpu.VMEM((seq, PAIR), F32),
            pltpu.VMEM((3, width, cols), BF),
            pltpu.VMEM((3, width, cols), BF),
            pltpu.VMEM((width, cols), BF),
            pltpu.VMEM((width, cols), BF),
            pltpu.VMEM((2, cols), F32),
            pltpu.VMEM((2, cols), F32),
            pltpu.VMEM((rows, width), BF),
            pltpu.VMEM((rows, width), BF),
            pltpu.VMEM((rows, width), F32),
            pltpu.SemaphoreType.DMA((6,)),
            pltpu.SemaphoreType.DMA((6,)),
            pltpu.SemaphoreType.DMA((2, 2)),
            pltpu.SemaphoreType.DMA((2, 2, n - 1)),
            pltpu.SemaphoreType.DMA((2, 2)),
            pltpu.SemaphoreType.DMA((2, 2, n - 1)),
            pltpu.SemaphoreType.DMA((14,)),
            pltpu.SemaphoreType.DMA((5,)),
        ],
        compiler_params=pltpu.CompilerParams(
            collective_id=4, has_side_effects=True, vmem_limit_bytes=60 << 20
        ),
        name="backward",
    )(mg, qkv, att, rows1, wq, wqf, wm, wmf, x, rgrad, rg, eg, carry, segments, g1)


GA = 0.7978845608028654
GB = 0.044715


def ff_kernel(
    n,
    n2_ref, og_hbm, we_hbm, wr_hbm, resid_hbm, be_ref, gain_ref,
    rgrad_out, mg_out, rg_out, eg_out, brn_out, brf_out, usum_ref, dsum_ref, carry_ref,
    rgrad_ref, mg_ref, rg_ref, eg_ref, brn_ref, brf_ref,
    og_ref, we_ref, wr_ref, resid_ref, n2b, act, pg, ng, br, ng_d, br_d, ng_s, br_s, ng_far, ng_out,
    rbuf, send, recv, ring_send, ring_recv, local, out,
):
    rows, width = n2_ref.shape
    units = we_ref.shape[1]
    part = rows // 2
    nb = 256
    me = lax.axis_index("tensor")
    core = me % 2
    sib = me + 1 - 2 * core
    far = (me + 2) % 4

    mine, pos, sides = ring_place(n)
    meet((sib, far), sides)
    h = rg_ref.shape[2]

    def remote(src, dst, k, other):
        return pltpu.make_async_remote_copy(
            src_ref=src,
            dst_ref=dst,
            send_sem=send.at[k],
            recv_sem=recv.at[k],
            device_id={"tensor": other},
            device_id_type=MESH_ID,
        )

    def y_at(c):
        return pl.ds((2 + c) * rows, part)

    def d_at(c):
        return pl.ds((2 + c) * rows + part, part)

    def rows_across(c):
        return remote(n2_ref.at[pl.ds(c * part, part)], n2b.at[y_at(c)], c, far)

    def rows_beside():
        return remote(n2_ref, n2b.at[pl.ds(rows, rows)], 2, sib)

    def rows_forward(c):
        return remote(n2b.at[y_at(c)], n2b.at[d_at(c)], 3 + c, sib)

    def ng_beside():
        return remote(ng.at[pl.ds(rows, rows)], ng_s, 5, sib)

    def br_beside():
        return remote(br.at[pl.ds(rows, rows)], br_s, 6, sib)

    def ng_combine(c):
        return remote(ng.at[d_at(c)], ng_d.at[c], 7 + c, sib)

    def br_combine(c):
        return remote(br.at[d_at(c)], br_d.at[c], 9 + c, sib)

    def ng_across(c):
        return remote(ng_out.at[c], ng_far.at[c], 11 + c, far)

    def own_half(c):
        return pl.ds(pl.multiple_of(core * rows + c * part, part), part)

    def mg_beside(c):
        return remote(mg_ref.at[pl.ds(c * part, part)], mg_out.at[own_half(c)], 13 + c, sib)

    def put(k):
        low, high = pl.ds(0, part), pl.ds(part, part)
        src, dst = (
            (rg_ref, rg_out),
            (eg_ref, eg_out),
            (brn_ref, brn_out),
            (brf_ref, brf_out),
            (rgrad_ref.at[low], rgrad_out.at[low]),
            (rgrad_ref.at[high], rgrad_out.at[high]),
            (mg_ref.at[low], mg_out.at[own_half(0)]),
            (mg_ref.at[high], mg_out.at[own_half(1)]),
        )[k]
        return pltpu.make_async_copy(src, dst, out.at[k])

    for c in range(2):
        rows_across(c).start()
    rows_beside().start()
    first = pl.ds(0, rows)
    rest = pl.ds(rows, 3 * rows)
    loads = [
        pltpu.make_async_copy(n2_ref, n2b.at[first], local.at[0]),
        pltpu.make_async_copy(we_hbm, we_ref, local.at[1]),
        pltpu.make_async_copy(og_hbm.at[first], og_ref.at[first], local.at[2]),
        pltpu.make_async_copy(wr_hbm, wr_ref, local.at[3]),
        pltpu.make_async_copy(og_hbm.at[rest], og_ref.at[rest], local.at[4]),
        pltpu.make_async_copy(resid_hbm, resid_ref, local.at[5]),
    ]
    for load in loads:
        load.start()
    usum_ref[...] = jnp.zeros_like(usum_ref)
    for load in loads[:4]:
        load.wait()

    @pl.loop(0, 4)
    def _(b):
        at = pl.ds(pl.multiple_of(b * rows, rows), rows)
        c = b - 2

        @pl.when(b == 1)
        def _():
            rows_beside().wait()
            loads[4].wait()

        @pl.when(b >= 2)
        def _():
            rows_across(c).wait()
            rows_forward(c).start()
            rows_forward(c).wait()

        for k in range(units // nb):
            cols = slice(k * nb, (k + 1) * nb)
            u = dot(n2b[at, :], we_ref[:, cols]) + be_ref[:, cols]
            act_grad = dot(og_ref[at, :], wr_ref[cols, :], NT)
            sq = u * u
            th = jnp.tanh(u * (GA + (GA * GB) * sq))
            cdf = 0.5 * (1.0 + th)
            slope = cdf + (0.5 * u) * (1.0 - th * th) * (GA + (3.0 * GA * GB) * sq)
            pre = (act_grad * slope).astype(BF)
            act[at, cols] = (u * cdf).astype(BF)
            pg[at, cols] = pre
            usum_ref[:, cols] += jnp.sum(pre.astype(F32), axis=0, keepdims=True)
        @pl.loop(0, width // nb)
        def _(k):
            cols = pl.ds(pl.multiple_of(k * nb, nb), nb)
            ng[at, cols] = dot(pg[at, :], we_ref[cols, :], NT).astype(BF)

        @pl.when(b == 1)
        def _():
            ng_beside().start()

        @pl.when(b >= 2)
        def _():
            ng_combine(c).start()

        @pl.loop(0, width // nb)
        def _(k):
            cols = pl.ds(pl.multiple_of(k * nb, nb), nb)
            br[at, cols] = dot(act[at, :], wr_ref[:, cols]).astype(BF)

        @pl.when(b == 1)
        def _():
            br_beside().start()

        @pl.when(b >= 2)
        def _():
            br_combine(c).start()
            ng_combine(c).wait()
            ng_out[c] = (ng[y_at(c), :].astype(F32) + ng_d[c].astype(F32)).astype(BF)
            ng_across(c).start()

    def part_of(d, s):
        return ring_index(pos - 1 - s if d == 0 else pos + 1 + s, n)

    def ring_copy(src, kind, d, s):
        return pltpu.make_async_remote_copy(
            src_ref=src,
            dst_ref=rbuf.at[s, kind, d],
            send_sem=ring_send.at[kind, d],
            recv_sem=ring_recv.at[kind, d, s],
            device_id={"dp": sides[d]},
            device_id_type=MESH_ID,
        )

    ffg = (rg_ref, eg_ref)

    def ring_start(kind):
        for d in range(2):
            ring_copy(ffg[kind].at[part_of(d, 0), d], kind, d, 0).start()

    def tick(kind, s):
        for d in range(2):
            ring_copy(rbuf.at[s, kind, d], kind, d, s).wait()
            total = rbuf[s, kind, d].astype(F32) + ffg[kind][part_of(d, s + 1), d].astype(F32)
            rbuf[s, kind, d] = total.astype(BF)
            if s + 1 < EARLY:
                ring_copy(rbuf.at[s, kind, d], kind, d, s + 1).start()

    @pl.loop(0, width // nb)
    def _(k):
        cols = pl.ds(pl.multiple_of(k * nb, nb), nb)
        grad = dot(act[...], og_ref[:, cols], TN).astype(BF)
        rg_ref[:, :, :, cols] = grad.reshape(n, 2, h, nb)

    ring_start(0)
    put(0).start()

    @pl.loop(0, width // nb)
    def _(k):
        cols = pl.ds(pl.multiple_of(k * nb, nb), nb)
        grad = dot(n2b[...], pg[:, cols], TN).astype(BF)
        eg_ref[:, :, :, cols] = grad.reshape(n, 2, h, nb)

    ring_start(1)
    put(1).start()
    br_beside().wait()
    brn_ref[...] = (br[0:rows, :].astype(F32) + br_s[...].astype(F32)).astype(BF)
    for c in range(2):
        br_combine(c).wait()
        brf_ref[c * part : (c + 1) * part, :] = (
            br[y_at(c), :].astype(F32) + br_d[c].astype(F32)
        ).astype(BF)
    put(2).start()
    put(3).start()
    ng_beside().wait()
    loads[5].wait()
    dsum_ref[...] = jnp.zeros_like(dsum_ref)
    step = 64
    for c in range(2):
        ng_across(c).wait()

        @pl.loop(0, part // step)
        def _(r):
            inner = pl.ds(pl.multiple_of(r * step, step), step)
            at = pl.ds(pl.multiple_of(c * part + r * step, step), step)
            grad = ng[at, :].astype(F32) + ng_s[at, :].astype(F32) + ng_far[c, inner, :].astype(F32)
            normed, scale = norm_stats(resid_ref[at, :])
            g = grad * gain_ref[...]
            gn = g * normed
            mean_g = jnp.mean(g, axis=-1, keepdims=True)
            mean_gn = jnp.mean(gn, axis=-1, keepdims=True)
            og = og_ref[at, :].astype(F32)
            rgrad = og + scale * (g - mean_g - normed * mean_gn)
            rgrad_ref[at, :] = rgrad
            mg = rgrad.astype(BF)
            mg_ref[at, :] = mg
            dsum_ref[0:1, :] += jnp.sum(mg.astype(F32), axis=0, keepdims=True)
            dsum_ref[1:2, :] += jnp.sum(grad * normed, axis=0, keepdims=True)
            dsum_ref[2:3, :] += jnp.sum(grad, axis=0, keepdims=True)
            dsum_ref[3:4, :] += jnp.sum(og, axis=0, keepdims=True)

        mg_beside(c).start()
        put(4 + c).start()
        put(6 + c).start()
        if c == 0:
            for s in range(EARLY):
                tick(0, s)
    for s in range(EARLY):
        tick(1, s)
    carry_ref[...] = rbuf[EARLY - 1]
    for c in range(2):
        mg_beside(c).wait()
    for k in range(8):
        put(k).wait()


def ff(n2, og_all, we, wr, be, resid, gain, n):
    rows, width = n2.shape
    units = we.shape[1]
    part = rows // 2
    vmem = pl.BlockSpec(memory_space=pltpu.VMEM)
    anyspace = pl.BlockSpec(memory_space=pl.ANY)
    return pl.pallas_call(
        functools.partial(ff_kernel, n),
        in_specs=[anyspace] * 5 + [vmem] * 2,
        out_specs=[anyspace] * 6 + [vmem] * 3,
        out_shape=[
            jax.ShapeDtypeStruct((rows, width), F32),
            jax.ShapeDtypeStruct((2 * rows, width), BF),
            jax.ShapeDtypeStruct((n, 2, units // (2 * n), width), BF),
            jax.ShapeDtypeStruct((n, 2, width // (2 * n), units), BF),
            jax.ShapeDtypeStruct((rows, width), BF),
            jax.ShapeDtypeStruct((rows, width), BF),
            jax.ShapeDtypeStruct((1, units), F32),
            jax.ShapeDtypeStruct((4, width), F32),
            jax.ShapeDtypeStruct((2, 2, units // (2 * n), width), BF),
        ],
        scratch_shapes=[
            pltpu.VMEM((rows, width), F32),
            pltpu.VMEM((rows, width), BF),
            pltpu.VMEM((n, 2, units // (2 * n), width), BF),
            pltpu.VMEM((n, 2, width // (2 * n), units), BF),
            pltpu.VMEM((rows, width), BF),
            pltpu.VMEM((rows, width), BF),
            pltpu.VMEM((4 * rows, width), BF),
            pltpu.VMEM(we.shape, BF),
            pltpu.VMEM(wr.shape, BF),
            pltpu.VMEM((rows, width), F32),
            pltpu.VMEM((4 * rows, width), BF),
            pltpu.VMEM((4 * rows, units), BF),
            pltpu.VMEM((4 * rows, units), BF),
            pltpu.VMEM((4 * rows, width), BF),
            pltpu.VMEM((4 * rows, width), BF),
            pltpu.VMEM((2, part, width), BF),
            pltpu.VMEM((2, part, width), BF),
            pltpu.VMEM((rows, width), BF),
            pltpu.VMEM((rows, width), BF),
            pltpu.VMEM((2, part, width), BF),
            pltpu.VMEM((2, part, width), BF),
            pltpu.VMEM((EARLY, 2, 2, units // (2 * n), width), BF),
            pltpu.SemaphoreType.DMA((15,)),
            pltpu.SemaphoreType.DMA((15,)),
            pltpu.SemaphoreType.DMA((2, 2)),
            pltpu.SemaphoreType.DMA((2, 2, EARLY)),
            pltpu.SemaphoreType.DMA((6,)),
            pltpu.SemaphoreType.DMA((8,)),
        ],
        compiler_params=pltpu.CompilerParams(
            collective_id=2, has_side_effects=True, vmem_limit_bytes=60 << 20
        ),
        name="ff",
    )(n2, og_all, we, wr, resid, be, gain)


def ring_kernel(
    n, g_ref, small_ref, rbias_ref, resid_hbm, brn_hbm, brf_hbm, _r, _e,
    qo_ref, mo_ref, ro_ref, eo_ref, so_ref, bo_ref,
    buf, sbuf, sall, speer, ssum, resid, brn, bro,
    send, recv, fsend, frecv, ssend, srecv, tsend, trecv, local,
):
    mine, pos, sides = ring_place(n)
    me = lax.axis_index("tensor")
    far = (me + 2) % 4
    peers = [(me + k) % 4 for k in range(1, 4)]
    loads = (
        pltpu.make_async_copy(resid_hbm, resid, local.at[0]),
        pltpu.make_async_copy(brn_hbm, brn, local.at[1]),
    )
    for load in loads:
        load.start()
    meet(peers, sides)

    def remote(src, dst, kind, d, s):
        return pltpu.make_async_remote_copy(
            src_ref=src,
            dst_ref=dst,
            send_sem=send.at[kind, d],
            recv_sem=recv.at[kind, d, s],
            device_id={"dp": sides[d]},
            device_id_type=MESH_ID,
        )

    def little(src, dst, kind, s):
        return pltpu.make_async_remote_copy(
            src_ref=src,
            dst_ref=dst,
            send_sem=ssend.at[kind],
            recv_sem=srecv.at[kind, s],
            device_id={"dp": sides[0]},
            device_id_type=MESH_ID,
        )

    def beside(src, dst, k, other):
        return pltpu.make_async_remote_copy(
            src_ref=src,
            dst_ref=dst,
            send_sem=tsend.at[k],
            recv_sem=trecv.at[k],
            device_id={"tensor": other},
            device_id_type=MESH_ID,
        )

    def share(k):
        return beside(small_ref, speer.at[k], k, peers[k])

    def branch():
        return beside(brf_hbm, bro, 3, far)

    def part(d, s):
        return ring_index(pos - 1 - s if d == 0 else pos + 1 + s, n)

    def held(d, s):
        return ring_index(pos - s if d == 0 else pos + s, n)

    streams = [(k, d) for k in range(4) for d in range(2)]

    def source(k, chunk, d):
        return g_ref.at[k, chunk, d]

    def slot(k, s, d):
        return buf.at[s, d, k]

    def put_at(k, chunk, d):
        return qo_ref.at[k, chunk, d] if k < 3 else mo_ref.at[chunk, d]

    def add(k, d, s):
        ref = slot(k, s, d)
        total = ref[...].astype(F32) + source(k, part(d, s + 1), d)[...].astype(F32)
        ref[...] = total.astype(BF)

    def gather(k, d, s):
        ref = put_at(k, held(d, s), d)
        return remote(ref, ref, 4 + k, d, s)

    left = n - 1 - AHEAD
    half = ro_ref.shape[3] // 2

    def ff_hop(kind, c, d, s):
        ref = (ro_ref, eo_ref)[kind].at[held(d, s), d, :, pl.ds(c * half, half)]
        k = 2 * kind + c
        return pltpu.make_async_remote_copy(
            src_ref=ref,
            dst_ref=ref,
            send_sem=fsend.at[k, d],
            recv_sem=frecv.at[k, d, s - AHEAD],
            device_id={"dp": sides[d]},
            device_id_type=MESH_ID,
        )

    def beside_step(kind, s, act):
        @pl.when(s < left)
        def _():
            for d in range(2):
                act(ff_hop(kind, 0, d, AHEAD + s))

        @pl.when(s >= n - 1 - left)
        def _():
            for d in range(2):
                act(ff_hop(kind, 1, d, AHEAD + s - (n - 1 - left)))

    def start(copy):
        copy.start()

    def finish(copy):
        copy.wait()

    def gather_small(s):
        ref = sall.at[held(0, s)]
        return little(ref, ref, 1, s)

    for k, d in streams:
        remote(source(k, part(d, 0), d), slot(k, 0, d), k, d, 0).start()
    for k in range(3):
        share(k).start()
    branch().start()
    for k in range(3):
        share(k).wait()
    ssum[...] = small_ref[...]
    shared = n * 6 // 8
    ssum[0:shared] = ssum[0:shared] + speer[0, 0:shared] + speer[1, 0:shared] + speer[2, 0:shared]
    little(ssum.at[part(0, 0)], sbuf.at[0], 0, 0).start()

    @pl.loop(0, n - 2)
    def _(s):
        beside_step(0, s, start)
        for k, d in streams:
            remote(slot(k, s, d), slot(k, s, d), k, d, s).wait()
            add(k, d, s)
            remote(slot(k, s, d), slot(k, s + 1, d), k, d, s + 1).start()
        little(sbuf.at[s], sbuf.at[s], 0, s).wait()
        sbuf[s] = sbuf[s] + ssum[part(0, s + 1)]
        little(sbuf.at[s], sbuf.at[s + 1], 0, s + 1).start()
        beside_step(0, s, finish)

    last = n - 2
    beside_step(0, last, start)
    puts = []
    for k, d in streams:
        remote(slot(k, last, d), slot(k, last, d), k, d, last).wait()
        add(k, d, last)
        put = pltpu.make_async_copy(slot(k, last, d), put_at(k, mine, d), local.at[2 + 2 * k + d])
        put.start()
        puts.append(put)
    for (k, d), put in zip(streams, puts):
        put.wait()
        gather(k, d, 0).start()
    little(sbuf.at[last], sbuf.at[last], 0, last).wait()
    sall[mine] = sbuf[last] + ssum[mine]
    gather_small(0).start()
    beside_step(0, last, finish)

    @pl.loop(0, n - 2)
    def _(s):
        beside_step(1, s, start)
        for k, d in streams:
            gather(k, d, s).wait()
            gather(k, d, s + 1).start()
        gather_small(s).wait()
        gather_small(s + 1).start()
        beside_step(1, s, finish)

    beside_step(1, last, start)

    branch().wait()
    for load in loads:
        load.wait()
    step = 64

    @pl.loop(0, bo_ref.shape[0] // step)
    def _(r):
        at = pl.ds(pl.multiple_of(r * step, step), step)
        total = resid[at, :] + brn[at, :].astype(F32) + bro[at, :].astype(F32) + rbias_ref[...]
        bo_ref[at, :] = total.astype(BF)

    for k, d in streams:
        gather(k, d, last).wait()
    gather_small(last).wait()
    so_ref[...] = sall[...]
    beside_step(1, last, finish)


def ring_sum(g, small, resid, brn, brf, r, e, rbias, n):
    split = (4, n, 2, g.shape[1] // (2 * n), g.shape[2])
    s3 = small.reshape(n, 1, small.size // n)
    vmem = pl.BlockSpec(memory_space=pltpu.VMEM)
    anyspace = pl.BlockSpec(memory_space=pl.ANY)
    qo, mo, ro, eo, so, bo = pl.pallas_call(
        functools.partial(ring_kernel, n),
        in_specs=[vmem] * 3 + [anyspace] * 5,
        out_specs=[anyspace] * 4 + [vmem] * 2,
        input_output_aliases={6: 2, 7: 3},
        out_shape=[
            jax.ShapeDtypeStruct((3,) + split[1:], BF),
            jax.ShapeDtypeStruct(split[1:], BF),
            jax.ShapeDtypeStruct(r.shape, BF),
            jax.ShapeDtypeStruct(e.shape, BF),
            jax.ShapeDtypeStruct(s3.shape, F32),
            jax.ShapeDtypeStruct(brf.shape, BF),
        ],
        scratch_shapes=[
            pltpu.VMEM((n - 1, 2, 4) + split[3:], BF),
            pltpu.VMEM((n - 1,) + s3.shape[1:], F32),
            pltpu.VMEM(s3.shape, F32),
            pltpu.VMEM((3,) + s3.shape, F32),
            pltpu.VMEM(s3.shape, F32),
            pltpu.VMEM(resid.shape, F32),
            pltpu.VMEM(brn.shape, BF),
            pltpu.VMEM(brf.shape, BF),
            pltpu.SemaphoreType.DMA((8, 2)),
            pltpu.SemaphoreType.DMA((8, 2, n - 1)),
            pltpu.SemaphoreType.DMA((4, 2)),
            pltpu.SemaphoreType.DMA((4, 2, n - 1 - AHEAD)),
            pltpu.SemaphoreType.DMA((2,)),
            pltpu.SemaphoreType.DMA((2, n - 1)),
            pltpu.SemaphoreType.DMA((4,)),
            pltpu.SemaphoreType.DMA((4,)),
            pltpu.SemaphoreType.DMA((10,)),
        ],
        compiler_params=pltpu.CompilerParams(
            collective_id=1, has_side_effects=True, vmem_limit_bytes=60 << 20
        ),
        name="ring_sum",
    )(g.reshape(split), s3, rbias, resid, brn, brf, r, e)
    wide = (-1, r.shape[-1])
    return (
        qo.reshape((3,) + g.shape[1:]),
        mo.reshape(g.shape[1:]),
        ro.reshape(wide),
        eo.reshape(wide),
        so.reshape(small.shape),
        bo,
    )


def body(
    block_in,
    segments,
    first_gain,
    first_shift,
    w_qkv,
    qv_bias,
    w_mix,
    mix_bias,
    second_gain,
    second_shift,
    w_expand,
    expand_bias,
    w_reduce,
    reduce_bias,
    out_grad,
):
    width = block_in.shape[1]
    cols = w_qkv.shape[2]
    units = w_expand.shape[1]
    dp_size = lax.axis_size("dp")
    flat = (1, width)
    wq = w_qkv.transpose(1, 0, 2)
    rows1, qkv, att, resid, n2, wq_far, wm_far, og_all = forward(
        block_in,
        segments,
        first_gain.reshape(flat),
        first_shift.reshape(flat),
        qv_bias,
        mix_bias.reshape(flat),
        second_gain.reshape(flat),
        second_shift.reshape(flat),
        wq,
        w_mix,
        out_grad,
        dp_size,
    )
    resid_grad, mg_all, reduce_grad, expand_grad, br_near, br_far, unit_sums, sums2, carry = ff(
        n2, og_all, w_expand, w_reduce, expand_bias.reshape(1, units), resid, second_gain.reshape(flat), dp_size
    )
    in_grad, grads, qv_sums, norm_sums, reduce_all, expand_all = backward(
        mg_all,
        qkv,
        att,
        rows1,
        wq,
        wq_far,
        w_mix,
        wm_far,
        block_in,
        resid_grad,
        reduce_grad,
        expand_grad,
        carry,
        segments,
        first_gain.reshape(flat),
        dp_size,
    )
    small = jnp.concatenate(
        [
            norm_sums,
            sums2,
            unit_sums,
            jnp.pad(qv_sums.reshape(1, 2 * cols), ((0, 0), (0, width - 2 * cols))),
        ],
        axis=0,
    )
    qkv_grad, mix_grad, reduce_all, expand_all, small, block_out = ring_sum(
        grads,
        small,
        resid,
        br_near,
        br_far,
        reduce_all,
        expand_all,
        reduce_bias.reshape(flat),
        dp_size,
    )
    return (
        block_out,
        in_grad,
        small[0],
        small[1],
        qkv_grad.astype(F32).transpose(1, 0, 2),
        small[7, : 2 * cols].reshape(2, cols),
        mix_grad.astype(F32).T,
        small[2],
        small[3],
        small[4],
        expand_all.astype(F32),
        small[6],
        reduce_all.astype(F32),
        small[5],
    )


def solution(mesh):
    both = P(("dp", "tensor"), None)
    return jax.shard_map(
        body,
        mesh=mesh,
        in_specs=(
            both,
            P("dp", None),
            P(),
            P(),
            P(None, None, "tensor"),
            P(None, "tensor"),
            P("tensor", None),
            P(),
            P(),
            P(),
            P(None, "tensor"),
            P("tensor"),
            P("tensor", None),
            P(),
            both,
        ),
        out_specs=(
            both,
            both,
            P(),
            P(),
            P(None, None, "tensor"),
            P(None, "tensor"),
            P("tensor", None),
            P(),
            P(),
            P(),
            P(None, "tensor"),
            P("tensor"),
            P("tensor", None),
            P(),
        ),
        check_vma=False,
    )
```

```python
import functools

import jax
import jax.numpy as jnp
from jax import lax
from jax.experimental import pallas as pl
from jax.experimental.pallas import tpu as pltpu
from jax.sharding import PartitionSpec as P

HD = 64
PAIR = 2 * HD
QB = 256
EPS = 1e-5
BF = jnp.bfloat16
F32 = jnp.float32
SCALE = HD ** (-0.5)
MESH_ID = pl.DeviceIdType.MESH
AHEAD = 4
NT = (((1,), (1,)), ((), ()))
TN = (((0,), (0,)), ((), ()))


def dot(a, b, dims=(((1,), (0,)), ((), ()))):
    return lax.dot_general(a, b, dims, preferred_element_type=F32)


def norm_stats(values):
    mean = jnp.mean(values, axis=-1, keepdims=True)
    centered = values - mean
    variance = jnp.mean(centered * centered, axis=-1, keepdims=True)
    scale = lax.rsqrt(variance + EPS)
    return centered * scale, scale


def fill_bias(seg_ref, row, bias_ref, blocks):
    segr = seg_ref[pl.ds(row, 1), :].astype(F32)
    segc = jnp.broadcast_to(segr, (8, segr.shape[1])).T[:, 0:1]
    off = 0
    for i in range(blocks):
        keys = (i + 1) * QB
        kpos = lax.broadcasted_iota(jnp.int32, (keys, QB), 0)
        qpos = lax.broadcasted_iota(jnp.int32, (keys, QB), 1) + i * QB
        same = segc[:keys, :] == segr[:, i * QB : (i + 1) * QB]
        allowed = jnp.logical_and(kpos <= qpos, same)
        bias_ref[off : off + keys, :] = jnp.where(allowed, 0.0, -1e30)
        off += keys


def half_masks():
    lane = lax.broadcasted_iota(jnp.int32, (1, PAIR), 1)
    return (lane < HD, lane >= HD)


def ring_index(at, n):
    at = (at + 2 * n) % n
    far = at // (n // 2)
    return (1 - far) * 2 * at + far * (2 * (n - 1 - at) + 1)


def ring_place(n):
    mine = lax.axis_index("dp")
    odd = mine % 2
    pos = (1 - odd) * (mine // 2) + odd * (n - 1 - mine // 2)
    return mine, pos, (ring_index(pos + 1, n), ring_index(pos - 1, n))


def meet(tensor_peers, dp_peers):
    barrier = pltpu.get_barrier_semaphore()
    for other in tensor_peers:
        pl.semaphore_signal(barrier, inc=1, device_id={"tensor": other}, device_id_type=MESH_ID)
    for other in dp_peers:
        pl.semaphore_signal(barrier, inc=1, device_id={"dp": other}, device_id_type=MESH_ID)
    pl.semaphore_wait(barrier, len(tensor_peers) + len(dp_peers))


def both_heads(a, masks):
    zero = jnp.zeros_like(a)
    return jnp.concatenate([jnp.where(masks[0], a, zero), jnp.where(masks[1], a, zero)], axis=0)


def twice(a):
    return jnp.concatenate([a, a], axis=1)


def fwd_kernel(
    n,
    x_ref, seg_ref, g1_ref, s1_ref, bq_ref, mixb_ref, g2_ref, s2_ref, wq_hbm, wm_hbm, og_ref,
    rows1_out, qkv_out, att_out, resid_out, n2_out, wqf_out, wmf_out, oga_ref,
    rows1_ref, qkv_ref, att_ref, resid_ref, n2_ref, w_all, wm_all,
    b_all, bqf, bias_ref, psend, pgot, send, recv, ring_send, ring_recv, local, out,
):
    rows, width = x_ref.shape
    seq = rows1_ref.shape[0]
    cols = w_all.shape[3]
    wqf_ref = w_all.at[1]
    wmf_ref = wm_all.at[1]
    cols3 = 3 * cols
    half = rows // 2
    blocks = seq // QB
    me = lax.axis_index("tensor")
    core = me % 2
    sib = me + 1 - 2 * core
    far = (me + 2) % 4
    mine, pos, sides = ring_place(n)
    meet((sib, far), sides)

    def remote(src, dst, k, other):
        return pltpu.make_async_remote_copy(
            src_ref=src,
            dst_ref=dst,
            send_sem=send.at[k],
            recv_sem=recv.at[k],
            device_id={"tensor": other},
            device_id_type=MESH_ID,
        )

    slab = width // n
    wide = cols // 2

    def slab_rows(chunk):
        return pl.ds(pl.multiple_of(chunk * slab, slab), slab)

    mix_slab = wm_hbm.shape[0] // n
    around = mix_slab % 16 == 0
    streams = 4 if around else 3

    def mix_rows(chunk):
        return pl.ds(pl.multiple_of(chunk * mix_slab, mix_slab), mix_slab)

    def piece():
        return remote(wq_hbm.at[:, slab_rows(mine)], wqf_ref.at[:, slab_rows(mine)], 0, far)

    def bias_across():
        return remote(bq_ref, bqf, 1, far)

    def own_half(c):
        return pl.ds(pl.multiple_of(core * rows + c * half, half), half)

    def rows_beside(c):
        return remote(rows1_ref.at[own_half(c)], rows1_ref.at[own_half(c)], 2 + c, sib)

    def mix_across():
        if around:
            return remote(wm_hbm.at[mix_rows(mine)], wmf_ref.at[mix_rows(mine)], 4, far)
        return remote(wm_hbm, wmf_ref, 4, far)

    def og_across(c):
        return remote(
            og_ref.at[pl.ds(c * half, half)], oga_ref.at[pl.ds((2 + c) * rows, half)], 5 + c, far
        )

    def og_beside():
        return remote(og_ref, oga_ref.at[pl.ds(rows, rows)], 7, sib)

    def og_forward(c):
        return remote(
            oga_ref.at[pl.ds((2 + c) * rows, half)],
            oga_ref.at[pl.ds((2 + c) * rows + half, half)],
            8 + c,
            sib,
        )

    def part_beside():
        return remote(psend, pgot, 10, sib)

    def og_own():
        return pltpu.make_async_copy(og_ref, oga_ref.at[pl.ds(0, rows)], local.at[0])

    reach = n // 2

    def hop(k, d, s, part=False):
        chunk = ring_index(pos - s if d == 0 else pos + s, n)
        side = width // 2 if k == 3 else wide
        lanes = slice(d * side, (d + 1) * side) if part else slice(None)
        ref = wmf_ref.at[mix_rows(chunk), lanes] if k == 3 else wqf_ref.at[k, slab_rows(chunk), lanes]
        return pltpu.make_async_remote_copy(
            src_ref=ref,
            dst_ref=ref,
            send_sem=ring_send.at[k, d],
            recv_sem=ring_recv.at[k, d, s],
            device_id={"dp": sides[d]},
            device_id_type=MESH_ID,
        )

    def tick(s):
        for k in range(streams):
            for d in range(2):
                hop(k, d, s).wait()

                @pl.when(s < reach - 2)
                def _():
                    hop(k, d, s + 1).start()

                @pl.when(s == reach - 2)
                def _():
                    hop(k, d, s + 1, True).start()

    def last_tick():
        for k in range(3):
            for d in range(2):
                hop(k, d, reach - 1, True).wait()

    def put(k):
        near = pl.ds(0, cols3)
        far_part = pl.ds(cols3, cols3)
        low, high = pl.ds(0, half), pl.ds(half, half)
        src, dst = (
            (rows1_ref, rows1_out),
            (qkv_ref.at[:, near], qkv_out.at[:, near]),
            (qkv_ref.at[:, far_part], qkv_out.at[:, far_part]),
            (wqf_ref, wqf_out),
            (wmf_ref, wmf_out),
            (att_ref, att_out),
            (resid_ref.at[low], resid_out.at[low]),
            (resid_ref.at[high], resid_out.at[high]),
            (n2_ref.at[low], n2_out.at[low]),
            (n2_ref.at[high], n2_out.at[high]),
        )[k]
        return pltpu.make_async_copy(src, dst, out.at[k])

    piece().start()
    if around:
        mix_across().start()
    bias_across().start()
    loads = (
        pltpu.make_async_copy(wq_hbm, w_all.at[0], local.at[1]),
        pltpu.make_async_copy(wm_hbm, wm_all.at[0], local.at[2]),
    )
    for load in loads:
        load.start()
    step = 64
    for c in range(2):

        @pl.loop(0, half // step)
        def _(r):
            normed = norm_stats(x_ref[pl.ds(pl.multiple_of(c * half + r * step, step), step), :].astype(F32))[0]
            to = pl.ds(pl.multiple_of(core * rows + c * half + r * step, step), step)
            rows1_ref[to, :] = (normed * g1_ref[...] + s1_ref[...]).astype(BF)

        rows_beside(c).start()
    piece().wait()
    for k in range(3):
        for d in range(2):
            hop(k, d, 0).start()
    if around:
        mix_across().wait()
        for d in range(2):
            hop(3, d, 0).start()
    else:
        mix_across().start()
    for c in range(2):
        og_across(c).start()
    og_beside().start()
    og_own().start()
    fill_bias(seg_ref, me // 2, bias_ref, blocks)

    def fill_shift(g, ref):
        b_all[g, 0:1] = ref[0:1]
        b_all[g, 1:2] = jnp.zeros_like(ref[0:1])
        b_all[g, 2:3] = ref[1:2]

    fill_shift(0, bq_ref)
    for c in range(2):
        rows_beside(c).wait()
    for load in loads:
        load.wait()
    put(0).start()
    masks = half_masks()
    pairs = cols // PAIR
    ticks = 1 + pairs

    @pl.loop(0, 2 * pairs)
    def _(p):
        group = p // pairs

        @pl.when(p == pairs)
        def _():
            @pl.loop(ticks, reach - 1)
            def _(s):
                tick(s)

            last_tick()
            bias_across().wait()
            fill_shift(1, bqf)
            put(3).start()

        @pl.when(p % pairs == 0)
        def _():
            @pl.loop(0, 3)
            def _(k):
                to = pl.ds(pl.multiple_of(group * cols3 + k * cols, cols), cols)
                part = dot(rows1_ref[...], w_all[group, k]) + b_all[group, pl.ds(k, 1)]
                qkv_ref[:, to] = part.astype(BF)

        @pl.when(p == 0)
        def _():
            put(1).start()
            tick(0)

        @pl.when(p == pairs)
        def _():
            put(2).start()

        base = group * cols3 + (p % pairs) * PAIR

        def lanes(k):
            return pl.ds(pl.multiple_of(base + k * cols, PAIR), PAIR)

        vt = qkv_ref[:, lanes(2)].T
        off = 0
        for i in range(blocks):
            keys = (i + 1) * QB
            at = slice(i * QB, (i + 1) * QB)
            qi = qkv_ref[at, lanes(0)] * jnp.asarray(SCALE, BF)
            kk = qkv_ref[:keys, lanes(1)]
            s = dot(kk, both_heads(qi, masks), NT) + twice(bias_ref[off : off + keys, :])
            e = jnp.exp(s - jnp.max(s, axis=0, keepdims=True))
            inverse = 1.0 / jnp.sum(e, axis=0, keepdims=True)
            e = e.astype(BF)
            outs = []
            for h in range(2):
                side = slice(h * QB, (h + 1) * QB)
                outs.append(dot(vt[h * HD : (h + 1) * HD, :keys], e[:, side]) * inverse[:, side])
            att_ref[at, pl.ds(pl.multiple_of(p * PAIR, PAIR), PAIR)] = jnp.concatenate(outs, axis=0).T.astype(BF)
            off += keys
            if i == blocks - 1:

                @pl.when(p < pairs)
                def _():
                    tick(1 + p)

    if around:
        for d in range(2):
            hop(3, d, reach - 1, True).wait()
    else:
        mix_across().wait()
    put(4).start()
    put(5).start()
    nb = 256

    def mixed(start, at):
        sel = pl.ds(pl.multiple_of(start, rows), rows)
        total = dot(att_ref[sel, 0:cols], wm_all[0, :, at])
        return total + dot(att_ref[sel, cols : 2 * cols], wm_all[1, :, at])

    @pl.loop(0, width // nb)
    def _(k):
        at = pl.ds(pl.multiple_of(k * nb, nb), nb)
        psend[:, at] = mixed((1 - core) * rows, at).astype(BF)

    part_beside().start()

    @pl.loop(0, width // nb)
    def _(k):
        at = pl.ds(pl.multiple_of(k * nb, nb), nb)
        resid_ref[:, at] = x_ref[:, at].astype(F32) + mixed(core * rows, at) + mixb_ref[:, at]

    for c in range(2):
        og_across(c).wait()
        og_forward(c).start()
    part_beside().wait()

    for c in range(2):

        @pl.loop(0, half // step)
        def _(r):
            at = pl.ds(pl.multiple_of(c * half + r * step, step), step)
            full = resid_ref[at, :] + pgot[at, :].astype(F32)
            resid_ref[at, :] = full
            n2_ref[at, :] = (norm_stats(full)[0] * g2_ref[...] + s2_ref[...]).astype(BF)

        put(6 + c).start()
        put(8 + c).start()

    for k in range(10):
        put(k).wait()
    og_own().wait()
    og_beside().wait()
    for c in range(2):
        og_forward(c).wait()


def forward(x, segments, g1, s1, bq, mixb, g2, s2, wq, wm, og, n):
    rows, width = x.shape
    seq = segments.shape[1]
    cols = wq.shape[2]
    blocks = seq // QB
    vmem = pl.BlockSpec(memory_space=pltpu.VMEM)
    anyspace = pl.BlockSpec(memory_space=pl.ANY)
    return pl.pallas_call(
        functools.partial(fwd_kernel, n),
        in_specs=[vmem] * 8 + [anyspace] * 3,
        out_specs=[anyspace] * 8,
        out_shape=[
            jax.ShapeDtypeStruct((seq, width), BF),
            jax.ShapeDtypeStruct((seq, 6 * cols), BF),
            jax.ShapeDtypeStruct((seq, 2 * cols), BF),
            jax.ShapeDtypeStruct((rows, width), F32),
            jax.ShapeDtypeStruct((rows, width), BF),
            jax.ShapeDtypeStruct(wq.shape, BF),
            jax.ShapeDtypeStruct(wm.shape, BF),
            jax.ShapeDtypeStruct((4 * rows, width), BF),
        ],
        scratch_shapes=[
            pltpu.VMEM((seq, width), BF),
            pltpu.VMEM((seq, 6 * cols), BF),
            pltpu.VMEM((seq, 2 * cols), BF),
            pltpu.VMEM((rows, width), F32),
            pltpu.VMEM((rows, width), BF),
            pltpu.VMEM((2,) + wq.shape, BF),
            pltpu.VMEM((2,) + wm.shape, BF),
            pltpu.VMEM((2, 3, cols), F32),
            pltpu.VMEM((2, cols), F32),
            pltpu.VMEM((QB * blocks * (blocks + 1) // 2, QB), F32),
            pltpu.VMEM((rows, width), BF),
            pltpu.VMEM((rows, width), BF),
            pltpu.SemaphoreType.DMA((11,)),
            pltpu.SemaphoreType.DMA((11,)),
            pltpu.SemaphoreType.DMA((4, 2)),
            pltpu.SemaphoreType.DMA((4, 2, n // 2)),
            pltpu.SemaphoreType.DMA((3,)),
            pltpu.SemaphoreType.DMA((10,)),
        ],
        compiler_params=pltpu.CompilerParams(
            collective_id=3, has_side_effects=True, vmem_limit_bytes=56 << 20
        ),
        name="forward",
    )(x, segments, g1, s1, bq, mixb, g2, s2, wq, wm, og)


def bwd_kernel(
    n,
    mg_hbm, qkv_hbm, att_hbm, rows1_hbm, wq_hbm, wqf_hbm, wm_hbm, wmf_hbm, x_hbm, rgrad_hbm, rg_hbm, eg_hbm, carry_hbm,
    seg_ref, g1_ref,
    in_out, qg_out, qsum_ref, nsum_ref, ro_ref, eo_ref,
    in_ref, qg_ref,
    mg, qkv, att, rows1, wq, wqf, wm, wmf, x, rgrad, ffg,
    rbuf, dqkv, ag, bias_ref, dk_ref, dv_ref, q_send, q_got, m_send, m_got, s_got, s_send, psend, pgot, n1g,
    send, recv, ring_send, ring_recv, gather_send, gather_recv, local, out,
):
    rows, width = in_ref.shape
    seq = mg.shape[0]
    cols = wq.shape[2]
    cols3 = 3 * cols
    pairs = cols // PAIR
    blocks = seq // QB
    me = lax.axis_index("tensor")
    core = me % 2
    sib = me + 1 - 2 * core
    far = (me + 2) % 4
    mine, pos, sides = ring_place(n)

    pairs_in = (
        (mg_hbm, mg), (wmf_hbm, wmf), (att_hbm, att), (qkv_hbm, qkv), (rg_hbm, ffg.at[0]), (eg_hbm, ffg.at[1]),
        (rows1_hbm, rows1), (wm_hbm, wm), (wqf_hbm, wqf), (wq_hbm, wq), (x_hbm, x), (rgrad_hbm, rgrad),
    )

    def load(k):
        return pltpu.make_async_copy(pairs_in[k][0], pairs_in[k][1], local.at[k])

    for k in range(len(pairs_in)):
        load(k).start()
    meet((sib, far), sides)

    def remote(src, dst, k, other):
        return pltpu.make_async_remote_copy(
            src_ref=src,
            dst_ref=dst,
            send_sem=send.at[k],
            recv_sem=recv.at[k],
            device_id={"tensor": other},
            device_id_type=MESH_ID,
        )

    def q_across(k):
        return remote(q_send.at[k], q_got.at[k], k, far)

    def m_across():
        return remote(m_send, m_got, 3, far)

    def s_across():
        return remote(s_send, s_got, 4, far)

    def part_beside():
        return remote(psend, pgot, 5, sib)

    def ring_copy(src, kind, d, s):
        return pltpu.make_async_remote_copy(
            src_ref=src,
            dst_ref=rbuf.at[s, kind, d],
            send_sem=ring_send.at[kind, d],
            recv_sem=ring_recv.at[kind, d, s],
            device_id={"dp": sides[d]},
            device_id_type=MESH_ID,
        )

    def part(d, s):
        return ring_index(pos - 1 - s if d == 0 else pos + 1 + s, n)

    def tick(kind, s):
        for d in range(2):
            ring_copy(rbuf.at[s, kind, d], kind, d, s).wait()
            mixed = rbuf[s, kind, d].astype(F32) + ffg[kind, part(d, s + 1), d].astype(F32)
            rbuf[s, kind, d] = mixed.astype(BF)

            @pl.when(s < n - 2)
            def _():
                ring_copy(rbuf.at[s, kind, d], kind, d, s + 1).start()

    outs_hbm = (ro_ref, eo_ref)

    def put(k):
        if isinstance(k, int) and k == 4:
            return pltpu.make_async_copy(in_ref, in_out, out.at[4])
        return pltpu.make_async_copy(qg_ref.at[k], qg_out.at[k], out.at[k])

    def gather(kind, d, s):
        chunk = ring_index(pos - s if d == 0 else pos + s, n)
        ref = outs_hbm[kind].at[chunk, d]
        return pltpu.make_async_remote_copy(
            src_ref=ref,
            dst_ref=ref,
            send_sem=gather_send.at[kind, d],
            recv_sem=gather_recv.at[kind, d, s],
            device_id={"dp": sides[d]},
            device_id_type=MESH_ID,
        )

    def gather_tick(kind, s):
        for d in range(2):
            gather(kind, d, s).wait()

            @pl.when(s + 1 < AHEAD)
            def _():
                gather(kind, d, s + 1).start()

    def gather_begin():
        owns = [
            pltpu.make_async_copy(rbuf.at[n - 2, kind], outs_hbm[kind].at[mine], local.at[12 + kind])
            for kind in range(2)
        ]
        for item in owns:
            item.start()
        for kind in range(2):
            owns[kind].wait()
            for d in range(2):
                gather(kind, d, 0).start()

    for d in range(2):
        ring_copy(eg_hbm.at[part(d, 0), d], 1, d, 0).start()
    for d in range(2):
        ring_copy(carry_hbm.at[d], 0, d, 1).start()

    fill_bias(seg_ref, me // 2, bias_ref, blocks)
    masks = half_masks()
    for k in range(6):
        load(k).wait()
    m_send[...] = dot(mg[...], att[:, cols : 2 * cols], TN).astype(BF)
    m_across().start()
    ag[...] = dot(mg[...], wmf[...], NT).astype(BF)

    turns = 2 * pairs * blocks
    reduce_turns = 2 * (n - 1) - 1
    inside = reduce_turns < turns
    hops = [(h % 2, h // 2) for h in range(max(turns - reduce_turns - 1, 0), 2 * AHEAD)]
    if not inside:
        hops = [(h % 2, h // 2) for h in range(2 * AHEAD)]

    def next_hop():
        if hops:
            gather_tick(*hops.pop(0))

    @pl.loop(0, 2 * pairs)
    def _(q):
        first = q < pairs
        group = 1 - q // pairs
        slot = q % pairs
        base = group * cols3 + slot * PAIR

        @pl.when(q == pairs)
        def _():
            ag[...] = dot(mg[...], wm[...], NT).astype(BF)

        def lanes(k):
            return pl.ds(pl.multiple_of(base + k * cols, PAIR), PAIR)

        own = pl.ds(pl.multiple_of(slot * PAIR, PAIR), PAIR)
        kt = qkv[:, lanes(1)].T
        dk_ref[...] = jnp.zeros_like(dk_ref)
        dv_ref[...] = jnp.zeros_like(dv_ref)
        off = 0
        qsum = jnp.zeros((1, PAIR), F32)
        for i in range(blocks):
            keys = (i + 1) * QB
            at = slice(i * QB, (i + 1) * QB)
            qi = qkv[at, lanes(0)] * jnp.asarray(SCALE, BF)
            gi = ag[at, own]
            kk = qkv[:keys, lanes(1)]
            vv = qkv[:keys, lanes(2)]
            q2 = both_heads(qi, masks)
            g2 = both_heads(gi, masks)
            s = dot(kk, q2, NT) + twice(bias_ref[off : off + keys, :])
            e = jnp.exp(s - jnp.max(s, axis=0, keepdims=True))
            prob = e * (1.0 / jnp.sum(e, axis=0, keepdims=True))
            weighted = prob * dot(vv, g2, NT)
            ds = (weighted - prob * jnp.sum(weighted, axis=0, keepdims=True)).astype(BF)
            dv_ref[:keys, :] += dot(prob.astype(BF), g2)
            dk_ref[:keys, :] += dot(ds, q2)
            outs = []
            for h in range(2):
                outs.append(dot(kt[h * HD : (h + 1) * HD, :keys], ds[:, h * QB : (h + 1) * QB]))
            dq = (jnp.concatenate(outs, axis=0).T * SCALE).astype(BF)
            dqkv[at, lanes(0)] = dq
            qsum += jnp.sum(dq.astype(F32), axis=0, keepdims=True)
            off += keys
            turn = blocks * q + i

            @pl.when(turn < reduce_turns)
            def _():
                tick((i + 1) % 2, (turn + 1) // 2)

            if inside and i == reduce_turns % blocks:

                @pl.when(turn == reduce_turns)
                def _():
                    gather_begin()

            if inside:
                hop = turn - reduce_turns - 1

                @pl.when(jnp.logical_and(hop >= 0, hop < 2 * AHEAD))
                def _():
                    gather_tick(i % 2, hop // 2)
        dv = dv_ref[...].astype(BF)
        dqkv[:, lanes(1)] = dk_ref[...].astype(BF)
        dqkv[:, lanes(2)] = dv
        vsum = jnp.sum(dv.astype(F32), axis=0, keepdims=True)
        for (name, sel) in ((s_send, first), (qsum_ref, jnp.logical_not(first))):

            @pl.when(sel)
            def _():
                name[0:1, own] = qsum
                name[1:2, own] = vsum

        @pl.when(q == pairs - 1)
        def _():
            s_across().start()
            load(6).wait()
            load(7).wait()

            @pl.loop(0, 3)
            def _(k):
                to = pl.ds(pl.multiple_of(cols3 + k * cols, cols), cols)
                q_send[k] = dot(rows1[...], dqkv[:, to], TN).astype(BF)
                q_across(k).start()

    if not inside:
        tick(1, turns // 2)

        @pl.loop(turns // 2 + 1, n - 1)
        def _(s):
            for kind in range(2):
                tick(kind, s)
        gather_begin()
    for k in (8, 9):
        load(k).wait()
    nb = 256

    def back(start, at):
        sel = pl.ds(pl.multiple_of(start, rows), rows)
        total = dot(dqkv[sel, 0:cols], wq[0, at, :], NT)
        for k in range(1, 6):
            w = wq if k < 3 else wqf
            total += dot(dqkv[sel, k * cols : (k + 1) * cols], w[k % 3, at, :], NT)
        return total

    @pl.loop(0, width // nb)
    def _(k):
        at = pl.ds(pl.multiple_of(k * nb, nb), nb)
        psend[:, at] = back((1 - core) * rows, at).astype(BF)

    part_beside().start()
    next_hop()

    @pl.loop(0, width // nb)
    def _(k):
        at = pl.ds(pl.multiple_of(k * nb, nb), nb)
        n1g[:, at] = back(core * rows, at)

    next_hop()
    part_beside().wait()
    load(10).wait()
    load(11).wait()
    nsum_ref[...] = jnp.zeros_like(nsum_ref)
    step = 64

    @pl.loop(0, rows // step)
    def _(r):
        at = pl.ds(pl.multiple_of(r * step, step), step)
        grad = n1g[at, :] + pgot[at, :].astype(F32)
        normed, scale = norm_stats(x[at, :].astype(F32))
        g = grad * g1_ref[...]
        mean_g = jnp.mean(g, axis=-1, keepdims=True)
        mean_gn = jnp.mean(g * normed, axis=-1, keepdims=True)
        in_ref[at, :] = rgrad[at, :] + scale * (g - mean_g - normed * mean_gn)
        nsum_ref[0:1, :] += jnp.sum(grad * normed, axis=0, keepdims=True)
        nsum_ref[1:2, :] += jnp.sum(grad, axis=0, keepdims=True)

    put(4).start()
    next_hop()
    mixed = dot(mg[...], att[:, 0:cols], TN)
    m_across().wait()
    qg_ref[3] = (mixed + m_got[...].astype(F32)).astype(BF)
    put(3).start()
    s_across().wait()
    qsum_ref[...] += s_got[...]
    next_hop()

    @pl.loop(0, 3)
    def _(k):
        to = pl.ds(pl.multiple_of(k * cols, cols), cols)
        qg = dot(rows1[...], dqkv[:, to], TN)
        q_across(k).wait()
        qg_ref[k] = (qg + q_got[k].astype(F32)).astype(BF)
        put(k).start()

    while hops:
        next_hop()
    for k in range(5):
        put(k).wait()


def backward(mg, qkv, att, rows1, wq, wqf, wm, wmf, x, rgrad, rg, eg, carry, segments, g1, n):
    rows, width = x.shape
    seq = mg.shape[0]
    cols = wq.shape[2]
    blocks = seq // QB
    vmem = pl.BlockSpec(memory_space=pltpu.VMEM)
    anyspace = pl.BlockSpec(memory_space=pl.ANY)
    split = rg.shape
    chunk = split[2:]
    return pl.pallas_call(
        functools.partial(bwd_kernel, n),
        in_specs=[anyspace] * 13 + [vmem] * 2,
        out_specs=[anyspace] * 2 + [vmem] * 2 + [anyspace] * 2,
        out_shape=[
            jax.ShapeDtypeStruct((rows, width), F32),
            jax.ShapeDtypeStruct((4, width, cols), BF),
            jax.ShapeDtypeStruct((2, cols), F32),
            jax.ShapeDtypeStruct((2, width), F32),
            jax.ShapeDtypeStruct(split, BF),
            jax.ShapeDtypeStruct(split, BF),
        ],
        scratch_shapes=[
            pltpu.VMEM((rows, width), F32),
            pltpu.VMEM((4, width, cols), BF),
            pltpu.VMEM(mg.shape, BF),
            pltpu.VMEM(qkv.shape, BF),
            pltpu.VMEM(att.shape, BF),
            pltpu.VMEM(rows1.shape, BF),
            pltpu.VMEM(wq.shape, BF),
            pltpu.VMEM(wq.shape, BF),
            pltpu.VMEM(wm.shape, BF),
            pltpu.VMEM(wm.shape, BF),
            pltpu.VMEM(x.shape, BF),
            pltpu.VMEM(rgrad.shape, F32),
            pltpu.VMEM((2,) + split, BF),
            pltpu.VMEM((n - 1, 2, 2) + chunk, BF),
            pltpu.VMEM(qkv.shape, BF),
            pltpu.VMEM((seq, cols), BF),
            pltpu.VMEM((QB * blocks * (blocks + 1) // 2, QB), F32),
            pltpu.VMEM((seq, PAIR), F32),
            pltpu.VMEM((seq, PAIR), F32),
            pltpu.VMEM((3, width, cols), BF),
            pltpu.VMEM((3, width, cols), BF),
            pltpu.VMEM((width, cols), BF),
            pltpu.VMEM((width, cols), BF),
            pltpu.VMEM((2, cols), F32),
            pltpu.VMEM((2, cols), F32),
            pltpu.VMEM((rows, width), BF),
            pltpu.VMEM((rows, width), BF),
            pltpu.VMEM((rows, width), F32),
            pltpu.SemaphoreType.DMA((6,)),
            pltpu.SemaphoreType.DMA((6,)),
            pltpu.SemaphoreType.DMA((2, 2)),
            pltpu.SemaphoreType.DMA((2, 2, n - 1)),
            pltpu.SemaphoreType.DMA((2, 2)),
            pltpu.SemaphoreType.DMA((2, 2, n - 1)),
            pltpu.SemaphoreType.DMA((14,)),
            pltpu.SemaphoreType.DMA((5,)),
        ],
        compiler_params=pltpu.CompilerParams(
            collective_id=4, has_side_effects=True, vmem_limit_bytes=60 << 20
        ),
        name="backward",
    )(mg, qkv, att, rows1, wq, wqf, wm, wmf, x, rgrad, rg, eg, carry, segments, g1)


GA = 0.7978845608028654
GB = 0.044715


def ff_kernel(
    n,
    n2_ref, og_hbm, we_hbm, wr_hbm, resid_hbm, be_ref, gain_ref,
    rgrad_out, mg_out, rg_out, eg_out, brn_out, brf_out, usum_ref, dsum_ref, carry_ref,
    rgrad_ref, mg_ref, rg_ref, eg_ref, brn_ref, brf_ref,
    og_ref, we_ref, wr_ref, resid_ref, n2b, act, pg, ng, br, ng_d, br_d, ng_s, br_s, ng_far, ng_out,
    rbuf, send, recv, ring_send, ring_recv, local, out,
):
    rows, width = n2_ref.shape
    units = we_ref.shape[1]
    part = rows // 2
    nb = 256
    me = lax.axis_index("tensor")
    core = me % 2
    sib = me + 1 - 2 * core
    far = (me + 2) % 4

    mine, pos, sides = ring_place(n)
    meet((sib, far), sides)
    h = rg_ref.shape[2]

    def remote(src, dst, k, other):
        return pltpu.make_async_remote_copy(
            src_ref=src,
            dst_ref=dst,
            send_sem=send.at[k],
            recv_sem=recv.at[k],
            device_id={"tensor": other},
            device_id_type=MESH_ID,
        )

    def y_at(c):
        return pl.ds((2 + c) * rows, part)

    def d_at(c):
        return pl.ds((2 + c) * rows + part, part)

    def rows_across(c):
        return remote(n2_ref.at[pl.ds(c * part, part)], n2b.at[y_at(c)], c, far)

    def rows_beside():
        return remote(n2_ref, n2b.at[pl.ds(rows, rows)], 2, sib)

    def rows_forward(c):
        return remote(n2b.at[y_at(c)], n2b.at[d_at(c)], 3 + c, sib)

    def ng_beside():
        return remote(ng.at[pl.ds(rows, rows)], ng_s, 5, sib)

    def br_beside():
        return remote(br.at[pl.ds(rows, rows)], br_s, 6, sib)

    def ng_combine(c):
        return remote(ng.at[d_at(c)], ng_d.at[c], 7 + c, sib)

    def br_combine(c):
        return remote(br.at[d_at(c)], br_d.at[c], 9 + c, sib)

    def ng_across(c):
        return remote(ng_out.at[c], ng_far.at[c], 11 + c, far)

    def own_half(c):
        return pl.ds(pl.multiple_of(core * rows + c * part, part), part)

    def mg_beside(c):
        return remote(mg_ref.at[pl.ds(c * part, part)], mg_out.at[own_half(c)], 13 + c, sib)

    def put(k):
        low, high = pl.ds(0, part), pl.ds(part, part)
        src, dst = (
            (rg_ref, rg_out),
            (eg_ref, eg_out),
            (brn_ref, brn_out),
            (brf_ref, brf_out),
            (rgrad_ref.at[low], rgrad_out.at[low]),
            (rgrad_ref.at[high], rgrad_out.at[high]),
            (mg_ref.at[low], mg_out.at[own_half(0)]),
            (mg_ref.at[high], mg_out.at[own_half(1)]),
        )[k]
        return pltpu.make_async_copy(src, dst, out.at[k])

    for c in range(2):
        rows_across(c).start()
    rows_beside().start()
    first = pl.ds(0, rows)
    rest = pl.ds(rows, 3 * rows)
    loads = [
        pltpu.make_async_copy(n2_ref, n2b.at[first], local.at[0]),
        pltpu.make_async_copy(we_hbm, we_ref, local.at[1]),
        pltpu.make_async_copy(og_hbm.at[first], og_ref.at[first], local.at[2]),
        pltpu.make_async_copy(wr_hbm, wr_ref, local.at[3]),
        pltpu.make_async_copy(og_hbm.at[rest], og_ref.at[rest], local.at[4]),
        pltpu.make_async_copy(resid_hbm, resid_ref, local.at[5]),
    ]
    for load in loads:
        load.start()
    usum_ref[...] = jnp.zeros_like(usum_ref)
    for load in loads[:4]:
        load.wait()

    @pl.loop(0, 4)
    def _(b):
        at = pl.ds(pl.multiple_of(b * rows, rows), rows)
        c = b - 2

        @pl.when(b == 1)
        def _():
            rows_beside().wait()
            loads[4].wait()

        @pl.when(b >= 2)
        def _():
            rows_across(c).wait()
            rows_forward(c).start()
            rows_forward(c).wait()

        for k in range(units // nb):
            cols = slice(k * nb, (k + 1) * nb)
            u = dot(n2b[at, :], we_ref[:, cols]) + be_ref[:, cols]
            act_grad = dot(og_ref[at, :], wr_ref[cols, :], NT)
            sq = u * u
            th = jnp.tanh(u * (GA + (GA * GB) * sq))
            cdf = 0.5 * (1.0 + th)
            slope = cdf + (0.5 * u) * (1.0 - th * th) * (GA + (3.0 * GA * GB) * sq)
            pre = (act_grad * slope).astype(BF)
            act[at, cols] = (u * cdf).astype(BF)
            pg[at, cols] = pre
            usum_ref[:, cols] += jnp.sum(pre.astype(F32), axis=0, keepdims=True)
        @pl.loop(0, width // nb)
        def _(k):
            cols = pl.ds(pl.multiple_of(k * nb, nb), nb)
            ng[at, cols] = dot(pg[at, :], we_ref[cols, :], NT).astype(BF)

        @pl.when(b == 1)
        def _():
            ng_beside().start()

        @pl.when(b >= 2)
        def _():
            ng_combine(c).start()

        @pl.loop(0, width // nb)
        def _(k):
            cols = pl.ds(pl.multiple_of(k * nb, nb), nb)
            br[at, cols] = dot(act[at, :], wr_ref[:, cols]).astype(BF)

        @pl.when(b == 1)
        def _():
            br_beside().start()

        @pl.when(b >= 2)
        def _():
            br_combine(c).start()
            ng_combine(c).wait()
            ng_out[c] = (ng[y_at(c), :].astype(F32) + ng_d[c].astype(F32)).astype(BF)
            ng_across(c).start()

    def part_of(d, s):
        return ring_index(pos - 1 - s if d == 0 else pos + 1 + s, n)

    def ring_copy(src, d):
        return pltpu.make_async_remote_copy(
            src_ref=src,
            dst_ref=rbuf.at[d],
            send_sem=ring_send.at[d],
            recv_sem=ring_recv.at[d],
            device_id={"dp": sides[d]},
            device_id_type=MESH_ID,
        )

    @pl.loop(0, width // nb)
    def _(k):
        cols = pl.ds(pl.multiple_of(k * nb, nb), nb)
        grad = dot(act[...], og_ref[:, cols], TN).astype(BF)
        rg_ref[:, :, :, cols] = grad.reshape(n, 2, h, nb)

    for d in range(2):
        ring_copy(rg_ref.at[part_of(d, 0), d], d).start()
    put(0).start()

    @pl.loop(0, width // nb)
    def _(k):
        cols = pl.ds(pl.multiple_of(k * nb, nb), nb)
        grad = dot(n2b[...], pg[:, cols], TN).astype(BF)
        eg_ref[:, :, :, cols] = grad.reshape(n, 2, h, nb)

    put(1).start()
    br_beside().wait()
    brn_ref[...] = (br[0:rows, :].astype(F32) + br_s[...].astype(F32)).astype(BF)
    for c in range(2):
        br_combine(c).wait()
        brf_ref[c * part : (c + 1) * part, :] = (
            br[y_at(c), :].astype(F32) + br_d[c].astype(F32)
        ).astype(BF)
    put(2).start()
    put(3).start()
    ng_beside().wait()
    loads[5].wait()
    dsum_ref[...] = jnp.zeros_like(dsum_ref)
    step = 64
    for c in range(2):
        ng_across(c).wait()

        @pl.loop(0, part // step)
        def _(r):
            inner = pl.ds(pl.multiple_of(r * step, step), step)
            at = pl.ds(pl.multiple_of(c * part + r * step, step), step)
            grad = ng[at, :].astype(F32) + ng_s[at, :].astype(F32) + ng_far[c, inner, :].astype(F32)
            normed, scale = norm_stats(resid_ref[at, :])
            g = grad * gain_ref[...]
            gn = g * normed
            mean_g = jnp.mean(g, axis=-1, keepdims=True)
            mean_gn = jnp.mean(gn, axis=-1, keepdims=True)
            og = og_ref[at, :].astype(F32)
            rgrad = og + scale * (g - mean_g - normed * mean_gn)
            rgrad_ref[at, :] = rgrad
            mg = rgrad.astype(BF)
            mg_ref[at, :] = mg
            dsum_ref[0:1, :] += jnp.sum(mg.astype(F32), axis=0, keepdims=True)
            dsum_ref[1:2, :] += jnp.sum(grad * normed, axis=0, keepdims=True)
            dsum_ref[2:3, :] += jnp.sum(grad, axis=0, keepdims=True)
            dsum_ref[3:4, :] += jnp.sum(og, axis=0, keepdims=True)

        mg_beside(c).start()
        put(4 + c).start()
        put(6 + c).start()

    for d in range(2):
        ring_copy(rg_ref.at[part_of(d, 0), d], d).wait()
        carry_ref[d] = (rbuf[d].astype(F32) + rg_ref[part_of(d, 1), d].astype(F32)).astype(BF)
    for c in range(2):
        mg_beside(c).wait()
    for k in range(8):
        put(k).wait()


def ff(n2, og_all, we, wr, be, resid, gain, n):
    rows, width = n2.shape
    units = we.shape[1]
    part = rows // 2
    vmem = pl.BlockSpec(memory_space=pltpu.VMEM)
    anyspace = pl.BlockSpec(memory_space=pl.ANY)
    return pl.pallas_call(
        functools.partial(ff_kernel, n),
        in_specs=[anyspace] * 5 + [vmem] * 2,
        out_specs=[anyspace] * 6 + [vmem] * 3,
        out_shape=[
            jax.ShapeDtypeStruct((rows, width), F32),
            jax.ShapeDtypeStruct((2 * rows, width), BF),
            jax.ShapeDtypeStruct((n, 2, units // (2 * n), width), BF),
            jax.ShapeDtypeStruct((n, 2, width // (2 * n), units), BF),
            jax.ShapeDtypeStruct((rows, width), BF),
            jax.ShapeDtypeStruct((rows, width), BF),
            jax.ShapeDtypeStruct((1, units), F32),
            jax.ShapeDtypeStruct((4, width), F32),
            jax.ShapeDtypeStruct((2, units // (2 * n), width), BF),
        ],
        scratch_shapes=[
            pltpu.VMEM((rows, width), F32),
            pltpu.VMEM((rows, width), BF),
            pltpu.VMEM((n, 2, units // (2 * n), width), BF),
            pltpu.VMEM((n, 2, width // (2 * n), units), BF),
            pltpu.VMEM((rows, width), BF),
            pltpu.VMEM((rows, width), BF),
            pltpu.VMEM((4 * rows, width), BF),
            pltpu.VMEM(we.shape, BF),
            pltpu.VMEM(wr.shape, BF),
            pltpu.VMEM((rows, width), F32),
            pltpu.VMEM((4 * rows, width), BF),
            pltpu.VMEM((4 * rows, units), BF),
            pltpu.VMEM((4 * rows, units), BF),
            pltpu.VMEM((4 * rows, width), BF),
            pltpu.VMEM((4 * rows, width), BF),
            pltpu.VMEM((2, part, width), BF),
            pltpu.VMEM((2, part, width), BF),
            pltpu.VMEM((rows, width), BF),
            pltpu.VMEM((rows, width), BF),
            pltpu.VMEM((2, part, width), BF),
            pltpu.VMEM((2, part, width), BF),
            pltpu.VMEM((2, units // (2 * n), width), BF),
            pltpu.SemaphoreType.DMA((15,)),
            pltpu.SemaphoreType.DMA((15,)),
            pltpu.SemaphoreType.DMA((2,)),
            pltpu.SemaphoreType.DMA((2,)),
            pltpu.SemaphoreType.DMA((6,)),
            pltpu.SemaphoreType.DMA((8,)),
        ],
        compiler_params=pltpu.CompilerParams(
            collective_id=2, has_side_effects=True, vmem_limit_bytes=60 << 20
        ),
        name="ff",
    )(n2, og_all, we, wr, resid, be, gain)


def ring_kernel(
    n, g_ref, norm_ref, dsum_ref, usum_ref, qsum_ref, rbias_ref, resid_hbm, brn_hbm, brf_hbm, _r, _e,
    qo_ref, mo_ref, ro_ref, eo_ref, so_ref, bo_ref,
    buf, rows8, small_ref, sbuf, sall, speer, ssum, resid, brn, bro,
    send, recv, fsend, frecv, ssend, srecv, tsend, trecv, local,
):
    mine, pos, sides = ring_place(n)
    me = lax.axis_index("tensor")
    far = (me + 2) % 4
    peers = [(me + k) % 4 for k in range(1, 4)]
    loads = (
        pltpu.make_async_copy(resid_hbm, resid, local.at[0]),
        pltpu.make_async_copy(brn_hbm, brn, local.at[1]),
    )
    for load in loads:
        load.start()
    meet(peers, sides)

    cols = qsum_ref.shape[1]
    piece = small_ref.shape[2]
    per = rows8.shape[1] // piece
    rows8[0:2] = norm_ref[...]
    rows8[2:6] = dsum_ref[...]
    rows8[6:7] = usum_ref[...]
    rows8[7:8] = jnp.zeros_like(rows8[7:8])
    for k in range(2):
        rows8[7:8, k * cols : (k + 1) * cols] = qsum_ref[k : k + 1, :]

    def in_row(c):
        return slice(c // per, c // per + 1), slice(c % per * piece, (c % per + 1) * piece)

    for c in range(n):
        small_ref[c] = rows8[in_row(c)]

    def remote(src, dst, kind, d, s):
        return pltpu.make_async_remote_copy(
            src_ref=src,
            dst_ref=dst,
            send_sem=send.at[kind, d],
            recv_sem=recv.at[kind, d, s],
            device_id={"dp": sides[d]},
            device_id_type=MESH_ID,
        )

    def little(src, dst, kind, s):
        return pltpu.make_async_remote_copy(
            src_ref=src,
            dst_ref=dst,
            send_sem=ssend.at[kind],
            recv_sem=srecv.at[kind, s],
            device_id={"dp": sides[0]},
            device_id_type=MESH_ID,
        )

    def beside(src, dst, k, other):
        return pltpu.make_async_remote_copy(
            src_ref=src,
            dst_ref=dst,
            send_sem=tsend.at[k],
            recv_sem=trecv.at[k],
            device_id={"tensor": other},
            device_id_type=MESH_ID,
        )

    def share(k):
        return beside(small_ref, speer.at[k], k, peers[k])

    def branch():
        return beside(brf_hbm, bro, 3, far)

    def part(d, s):
        return ring_index(pos - 1 - s if d == 0 else pos + 1 + s, n)

    def held(d, s):
        return ring_index(pos - s if d == 0 else pos + s, n)

    streams = [(k, d) for k in range(4) for d in range(2)]

    def source(k, chunk, d):
        return g_ref.at[k, chunk, d]

    def slot(k, s, d):
        return buf.at[s, d, k]

    def put_at(k, chunk, d):
        return qo_ref.at[k, chunk, d] if k < 3 else mo_ref.at[chunk, d]

    def add(k, d, s):
        ref = slot(k, s, d)
        total = ref[...].astype(F32) + source(k, part(d, s + 1), d)[...].astype(F32)
        ref[...] = total.astype(BF)

    def gather(k, d, s):
        ref = put_at(k, held(d, s), d)
        return remote(ref, ref, 4 + k, d, s)

    left = n - 1 - AHEAD
    half = ro_ref.shape[3] // 2

    def ff_hop(kind, c, d, s):
        ref = (ro_ref, eo_ref)[kind].at[held(d, s), d, :, pl.ds(c * half, half)]
        k = 2 * kind + c
        return pltpu.make_async_remote_copy(
            src_ref=ref,
            dst_ref=ref,
            send_sem=fsend.at[k, d],
            recv_sem=frecv.at[k, d, s - AHEAD],
            device_id={"dp": sides[d]},
            device_id_type=MESH_ID,
        )

    def beside_step(kind, s, act):
        @pl.when(s < left)
        def _():
            for d in range(2):
                act(ff_hop(kind, 0, d, AHEAD + s))

        @pl.when(s >= n - 1 - left)
        def _():
            for d in range(2):
                act(ff_hop(kind, 1, d, AHEAD + s - (n - 1 - left)))

    def start(copy):
        copy.start()

    def finish(copy):
        copy.wait()

    def gather_small(s):
        ref = sall.at[held(0, s)]
        return little(ref, ref, 1, s)

    for k, d in streams:
        remote(source(k, part(d, 0), d), slot(k, 0, d), k, d, 0).start()
    for k in range(3):
        share(k).start()
    branch().start()
    for k in range(3):
        share(k).wait()
    ssum[...] = small_ref[...]
    shared = n * 6 // 8
    ssum[0:shared] = ssum[0:shared] + speer[0, 0:shared] + speer[1, 0:shared] + speer[2, 0:shared]
    little(ssum.at[part(0, 0)], sbuf.at[0], 0, 0).start()

    @pl.loop(0, n - 2)
    def _(s):
        beside_step(0, s, start)
        for k, d in streams:
            remote(slot(k, s, d), slot(k, s, d), k, d, s).wait()
            add(k, d, s)
            remote(slot(k, s, d), slot(k, s + 1, d), k, d, s + 1).start()
        little(sbuf.at[s], sbuf.at[s], 0, s).wait()
        sbuf[s] = sbuf[s] + ssum[part(0, s + 1)]
        little(sbuf.at[s], sbuf.at[s + 1], 0, s + 1).start()
        beside_step(0, s, finish)

    last = n - 2
    beside_step(0, last, start)
    puts = []
    for k, d in streams:
        remote(slot(k, last, d), slot(k, last, d), k, d, last).wait()
        add(k, d, last)
        put = pltpu.make_async_copy(slot(k, last, d), put_at(k, mine, d), local.at[2 + 2 * k + d])
        put.start()
        puts.append(put)
    for (k, d), put in zip(streams, puts):
        put.wait()
        gather(k, d, 0).start()
    little(sbuf.at[last], sbuf.at[last], 0, last).wait()
    sall[mine] = sbuf[last] + ssum[mine]
    gather_small(0).start()
    beside_step(0, last, finish)

    @pl.loop(0, n - 2)
    def _(s):
        beside_step(1, s, start)
        for k, d in streams:
            gather(k, d, s).wait()
            gather(k, d, s + 1).start()
        gather_small(s).wait()
        gather_small(s + 1).start()
        beside_step(1, s, finish)

    beside_step(1, last, start)

    branch().wait()
    for load in loads:
        load.wait()
    step = 64

    @pl.loop(0, bo_ref.shape[0] // step)
    def _(r):
        at = pl.ds(pl.multiple_of(r * step, step), step)
        total = resid[at, :] + brn[at, :].astype(F32) + bro[at, :].astype(F32) + rbias_ref[...]
        bo_ref[at, :] = total.astype(BF)

    for k, d in streams:
        gather(k, d, last).wait()
    gather_small(last).wait()
    for c in range(n):
        so_ref[in_row(c)] = sall[c]
    beside_step(1, last, finish)


def ring_sum(g, norm, dsum, usum, qsum, resid, brn, brf, r, e, rbias, n):
    split = (4, n, 2, g.shape[1] // (2 * n), g.shape[2])
    s3 = jax.ShapeDtypeStruct((n, 1, 8 * norm.shape[1] // n), F32)
    small = jax.ShapeDtypeStruct((8, norm.shape[1]), F32)
    vmem = pl.BlockSpec(memory_space=pltpu.VMEM)
    anyspace = pl.BlockSpec(memory_space=pl.ANY)
    qo, mo, ro, eo, so, bo = pl.pallas_call(
        functools.partial(ring_kernel, n),
        in_specs=[vmem] * 6 + [anyspace] * 5,
        out_specs=[anyspace] * 4 + [vmem] * 2,
        input_output_aliases={9: 2, 10: 3},
        out_shape=[
            jax.ShapeDtypeStruct((3,) + split[1:], BF),
            jax.ShapeDtypeStruct(split[1:], BF),
            jax.ShapeDtypeStruct(r.shape, BF),
            jax.ShapeDtypeStruct(e.shape, BF),
            small,
            jax.ShapeDtypeStruct(brf.shape, BF),
        ],
        scratch_shapes=[
            pltpu.VMEM((n - 1, 2, 4) + split[3:], BF),
            pltpu.VMEM(small.shape, F32),
            pltpu.VMEM(s3.shape, F32),
            pltpu.VMEM((n - 1,) + s3.shape[1:], F32),
            pltpu.VMEM(s3.shape, F32),
            pltpu.VMEM((3,) + s3.shape, F32),
            pltpu.VMEM(s3.shape, F32),
            pltpu.VMEM(resid.shape, F32),
            pltpu.VMEM(brn.shape, BF),
            pltpu.VMEM(brf.shape, BF),
            pltpu.SemaphoreType.DMA((8, 2)),
            pltpu.SemaphoreType.DMA((8, 2, n - 1)),
            pltpu.SemaphoreType.DMA((4, 2)),
            pltpu.SemaphoreType.DMA((4, 2, n - 1 - AHEAD)),
            pltpu.SemaphoreType.DMA((2,)),
            pltpu.SemaphoreType.DMA((2, n - 1)),
            pltpu.SemaphoreType.DMA((4,)),
            pltpu.SemaphoreType.DMA((4,)),
            pltpu.SemaphoreType.DMA((10,)),
        ],
        compiler_params=pltpu.CompilerParams(
            collective_id=1, has_side_effects=True, vmem_limit_bytes=60 << 20
        ),
        name="ring_sum",
    )(g.reshape(split), norm, dsum, usum, qsum, rbias, resid, brn, brf, r, e)
    wide = (-1, r.shape[-1])
    return (
        qo.reshape((3,) + g.shape[1:]),
        mo.reshape(g.shape[1:]),
        ro.reshape(wide),
        eo.reshape(wide),
        so,
        bo,
    )


def finish_kernel(
    q_hbm, m_hbm, r_hbm, e_hbm, in_hbm, bo_hbm, small_ref,
    bo_out, in_out, q_out, m_out, r_out, e_out, g1_ref, s1_ref, mb_ref, g2_ref, s2_ref, rb_ref, eb_ref, qb_ref,
    q_in, m_in, r_in, e_in, q_wide, m_wide, r_wide, e_wide, in_mid, bo_mid, read, write,
):
    enter = (
        pltpu.make_async_copy(in_hbm, in_mid, read.at[12]),
        pltpu.make_async_copy(bo_hbm, bo_mid, read.at[13]),
    )
    leave = (
        pltpu.make_async_copy(in_mid, in_out, write.at[0]),
        pltpu.make_async_copy(bo_mid, bo_out, write.at[1]),
    )
    quarter = r_in.shape[0] // 4
    jobs = []
    for c in range(4):
        at = pl.ds(c * quarter, quarter)
        for src, mid, wide, dst in ((r_hbm, r_in, r_wide, r_out), (e_hbm, e_in, e_wide, e_out)):
            jobs.append((src.at[at], mid.at[at], wide.at[at], dst.at[at]))
    for k in range(3):
        jobs.append((q_hbm.at[k], q_in.at[k], q_wide.at[k], q_out.at[k]))
    gets = [pltpu.make_async_copy(job[0], job[1], read.at[k]) for k, job in enumerate(jobs)]
    get_m = pltpu.make_async_copy(m_hbm, m_in, read.at[len(jobs)])
    get_m.start()
    for copy in enter:
        copy.start()
    for get in gets:
        get.start()
    for k, ref in enumerate((g1_ref, s1_ref, mb_ref, g2_ref, s2_ref, rb_ref, eb_ref)):
        ref[...] = small_ref[k : k + 1, :]
    cols = qb_ref.shape[1]
    for k in range(2):
        qb_ref[k : k + 1, :] = small_ref[7:8, k * cols : (k + 1) * cols]
    for k in range(2):
        enter[k].wait()
        leave[k].start()
    get_m.wait()
    m_wide[...] = m_in[...].astype(F32).T
    puts = [pltpu.make_async_copy(m_wide, m_out, write.at[2])]
    puts[0].start()
    for k, (_src, mid, wide, dst) in enumerate(jobs):
        gets[k].wait()
        step = 64

        @pl.loop(0, mid.shape[0] // step)
        def _(r):
            at = pl.ds(pl.multiple_of(r * step, step), step)
            wide[at] = mid[at].astype(F32)

        put = pltpu.make_async_copy(wide, dst, write.at[3 + k])
        put.start()
        puts.append(put)
    for copy in leave:
        copy.wait()
    for put in puts:
        put.wait()


def finish(q, m, r, e, in_grad, block_out, small):
    vmem = pl.BlockSpec(memory_space=pltpu.VMEM)
    anyspace = pl.BlockSpec(memory_space=pl.ANY)
    width = small.shape[1]
    row = jax.ShapeDtypeStruct((1, width), F32)
    return pl.pallas_call(
        finish_kernel,
        in_specs=[anyspace] * 6 + [vmem],
        out_specs=[anyspace] * 6 + [vmem] * 8,
        out_shape=[
            jax.ShapeDtypeStruct(block_out.shape, BF),
            jax.ShapeDtypeStruct(in_grad.shape, F32),
            jax.ShapeDtypeStruct(q.shape, F32),
            jax.ShapeDtypeStruct(m.shape[::-1], F32),
            jax.ShapeDtypeStruct(r.shape, F32),
            jax.ShapeDtypeStruct(e.shape, F32),
        ]
        + [row] * 7
        + [jax.ShapeDtypeStruct((2, q.shape[2]), F32)],
        scratch_shapes=[
            pltpu.VMEM(q.shape, BF),
            pltpu.VMEM(m.shape, BF),
            pltpu.VMEM(r.shape, BF),
            pltpu.VMEM(e.shape, BF),
            pltpu.VMEM(q.shape, F32),
            pltpu.VMEM(m.shape[::-1], F32),
            pltpu.VMEM(r.shape, F32),
            pltpu.VMEM(e.shape, F32),
            pltpu.VMEM(in_grad.shape, F32),
            pltpu.VMEM(block_out.shape, BF),
            pltpu.SemaphoreType.DMA((14,)),
            pltpu.SemaphoreType.DMA((14,)),
        ],
        compiler_params=pltpu.CompilerParams(vmem_limit_bytes=60 << 20),
        name="finish",
    )(q, m, r, e, in_grad, block_out, small)


def body(
    block_in,
    segments,
    first_gain,
    first_shift,
    w_qkv,
    qv_bias,
    w_mix,
    mix_bias,
    second_gain,
    second_shift,
    w_expand,
    expand_bias,
    w_reduce,
    reduce_bias,
    out_grad,
):
    width = block_in.shape[1]
    cols = w_qkv.shape[2]
    units = w_expand.shape[1]
    dp_size = lax.axis_size("dp")
    flat = (1, width)
    wq = w_qkv.transpose(1, 0, 2)
    rows1, qkv, att, resid, n2, wq_far, wm_far, og_all = forward(
        block_in,
        segments,
        first_gain.reshape(flat),
        first_shift.reshape(flat),
        qv_bias,
        mix_bias.reshape(flat),
        second_gain.reshape(flat),
        second_shift.reshape(flat),
        wq,
        w_mix,
        out_grad,
        dp_size,
    )
    resid_grad, mg_all, reduce_grad, expand_grad, br_near, br_far, unit_sums, sums2, carry = ff(
        n2, og_all, w_expand, w_reduce, expand_bias.reshape(1, units), resid, second_gain.reshape(flat), dp_size
    )
    in_grad, grads, qv_sums, norm_sums, reduce_all, expand_all = backward(
        mg_all,
        qkv,
        att,
        rows1,
        wq,
        wq_far,
        w_mix,
        wm_far,
        block_in,
        resid_grad,
        reduce_grad,
        expand_grad,
        carry,
        segments,
        first_gain.reshape(flat),
        dp_size,
    )
    qkv_grad, mix_grad, reduce_all, expand_all, small, block_out = ring_sum(
        grads,
        norm_sums,
        sums2,
        unit_sums,
        qv_sums,
        resid,
        br_near,
        br_far,
        reduce_all,
        expand_all,
        reduce_bias.reshape(flat),
        dp_size,
    )
    block_out, in_grad, qkv_grad, mix_grad, reduce_all, expand_all, *rest, qv_bias_grad = finish(
        qkv_grad, mix_grad, reduce_all, expand_all, in_grad, block_out, small
    )
    g1, s1, mb, g2, s2, rb, eb = (item.reshape(-1) for item in rest)
    return (
        block_out,
        in_grad,
        g1,
        s1,
        qkv_grad.transpose(1, 0, 2),
        qv_bias_grad,
        mix_grad,
        mb,
        g2,
        s2,
        expand_all,
        eb,
        reduce_all,
        rb,
    )


def solution(mesh):
    both = P(("dp", "tensor"), None)
    return jax.shard_map(
        body,
        mesh=mesh,
        in_specs=(
            both,
            P("dp", None),
            P(),
            P(),
            P(None, None, "tensor"),
            P(None, "tensor"),
            P("tensor", None),
            P(),
            P(),
            P(),
            P(None, "tensor"),
            P("tensor"),
            P("tensor", None),
            P(),
            both,
        ),
        out_specs=(
            both,
            both,
            P(),
            P(),
            P(None, None, "tensor"),
            P(None, "tensor"),
            P("tensor", None),
            P(),
            P(),
            P(),
            P(None, "tensor"),
            P("tensor"),
            P("tensor", None),
            P(),
        ),
        check_vma=False,
    )
```

```python
import functools

import jax
import jax.numpy as jnp
from jax import lax
from jax.experimental import pallas as pl
from jax.experimental.pallas import tpu as pltpu
from jax.sharding import PartitionSpec as P

HD = 64
PAIR = 2 * HD
QB = 256
EPS = 1e-5
BF = jnp.bfloat16
F32 = jnp.float32
SCALE = HD ** (-0.5)
MESH_ID = pl.DeviceIdType.MESH
AHEAD = 3
NT = (((1,), (1,)), ((), ()))
TN = (((0,), (0,)), ((), ()))


def dot(a, b, dims=(((1,), (0,)), ((), ()))):
    return lax.dot_general(a, b, dims, preferred_element_type=F32)


def norm_stats(values):
    mean = jnp.mean(values, axis=-1, keepdims=True)
    centered = values - mean
    variance = jnp.mean(centered * centered, axis=-1, keepdims=True)
    scale = lax.rsqrt(variance + EPS)
    return centered * scale, scale


def fill_bias(seg_ref, row, bias_ref, blocks):
    segr = seg_ref[pl.ds(row, 1), :].astype(F32)
    segc = jnp.broadcast_to(segr, (8, segr.shape[1])).T[:, 0:1]
    off = 0
    for i in range(blocks):
        keys = (i + 1) * QB
        kpos = lax.broadcasted_iota(jnp.int32, (keys, QB), 0)
        qpos = lax.broadcasted_iota(jnp.int32, (keys, QB), 1) + i * QB
        same = segc[:keys, :] == segr[:, i * QB : (i + 1) * QB]
        allowed = jnp.logical_and(kpos <= qpos, same)
        bias_ref[off : off + keys, :] = jnp.where(allowed, 0.0, -1e30)
        off += keys


def half_masks():
    lane = lax.broadcasted_iota(jnp.int32, (1, PAIR), 1)
    return (lane < HD, lane >= HD)


def ring_index(at, n):
    at = (at + 2 * n) % n
    far = at // (n // 2)
    return (1 - far) * 2 * at + far * (2 * (n - 1 - at) + 1)


def ring_place(n):
    mine = lax.axis_index("dp")
    odd = mine % 2
    pos = (1 - odd) * (mine // 2) + odd * (n - 1 - mine // 2)
    return mine, pos, (ring_index(pos + 1, n), ring_index(pos - 1, n))


def meet(tensor_peers, dp_peers):
    barrier = pltpu.get_barrier_semaphore()
    for other in tensor_peers:
        pl.semaphore_signal(barrier, inc=1, device_id={"tensor": other}, device_id_type=MESH_ID)
    for other in dp_peers:
        pl.semaphore_signal(barrier, inc=1, device_id={"dp": other}, device_id_type=MESH_ID)
    pl.semaphore_wait(barrier, len(tensor_peers) + len(dp_peers))


def both_heads(a, masks):
    zero = jnp.zeros_like(a)
    return jnp.concatenate([jnp.where(masks[0], a, zero), jnp.where(masks[1], a, zero)], axis=0)


def twice(a):
    return jnp.concatenate([a, a], axis=1)


def fwd_kernel(
    n,
    x_ref, seg_ref, g1_ref, s1_ref, bq_ref, mixb_ref, g2_ref, s2_ref, wq_hbm, wm_hbm, og_ref,
    rows1_out, qkv_out, att_out, resid_out, n2_out, wqf_out, wmf_out, oga_ref,
    rows1_ref, qkv_ref, att_ref, resid_ref, n2_ref, w_all, wm_all,
    b_all, bqf, bias_ref, psend, pgot, send, recv, ring_send, ring_recv, local, out,
):
    rows, width = x_ref.shape
    seq = rows1_ref.shape[0]
    cols = w_all.shape[3]
    wqf_ref = w_all.at[1]
    wmf_ref = wm_all.at[1]
    cols3 = 3 * cols
    half = rows // 2
    blocks = seq // QB
    me = lax.axis_index("tensor")
    core = me % 2
    sib = me + 1 - 2 * core
    far = (me + 2) % 4
    mine, pos, sides = ring_place(n)
    meet((sib, far), sides)

    def remote(src, dst, k, other):
        return pltpu.make_async_remote_copy(
            src_ref=src,
            dst_ref=dst,
            send_sem=send.at[k],
            recv_sem=recv.at[k],
            device_id={"tensor": other},
            device_id_type=MESH_ID,
        )

    slab = width // n
    wide = cols // 2

    def slab_rows(chunk):
        return pl.ds(pl.multiple_of(chunk * slab, slab), slab)

    mix_slab = wm_hbm.shape[0] // n
    around = mix_slab % 16 == 0
    streams = 4 if around else 3

    def mix_rows(chunk):
        return pl.ds(pl.multiple_of(chunk * mix_slab, mix_slab), mix_slab)

    def piece():
        return remote(wq_hbm.at[:, slab_rows(mine)], wqf_ref.at[:, slab_rows(mine)], 0, far)

    def bias_across():
        return remote(bq_ref, bqf, 1, far)

    def own_half(c):
        return pl.ds(pl.multiple_of(core * rows + c * half, half), half)

    def rows_beside(c):
        return remote(rows1_ref.at[own_half(c)], rows1_ref.at[own_half(c)], 2 + c, sib)

    def mix_across():
        if around:
            return remote(wm_hbm.at[mix_rows(mine)], wmf_ref.at[mix_rows(mine)], 4, far)
        return remote(wm_hbm, wmf_ref, 4, far)

    def og_across(c):
        return remote(
            og_ref.at[pl.ds(c * half, half)], oga_ref.at[pl.ds((2 + c) * rows, half)], 5 + c, far
        )

    def og_beside():
        return remote(og_ref, oga_ref.at[pl.ds(rows, rows)], 7, sib)

    def og_forward(c):
        return remote(
            oga_ref.at[pl.ds((2 + c) * rows, half)],
            oga_ref.at[pl.ds((2 + c) * rows + half, half)],
            8 + c,
            sib,
        )

    def part_beside():
        return remote(psend, pgot, 10, sib)

    def og_own():
        return pltpu.make_async_copy(og_ref, oga_ref.at[pl.ds(0, rows)], local.at[0])

    reach = n // 2

    def hop(k, d, s, part=False):
        chunk = ring_index(pos - s if d == 0 else pos + s, n)
        side = width // 2 if k == 3 else wide
        lanes = slice(d * side, (d + 1) * side) if part else slice(None)
        ref = wmf_ref.at[mix_rows(chunk), lanes] if k == 3 else wqf_ref.at[k, slab_rows(chunk), lanes]
        return pltpu.make_async_remote_copy(
            src_ref=ref,
            dst_ref=ref,
            send_sem=ring_send.at[k, d],
            recv_sem=ring_recv.at[k, d, s],
            device_id={"dp": sides[d]},
            device_id_type=MESH_ID,
        )

    def tick(s):
        for k in range(streams):
            for d in range(2):
                hop(k, d, s).wait()

                @pl.when(s < reach - 2)
                def _():
                    hop(k, d, s + 1).start()

                @pl.when(s == reach - 2)
                def _():
                    hop(k, d, s + 1, True).start()

    def last_tick():
        for k in range(3):
            for d in range(2):
                hop(k, d, reach - 1, True).wait()

    def put(k):
        near = pl.ds(0, cols3)
        far_part = pl.ds(cols3, cols3)
        low, high = pl.ds(0, half), pl.ds(half, half)
        src, dst = (
            (rows1_ref, rows1_out),
            (qkv_ref.at[:, near], qkv_out.at[:, near]),
            (qkv_ref.at[:, far_part], qkv_out.at[:, far_part]),
            (wqf_ref, wqf_out),
            (wmf_ref, wmf_out),
            (att_ref, att_out),
            (resid_ref.at[low], resid_out.at[low]),
            (resid_ref.at[high], resid_out.at[high]),
            (n2_ref.at[low], n2_out.at[low]),
            (n2_ref.at[high], n2_out.at[high]),
        )[k]
        return pltpu.make_async_copy(src, dst, out.at[k])

    piece().start()
    if around:
        mix_across().start()
    bias_across().start()
    loads = (
        pltpu.make_async_copy(wq_hbm, w_all.at[0], local.at[1]),
        pltpu.make_async_copy(wm_hbm, wm_all.at[0], local.at[2]),
    )
    for load in loads:
        load.start()
    step = 64
    for c in range(2):

        @pl.loop(0, half // step)
        def _(r):
            normed = norm_stats(x_ref[pl.ds(pl.multiple_of(c * half + r * step, step), step), :].astype(F32))[0]
            to = pl.ds(pl.multiple_of(core * rows + c * half + r * step, step), step)
            rows1_ref[to, :] = (normed * g1_ref[...] + s1_ref[...]).astype(BF)

        rows_beside(c).start()
    piece().wait()
    for k in range(3):
        for d in range(2):
            hop(k, d, 0).start()
    if around:
        mix_across().wait()
        for d in range(2):
            hop(3, d, 0).start()
    else:
        mix_across().start()
    for c in range(2):
        og_across(c).start()
    og_beside().start()
    og_own().start()
    fill_bias(seg_ref, me // 2, bias_ref, blocks)

    def fill_shift(g, ref):
        b_all[g, 0:1] = ref[0:1]
        b_all[g, 1:2] = jnp.zeros_like(ref[0:1])
        b_all[g, 2:3] = ref[1:2]

    fill_shift(0, bq_ref)
    for c in range(2):
        rows_beside(c).wait()
    for load in loads:
        load.wait()
    put(0).start()
    masks = half_masks()
    pairs = cols // PAIR
    ticks = 1 + pairs

    @pl.loop(0, 2 * pairs)
    def _(p):
        group = p // pairs

        @pl.when(p == pairs)
        def _():
            @pl.loop(ticks, reach - 1)
            def _(s):
                tick(s)

            last_tick()
            bias_across().wait()
            fill_shift(1, bqf)
            put(3).start()

        @pl.when(p % pairs == 0)
        def _():
            @pl.loop(0, 3)
            def _(k):
                to = pl.ds(pl.multiple_of(group * cols3 + k * cols, cols), cols)
                part = dot(rows1_ref[...], w_all[group, k]) + b_all[group, pl.ds(k, 1)]
                qkv_ref[:, to] = part.astype(BF)

        @pl.when(p == 0)
        def _():
            put(1).start()
            tick(0)

        @pl.when(p == pairs)
        def _():
            put(2).start()

        base = group * cols3 + (p % pairs) * PAIR

        def lanes(k):
            return pl.ds(pl.multiple_of(base + k * cols, PAIR), PAIR)

        vt = qkv_ref[:, lanes(2)].T
        off = 0
        for i in range(blocks):
            keys = (i + 1) * QB
            at = slice(i * QB, (i + 1) * QB)
            qi = qkv_ref[at, lanes(0)] * jnp.asarray(SCALE, BF)
            kk = qkv_ref[:keys, lanes(1)]
            s = dot(kk, both_heads(qi, masks), NT) + twice(bias_ref[off : off + keys, :])
            e = jnp.exp(s - jnp.max(s, axis=0, keepdims=True))
            inverse = 1.0 / jnp.sum(e, axis=0, keepdims=True)
            e = e.astype(BF)
            outs = []
            for h in range(2):
                side = slice(h * QB, (h + 1) * QB)
                outs.append(dot(vt[h * HD : (h + 1) * HD, :keys], e[:, side]) * inverse[:, side])
            att_ref[at, pl.ds(pl.multiple_of(p * PAIR, PAIR), PAIR)] = jnp.concatenate(outs, axis=0).T.astype(BF)
            off += keys
            if i == blocks - 1:

                @pl.when(p < pairs)
                def _():
                    tick(1 + p)

    if around:
        for d in range(2):
            hop(3, d, reach - 1, True).wait()
    else:
        mix_across().wait()
    put(4).start()
    put(5).start()
    nb = 256

    def mixed(start, at):
        sel = pl.ds(pl.multiple_of(start, rows), rows)
        total = dot(att_ref[sel, 0:cols], wm_all[0, :, at])
        return total + dot(att_ref[sel, cols : 2 * cols], wm_all[1, :, at])

    @pl.loop(0, width // nb)
    def _(k):
        at = pl.ds(pl.multiple_of(k * nb, nb), nb)
        psend[:, at] = mixed((1 - core) * rows, at).astype(BF)

    part_beside().start()

    @pl.loop(0, width // nb)
    def _(k):
        at = pl.ds(pl.multiple_of(k * nb, nb), nb)
        resid_ref[:, at] = x_ref[:, at].astype(F32) + mixed(core * rows, at) + mixb_ref[:, at]

    for c in range(2):
        og_across(c).wait()
        og_forward(c).start()
    part_beside().wait()

    for c in range(2):

        @pl.loop(0, half // step)
        def _(r):
            at = pl.ds(pl.multiple_of(c * half + r * step, step), step)
            full = resid_ref[at, :] + pgot[at, :].astype(F32)
            resid_ref[at, :] = full
            n2_ref[at, :] = (norm_stats(full)[0] * g2_ref[...] + s2_ref[...]).astype(BF)

        put(6 + c).start()
        put(8 + c).start()

    for k in range(10):
        put(k).wait()
    og_own().wait()
    og_beside().wait()
    for c in range(2):
        og_forward(c).wait()


def forward(x, segments, g1, s1, bq, mixb, g2, s2, wq, wm, og, n):
    rows, width = x.shape
    seq = segments.shape[1]
    cols = wq.shape[2]
    blocks = seq // QB
    vmem = pl.BlockSpec(memory_space=pltpu.VMEM)
    anyspace = pl.BlockSpec(memory_space=pl.ANY)
    return pl.pallas_call(
        functools.partial(fwd_kernel, n),
        in_specs=[vmem] * 8 + [anyspace] * 3,
        out_specs=[anyspace] * 8,
        out_shape=[
            jax.ShapeDtypeStruct((seq, width), BF),
            jax.ShapeDtypeStruct((seq, 6 * cols), BF),
            jax.ShapeDtypeStruct((seq, 2 * cols), BF),
            jax.ShapeDtypeStruct((rows, width), F32),
            jax.ShapeDtypeStruct((rows, width), BF),
            jax.ShapeDtypeStruct(wq.shape, BF),
            jax.ShapeDtypeStruct(wm.shape, BF),
            jax.ShapeDtypeStruct((4 * rows, width), BF),
        ],
        scratch_shapes=[
            pltpu.VMEM((seq, width), BF),
            pltpu.VMEM((seq, 6 * cols), BF),
            pltpu.VMEM((seq, 2 * cols), BF),
            pltpu.VMEM((rows, width), F32),
            pltpu.VMEM((rows, width), BF),
            pltpu.VMEM((2,) + wq.shape, BF),
            pltpu.VMEM((2,) + wm.shape, BF),
            pltpu.VMEM((2, 3, cols), F32),
            pltpu.VMEM((2, cols), F32),
            pltpu.VMEM((QB * blocks * (blocks + 1) // 2, QB), F32),
            pltpu.VMEM((rows, width), BF),
            pltpu.VMEM((rows, width), BF),
            pltpu.SemaphoreType.DMA((11,)),
            pltpu.SemaphoreType.DMA((11,)),
            pltpu.SemaphoreType.DMA((4, 2)),
            pltpu.SemaphoreType.DMA((4, 2, n // 2)),
            pltpu.SemaphoreType.DMA((3,)),
            pltpu.SemaphoreType.DMA((10,)),
        ],
        compiler_params=pltpu.CompilerParams(
            collective_id=3, has_side_effects=True, vmem_limit_bytes=56 << 20
        ),
        name="forward",
    )(x, segments, g1, s1, bq, mixb, g2, s2, wq, wm, og)


def ring_part(
    n, between, g_ref, norm_ref, qsum_ref, dsum_ref, usum_ref, rbias_ref, resid_hbm, brn_hbm, brf_hbm,
    qo_ref, mo_ref, ro_ref, eo_ref, so_ref, bo_ref,
    buf, rows8, small_ref, sbuf, sall, speer, ssum, resid, brn, bro,
    send, recv, fsend, frecv, ssend, srecv, tsend, trecv, local,
):
    mine, pos, sides = ring_place(n)
    me = lax.axis_index("tensor")
    far = (me + 2) % 4
    peers = [(me + k) % 4 for k in range(1, 4)]
    loads = (
        pltpu.make_async_copy(resid_hbm, resid, local.at[0]),
        pltpu.make_async_copy(brn_hbm, brn, local.at[1]),
    )
    for load in loads:
        load.start()

    cols = qsum_ref.shape[1]
    piece = small_ref.shape[2]
    per = rows8.shape[1] // piece
    rows8[0:2] = norm_ref[...]
    rows8[2:6] = dsum_ref[...]
    rows8[6:7] = usum_ref[...]
    rows8[7:8] = jnp.zeros_like(rows8[7:8])
    for k in range(2):
        rows8[7:8, k * cols : (k + 1) * cols] = qsum_ref[k : k + 1, :]

    def in_row(c):
        return slice(c // per, c // per + 1), slice(c % per * piece, (c % per + 1) * piece)

    for c in range(n):
        small_ref[c] = rows8[in_row(c)]

    def remote(src, dst, kind, d, s):
        return pltpu.make_async_remote_copy(
            src_ref=src,
            dst_ref=dst,
            send_sem=send.at[kind, d],
            recv_sem=recv.at[kind, d, s],
            device_id={"dp": sides[d]},
            device_id_type=MESH_ID,
        )

    def little(src, dst, kind, s):
        return pltpu.make_async_remote_copy(
            src_ref=src,
            dst_ref=dst,
            send_sem=ssend.at[kind],
            recv_sem=srecv.at[kind, s],
            device_id={"dp": sides[0]},
            device_id_type=MESH_ID,
        )

    def beside(src, dst, k, other):
        return pltpu.make_async_remote_copy(
            src_ref=src,
            dst_ref=dst,
            send_sem=tsend.at[k],
            recv_sem=trecv.at[k],
            device_id={"tensor": other},
            device_id_type=MESH_ID,
        )

    def share(k):
        return beside(small_ref, speer.at[k], k, peers[k])

    def branch():
        return beside(brf_hbm, bro, 3, far)

    def part(d, s):
        return ring_index(pos - 1 - s if d == 0 else pos + 1 + s, n)

    def held(d, s):
        return ring_index(pos - s if d == 0 else pos + s, n)

    streams = [(k, d) for k in range(4) for d in range(2)]

    def source(k, chunk, d):
        return g_ref.at[k, chunk, d]

    def slot(k, s, d):
        return buf.at[s, d, k]

    def put_at(k, chunk, d):
        return qo_ref.at[k, chunk, d] if k < 3 else mo_ref.at[chunk, d]

    def add(k, d, s):
        ref = slot(k, s, d)
        total = ref[...].astype(F32) + source(k, part(d, s + 1), d)[...].astype(F32)
        ref[...] = total.astype(BF)

    def gather(k, d, s):
        ref = put_at(k, held(d, s), d)
        return remote(ref, ref, 4 + k, d, s)

    left = n - 1 - AHEAD
    half = ro_ref.shape[3] // 2

    def ff_hop(kind, c, d, s):
        ref = (ro_ref, eo_ref)[kind].at[held(d, s), d, :, pl.ds(c * half, half)]
        k = 2 * kind + c
        return pltpu.make_async_remote_copy(
            src_ref=ref,
            dst_ref=ref,
            send_sem=fsend.at[k, d],
            recv_sem=frecv.at[k, d, s - AHEAD],
            device_id={"dp": sides[d]},
            device_id_type=MESH_ID,
        )

    def beside_step(kind, s, act):
        @pl.when(s < left)
        def _():
            for d in range(2):
                act(ff_hop(kind, 0, d, AHEAD + s))

        @pl.when(s >= n - 1 - left)
        def _():
            for d in range(2):
                act(ff_hop(kind, 1, d, AHEAD + s - (n - 1 - left)))

    def start(copy):
        copy.start()

    def finish(copy):
        copy.wait()

    def gather_small(s):
        ref = sall.at[held(0, s)]
        return little(ref, ref, 1, s)

    for k, d in streams:
        remote(source(k, part(d, 0), d), slot(k, 0, d), k, d, 0).start()
    for k in range(3):
        share(k).start()
    branch().start()
    between()
    for k in range(3):
        share(k).wait()
    ssum[...] = small_ref[...]
    shared = n * 6 // 8
    ssum[0:shared] = ssum[0:shared] + speer[0, 0:shared] + speer[1, 0:shared] + speer[2, 0:shared]
    little(ssum.at[part(0, 0)], sbuf.at[0], 0, 0).start()

    @pl.loop(0, n - 2)
    def _(s):
        beside_step(0, s, start)
        for k, d in streams:
            remote(slot(k, s, d), slot(k, s, d), k, d, s).wait()
            add(k, d, s)
            remote(slot(k, s, d), slot(k, s + 1, d), k, d, s + 1).start()
        little(sbuf.at[s], sbuf.at[s], 0, s).wait()
        sbuf[s] = sbuf[s] + ssum[part(0, s + 1)]
        little(sbuf.at[s], sbuf.at[s + 1], 0, s + 1).start()
        beside_step(0, s, finish)

    last = n - 2
    beside_step(0, last, start)
    puts = []
    for k, d in streams:
        remote(slot(k, last, d), slot(k, last, d), k, d, last).wait()
        add(k, d, last)
        put = pltpu.make_async_copy(slot(k, last, d), put_at(k, mine, d), local.at[2 + 2 * k + d])
        put.start()
        puts.append(put)
    for (k, d), put in zip(streams, puts):
        put.wait()
        gather(k, d, 0).start()
    little(sbuf.at[last], sbuf.at[last], 0, last).wait()
    sall[mine] = sbuf[last] + ssum[mine]
    gather_small(0).start()
    beside_step(0, last, finish)

    @pl.loop(0, n - 2)
    def _(s):
        beside_step(1, s, start)
        for k, d in streams:
            gather(k, d, s).wait()
            gather(k, d, s + 1).start()
        gather_small(s).wait()
        gather_small(s + 1).start()
        beside_step(1, s, finish)

    beside_step(1, last, start)

    branch().wait()
    for load in loads:
        load.wait()
    step = 64

    @pl.loop(0, bo_ref.shape[0] // step)
    def _(r):
        at = pl.ds(pl.multiple_of(r * step, step), step)
        total = resid[at, :] + brn[at, :].astype(F32) + bro[at, :].astype(F32) + rbias_ref[...]
        bo_ref[at, :] = total.astype(BF)

    for k, d in streams:
        gather(k, d, last).wait()
    gather_small(last).wait()
    for c in range(n):
        so_ref[in_row(c)] = sall[c]
    beside_step(1, last, finish)


def bwd_kernel(
    n,
    mg_hbm, qkv_hbm, att_hbm, rows1_hbm, wq_hbm, wqf_hbm, wm_hbm, wmf_hbm, x_hbm, rgrad_hbm, rg_hbm, eg_hbm, carry_hbm,
    resid_hbm, brn_hbm, brf_hbm, seg_ref, g1_ref, dsum_ref, usum_ref, rbias_ref,
    in_out, qo_ref, mo_ref, ro_ref, eo_ref, so_ref, bo_ref,
    in_ref, qg_ref, qsum_ref, nsum_ref,
    mg, qkv, att, rows1, wq, wqf, wm, wmf, x, rgrad, ffg,
    rbuf, dqkv, ag, bias_ref, dk_ref, dv_ref, q_send, q_got, m_send, m_got, s_got, s_send, psend, pgot, n1g,
    send, recv, ring_send, ring_recv, gather_send, gather_recv, local, out,
    *ring_scratch,
):
    rows, width = in_ref.shape
    seq = mg.shape[0]
    cols = wq.shape[2]
    cols3 = 3 * cols
    pairs = cols // PAIR
    blocks = seq // QB
    me = lax.axis_index("tensor")
    core = me % 2
    sib = me + 1 - 2 * core
    far = (me + 2) % 4
    mine, pos, sides = ring_place(n)

    pairs_in = (
        (mg_hbm, mg), (wmf_hbm, wmf), (att_hbm, att), (qkv_hbm, qkv), (rg_hbm, ffg.at[0]), (eg_hbm, ffg.at[1]),
        (rows1_hbm, rows1), (wm_hbm, wm), (wqf_hbm, wqf), (wq_hbm, wq), (x_hbm, x), (rgrad_hbm, rgrad),
    )

    def load(k):
        return pltpu.make_async_copy(pairs_in[k][0], pairs_in[k][1], local.at[k])

    for k in range(len(pairs_in)):
        load(k).start()
    meet([(me + k) % 4 for k in range(1, 4)], sides)

    def remote(src, dst, k, other):
        return pltpu.make_async_remote_copy(
            src_ref=src,
            dst_ref=dst,
            send_sem=send.at[k],
            recv_sem=recv.at[k],
            device_id={"tensor": other},
            device_id_type=MESH_ID,
        )

    def q_across(k):
        return remote(q_send.at[k], q_got.at[k], k, far)

    def m_across():
        return remote(m_send, m_got, 3, far)

    def s_across():
        return remote(s_send, s_got, 4, far)

    def part_beside():
        return remote(psend, pgot, 5, sib)

    def ring_copy(src, kind, d, s):
        return pltpu.make_async_remote_copy(
            src_ref=src,
            dst_ref=rbuf.at[s, kind, d],
            send_sem=ring_send.at[kind, d],
            recv_sem=ring_recv.at[kind, d, s],
            device_id={"dp": sides[d]},
            device_id_type=MESH_ID,
        )

    def part(d, s):
        return ring_index(pos - 1 - s if d == 0 else pos + 1 + s, n)

    def tick(kind, s):
        for d in range(2):
            ring_copy(rbuf.at[s, kind, d], kind, d, s).wait()
            mixed = rbuf[s, kind, d].astype(F32) + ffg[kind, part(d, s + 1), d].astype(F32)
            rbuf[s, kind, d] = mixed.astype(BF)

            @pl.when(s < n - 2)
            def _():
                ring_copy(rbuf.at[s, kind, d], kind, d, s + 1).start()

    outs_hbm = (ro_ref, eo_ref)

    def put_in():
        return pltpu.make_async_copy(in_ref, in_out, out.at[0])

    def gather(kind, d, s):
        chunk = ring_index(pos - s if d == 0 else pos + s, n)
        ref = outs_hbm[kind].at[chunk, d]
        return pltpu.make_async_remote_copy(
            src_ref=ref,
            dst_ref=ref,
            send_sem=gather_send.at[kind, d],
            recv_sem=gather_recv.at[kind, d, s],
            device_id={"dp": sides[d]},
            device_id_type=MESH_ID,
        )

    def gather_tick(kind, s):
        for d in range(2):
            gather(kind, d, s).wait()

            @pl.when(s + 1 < AHEAD)
            def _():
                gather(kind, d, s + 1).start()

    def gather_begin():
        owns = [
            pltpu.make_async_copy(rbuf.at[n - 2, kind], outs_hbm[kind].at[mine], local.at[12 + kind])
            for kind in range(2)
        ]
        for item in owns:
            item.start()
        for kind in range(2):
            owns[kind].wait()
            for d in range(2):
                gather(kind, d, 0).start()

    for kind in range(2):
        for d in range(2):
            ring_copy(carry_hbm.at[kind, d], kind, d, 1).start()

    fill_bias(seg_ref, me // 2, bias_ref, blocks)
    masks = half_masks()
    for k in range(6):
        load(k).wait()
    m_send[...] = dot(mg[...], att[:, cols : 2 * cols], TN).astype(BF)
    m_across().start()
    ag[...] = dot(mg[...], wmf[...], NT).astype(BF)

    turns = 2 * pairs + blocks * pairs
    hops = [(kind, s) for s in range(AHEAD) for kind in range(2)]

    def next_hop():
        if hops:
            gather_tick(*hops.pop(0))

    @pl.loop(0, 2 * pairs)
    def _(q):
        first = q < pairs
        group = 1 - q // pairs
        slot = q % pairs
        base = group * cols3 + slot * PAIR

        @pl.when(q == pairs)
        def _():
            ag[...] = dot(mg[...], wm[...], NT).astype(BF)

        def lanes(k):
            return pl.ds(pl.multiple_of(base + k * cols, PAIR), PAIR)

        own = pl.ds(pl.multiple_of(slot * PAIR, PAIR), PAIR)
        kt = qkv[:, lanes(1)].T
        dk_ref[...] = jnp.zeros_like(dk_ref)
        dv_ref[...] = jnp.zeros_like(dv_ref)
        off = 0
        qsum = jnp.zeros((1, PAIR), F32)
        for i in range(blocks):
            keys = (i + 1) * QB
            at = slice(i * QB, (i + 1) * QB)
            qi = qkv[at, lanes(0)] * jnp.asarray(SCALE, BF)
            gi = ag[at, own]
            kk = qkv[:keys, lanes(1)]
            vv = qkv[:keys, lanes(2)]
            q2 = both_heads(qi, masks)
            g2 = both_heads(gi, masks)
            s = dot(kk, q2, NT) + twice(bias_ref[off : off + keys, :])
            e = jnp.exp(s - jnp.max(s, axis=0, keepdims=True))
            prob = e * (1.0 / jnp.sum(e, axis=0, keepdims=True))
            weighted = prob * dot(vv, g2, NT)
            ds = (weighted - prob * jnp.sum(weighted, axis=0, keepdims=True)).astype(BF)
            dv_ref[:keys, :] += dot(prob.astype(BF), g2)
            dk_ref[:keys, :] += dot(ds, q2)
            outs = []
            for h in range(2):
                outs.append(dot(kt[h * HD : (h + 1) * HD, :keys], ds[:, h * QB : (h + 1) * QB]))
            dq = (jnp.concatenate(outs, axis=0).T * SCALE).astype(BF)
            dqkv[at, lanes(0)] = dq
            qsum += jnp.sum(dq.astype(F32), axis=0, keepdims=True)
            off += keys
            late = 2 * pairs + blocks * (q - pairs) + i

            @pl.when(jnp.logical_and(q >= pairs, late < 2 * (n - 2)))
            def _():
                tick(i % 2, 1 + late // 2)

            if i % 2 == 1:

                @pl.when(first)
                def _():
                    tick(i // 2, 1 + q)

        dv = dv_ref[...].astype(BF)
        dqkv[:, lanes(1)] = dk_ref[...].astype(BF)
        dqkv[:, lanes(2)] = dv
        vsum = jnp.sum(dv.astype(F32), axis=0, keepdims=True)
        for (name, sel) in ((s_send, first), (qsum_ref, jnp.logical_not(first))):

            @pl.when(sel)
            def _():
                name[0:1, own] = qsum
                name[1:2, own] = vsum

        @pl.when(q == pairs - 1)
        def _():
            s_across().start()
            load(6).wait()
            load(7).wait()

            @pl.loop(0, 3)
            def _(k):
                to = pl.ds(pl.multiple_of(cols3 + k * cols, cols), cols)
                q_send[k] = dot(rows1[...], dqkv[:, to], TN).astype(BF)
                q_across(k).start()

    @pl.loop(1 + turns // 2, n - 1)
    def _(s):
        for kind in range(2):
            tick(kind, s)

    gather_begin()
    for k in (8, 9):
        load(k).wait()
    nb = 256

    def back(start, at):
        sel = pl.ds(pl.multiple_of(start, rows), rows)
        total = dot(dqkv[sel, 0:cols], wq[0, at, :], NT)
        for k in range(1, 6):
            w = wq if k < 3 else wqf
            total += dot(dqkv[sel, k * cols : (k + 1) * cols], w[k % 3, at, :], NT)
        return total

    @pl.loop(0, width // nb)
    def _(k):
        at = pl.ds(pl.multiple_of(k * nb, nb), nb)
        psend[:, at] = back((1 - core) * rows, at).astype(BF)

    part_beside().start()
    next_hop()

    @pl.loop(0, width // nb)
    def _(k):
        at = pl.ds(pl.multiple_of(k * nb, nb), nb)
        n1g[:, at] = back(core * rows, at)

    next_hop()
    part_beside().wait()
    load(10).wait()
    load(11).wait()
    nsum_ref[...] = jnp.zeros_like(nsum_ref)
    step = 64

    @pl.loop(0, rows // step)
    def _(r):
        at = pl.ds(pl.multiple_of(r * step, step), step)
        grad = n1g[at, :] + pgot[at, :].astype(F32)
        normed, scale = norm_stats(x[at, :].astype(F32))
        g = grad * g1_ref[...]
        mean_g = jnp.mean(g, axis=-1, keepdims=True)
        mean_gn = jnp.mean(g * normed, axis=-1, keepdims=True)
        in_ref[at, :] = rgrad[at, :] + scale * (g - mean_g - normed * mean_gn)
        nsum_ref[0:1, :] += jnp.sum(grad * normed, axis=0, keepdims=True)
        nsum_ref[1:2, :] += jnp.sum(grad, axis=0, keepdims=True)

    put_in().start()
    next_hop()
    mixed = dot(mg[...], att[:, 0:cols], TN)
    m_across().wait()
    pieces = qg_ref.shape[1:]
    qg_ref[3] = (mixed + m_got[...].astype(F32)).astype(BF).reshape(pieces)
    s_across().wait()
    qsum_ref[...] += s_got[...]
    next_hop()

    @pl.loop(0, 3)
    def _(k):
        to = pl.ds(pl.multiple_of(k * cols, cols), cols)
        qg = dot(rows1[...], dqkv[:, to], TN)
        q_across(k).wait()
        qg_ref[k] = (qg + q_got[k].astype(F32)).astype(BF).reshape(pieces)

    def rest_of_hops():
        while hops:
            next_hop()

    ring_part(
        n, rest_of_hops, qg_ref, nsum_ref, qsum_ref, dsum_ref, usum_ref, rbias_ref, resid_hbm, brn_hbm, brf_hbm,
        qo_ref, mo_ref, ro_ref, eo_ref, so_ref, bo_ref,
        *ring_scratch,
    )
    put_in().wait()


def backward(
    mg, qkv, att, rows1, wq, wqf, wm, wmf, x, rgrad, rg, eg, carry, resid, brn, brf,
    segments, g1, dsum, usum, rbias, n,
):
    rows, width = x.shape
    seq = mg.shape[0]
    cols = wq.shape[2]
    blocks = seq // QB
    vmem = pl.BlockSpec(memory_space=pltpu.VMEM)
    anyspace = pl.BlockSpec(memory_space=pl.ANY)
    split = rg.shape
    chunk = split[2:]
    pieces = (4, n, 2, width // (2 * n), cols)
    small = (n, 1, 8 * width // n)
    in_grad, qo, mo, ro, eo, so, bo = pl.pallas_call(
        functools.partial(bwd_kernel, n),
        in_specs=[anyspace] * 16 + [vmem] * 5,
        out_specs=[anyspace] * 5 + [vmem] * 2,
        out_shape=[
            jax.ShapeDtypeStruct((rows, width), F32),
            jax.ShapeDtypeStruct((3,) + pieces[1:], BF),
            jax.ShapeDtypeStruct(pieces[1:], BF),
            jax.ShapeDtypeStruct(split, BF),
            jax.ShapeDtypeStruct(split, BF),
            jax.ShapeDtypeStruct((8, width), F32),
            jax.ShapeDtypeStruct((rows, width), BF),
        ],
        scratch_shapes=[
            pltpu.VMEM((rows, width), F32),
            pltpu.VMEM(pieces, BF),
            pltpu.VMEM((2, cols), F32),
            pltpu.VMEM((2, width), F32),
            pltpu.VMEM(mg.shape, BF),
            pltpu.VMEM(qkv.shape, BF),
            pltpu.VMEM(att.shape, BF),
            pltpu.VMEM(rows1.shape, BF),
            pltpu.VMEM(wq.shape, BF),
            pltpu.VMEM(wq.shape, BF),
            pltpu.VMEM(wm.shape, BF),
            pltpu.VMEM(wm.shape, BF),
            pltpu.VMEM(x.shape, BF),
            pltpu.VMEM(rgrad.shape, F32),
            pltpu.VMEM((2,) + split, BF),
            pltpu.VMEM((n - 1, 2, 2) + chunk, BF),
            pltpu.VMEM(qkv.shape, BF),
            pltpu.VMEM((seq, cols), BF),
            pltpu.VMEM((QB * blocks * (blocks + 1) // 2, QB), F32),
            pltpu.VMEM((seq, PAIR), F32),
            pltpu.VMEM((seq, PAIR), F32),
            pltpu.VMEM((3, width, cols), BF),
            pltpu.VMEM((3, width, cols), BF),
            pltpu.VMEM((width, cols), BF),
            pltpu.VMEM((width, cols), BF),
            pltpu.VMEM((2, cols), F32),
            pltpu.VMEM((2, cols), F32),
            pltpu.VMEM((rows, width), BF),
            pltpu.VMEM((rows, width), BF),
            pltpu.VMEM((rows, width), F32),
            pltpu.SemaphoreType.DMA((6,)),
            pltpu.SemaphoreType.DMA((6,)),
            pltpu.SemaphoreType.DMA((2, 2)),
            pltpu.SemaphoreType.DMA((2, 2, n - 1)),
            pltpu.SemaphoreType.DMA((2, 2)),
            pltpu.SemaphoreType.DMA((2, 2, n - 1)),
            pltpu.SemaphoreType.DMA((14,)),
            pltpu.SemaphoreType.DMA((1,)),
            pltpu.VMEM((n - 1, 2, 4) + pieces[3:], BF),
            pltpu.VMEM((8, width), F32),
            pltpu.VMEM(small, F32),
            pltpu.VMEM((n - 1,) + small[1:], F32),
            pltpu.VMEM(small, F32),
            pltpu.VMEM((3,) + small, F32),
            pltpu.VMEM(small, F32),
            pltpu.VMEM((rows, width), F32),
            pltpu.VMEM((rows, width), BF),
            pltpu.VMEM((rows, width), BF),
            pltpu.SemaphoreType.DMA((8, 2)),
            pltpu.SemaphoreType.DMA((8, 2, n - 1)),
            pltpu.SemaphoreType.DMA((4, 2)),
            pltpu.SemaphoreType.DMA((4, 2, n - 1 - AHEAD)),
            pltpu.SemaphoreType.DMA((2,)),
            pltpu.SemaphoreType.DMA((2, n - 1)),
            pltpu.SemaphoreType.DMA((4,)),
            pltpu.SemaphoreType.DMA((4,)),
            pltpu.SemaphoreType.DMA((10,)),
        ],
        compiler_params=pltpu.CompilerParams(
            collective_id=4, has_side_effects=True, vmem_limit_bytes=60 << 20
        ),
        name="backward",
    )(
        mg, qkv, att, rows1, wq, wqf, wm, wmf, x, rgrad, rg, eg, carry, resid, brn, brf,
        segments, g1, dsum, usum, rbias,
    )
    wide = (-1, width)
    mixed = mo.reshape(width, cols)
    return in_grad, qo.reshape(3, width, cols), mixed, ro.reshape(wide), eo.reshape(wide), so, bo


GA = 0.7978845608028654
GB = 0.044715


def ff_kernel(
    n,
    n2_ref, og_hbm, we_hbm, wr_hbm, resid_hbm, be_ref, gain_ref,
    rgrad_out, mg_out, rg_out, eg_out, brn_out, brf_out, usum_ref, dsum_ref, carry_ref,
    rgrad_ref, mg_ref, rg_ref, eg_ref, brn_ref, brf_ref,
    og_ref, we_ref, wr_ref, resid_ref, n2b, act, pg, ng, br, ng_d, br_d, ng_s, br_s, ng_far, ng_out,
    rbuf, send, recv, ring_send, ring_recv, local, out,
):
    rows, width = n2_ref.shape
    units = we_ref.shape[1]
    part = rows // 2
    nb = 256
    me = lax.axis_index("tensor")
    core = me % 2
    sib = me + 1 - 2 * core
    far = (me + 2) % 4

    mine, pos, sides = ring_place(n)
    meet((sib, far), sides)
    h = rg_ref.shape[2]

    def remote(src, dst, k, other):
        return pltpu.make_async_remote_copy(
            src_ref=src,
            dst_ref=dst,
            send_sem=send.at[k],
            recv_sem=recv.at[k],
            device_id={"tensor": other},
            device_id_type=MESH_ID,
        )

    def y_at(c):
        return pl.ds((2 + c) * rows, part)

    def d_at(c):
        return pl.ds((2 + c) * rows + part, part)

    def rows_across(c):
        return remote(n2_ref.at[pl.ds(c * part, part)], n2b.at[y_at(c)], c, far)

    def rows_beside():
        return remote(n2_ref, n2b.at[pl.ds(rows, rows)], 2, sib)

    def rows_forward(c):
        return remote(n2b.at[y_at(c)], n2b.at[d_at(c)], 3 + c, sib)

    def ng_beside():
        return remote(ng.at[pl.ds(rows, rows)], ng_s, 5, sib)

    def br_beside():
        return remote(br.at[pl.ds(rows, rows)], br_s, 6, sib)

    def ng_combine(c):
        return remote(ng.at[d_at(c)], ng_d.at[c], 7 + c, sib)

    def br_combine(c):
        return remote(br.at[d_at(c)], br_d.at[c], 9 + c, sib)

    def ng_across(c):
        return remote(ng_out.at[c], ng_far.at[c], 11 + c, far)

    def own_half(c):
        return pl.ds(pl.multiple_of(core * rows + c * part, part), part)

    def mg_beside(c):
        return remote(mg_ref.at[pl.ds(c * part, part)], mg_out.at[own_half(c)], 13 + c, sib)

    def put(k):
        low, high = pl.ds(0, part), pl.ds(part, part)
        src, dst = (
            (rg_ref, rg_out),
            (eg_ref, eg_out),
            (brn_ref, brn_out),
            (brf_ref, brf_out),
            (rgrad_ref.at[low], rgrad_out.at[low]),
            (rgrad_ref.at[high], rgrad_out.at[high]),
            (mg_ref.at[low], mg_out.at[own_half(0)]),
            (mg_ref.at[high], mg_out.at[own_half(1)]),
        )[k]
        return pltpu.make_async_copy(src, dst, out.at[k])

    for c in range(2):
        rows_across(c).start()
    rows_beside().start()
    first = pl.ds(0, rows)
    rest = pl.ds(rows, 3 * rows)
    loads = [
        pltpu.make_async_copy(n2_ref, n2b.at[first], local.at[0]),
        pltpu.make_async_copy(we_hbm, we_ref, local.at[1]),
        pltpu.make_async_copy(og_hbm.at[first], og_ref.at[first], local.at[2]),
        pltpu.make_async_copy(wr_hbm, wr_ref, local.at[3]),
        pltpu.make_async_copy(og_hbm.at[rest], og_ref.at[rest], local.at[4]),
        pltpu.make_async_copy(resid_hbm, resid_ref, local.at[5]),
    ]
    for load in loads:
        load.start()
    usum_ref[...] = jnp.zeros_like(usum_ref)
    for load in loads[:4]:
        load.wait()

    @pl.loop(0, 4)
    def _(b):
        at = pl.ds(pl.multiple_of(b * rows, rows), rows)
        c = b - 2

        @pl.when(b == 1)
        def _():
            rows_beside().wait()
            loads[4].wait()

        @pl.when(b >= 2)
        def _():
            rows_across(c).wait()
            rows_forward(c).start()
            rows_forward(c).wait()

        for k in range(units // nb):
            cols = slice(k * nb, (k + 1) * nb)
            u = dot(n2b[at, :], we_ref[:, cols]) + be_ref[:, cols]
            act_grad = dot(og_ref[at, :], wr_ref[cols, :], NT)
            sq = u * u
            th = jnp.tanh(u * (GA + (GA * GB) * sq))
            cdf = 0.5 * (1.0 + th)
            slope = cdf + (0.5 * u) * (1.0 - th * th) * (GA + (3.0 * GA * GB) * sq)
            pre = (act_grad * slope).astype(BF)
            act[at, cols] = (u * cdf).astype(BF)
            pg[at, cols] = pre
            usum_ref[:, cols] += jnp.sum(pre.astype(F32), axis=0, keepdims=True)
        @pl.loop(0, width // nb)
        def _(k):
            cols = pl.ds(pl.multiple_of(k * nb, nb), nb)
            ng[at, cols] = dot(pg[at, :], we_ref[cols, :], NT).astype(BF)

        @pl.when(b == 1)
        def _():
            ng_beside().start()

        @pl.when(b >= 2)
        def _():
            ng_combine(c).start()

        @pl.loop(0, width // nb)
        def _(k):
            cols = pl.ds(pl.multiple_of(k * nb, nb), nb)
            br[at, cols] = dot(act[at, :], wr_ref[:, cols]).astype(BF)

        @pl.when(b == 1)
        def _():
            br_beside().start()

        @pl.when(b >= 2)
        def _():
            br_combine(c).start()
            ng_combine(c).wait()
            ng_out[c] = (ng[y_at(c), :].astype(F32) + ng_d[c].astype(F32)).astype(BF)
            ng_across(c).start()

    def part_of(d, s):
        return ring_index(pos - 1 - s if d == 0 else pos + 1 + s, n)

    ffg = (rg_ref, eg_ref)

    def ring_copy(kind, d):
        return pltpu.make_async_remote_copy(
            src_ref=ffg[kind].at[part_of(d, 0), d],
            dst_ref=rbuf.at[kind, d],
            send_sem=ring_send.at[kind, d],
            recv_sem=ring_recv.at[kind, d],
            device_id={"dp": sides[d]},
            device_id_type=MESH_ID,
        )

    @pl.loop(0, width // nb)
    def _(k):
        cols = pl.ds(pl.multiple_of(k * nb, nb), nb)
        grad = dot(act[...], og_ref[:, cols], TN).astype(BF)
        rg_ref[:, :, :, cols] = grad.reshape(n, 2, h, nb)

    for d in range(2):
        ring_copy(0, d).start()
    put(0).start()

    @pl.loop(0, width // nb)
    def _(k):
        cols = pl.ds(pl.multiple_of(k * nb, nb), nb)
        grad = dot(n2b[...], pg[:, cols], TN).astype(BF)
        eg_ref[:, :, :, cols] = grad.reshape(n, 2, h, nb)

    for d in range(2):
        ring_copy(1, d).start()
    put(1).start()
    br_beside().wait()
    brn_ref[...] = (br[0:rows, :].astype(F32) + br_s[...].astype(F32)).astype(BF)
    for c in range(2):
        br_combine(c).wait()
        brf_ref[c * part : (c + 1) * part, :] = (
            br[y_at(c), :].astype(F32) + br_d[c].astype(F32)
        ).astype(BF)
    put(2).start()
    put(3).start()
    ng_beside().wait()
    loads[5].wait()
    dsum_ref[...] = jnp.zeros_like(dsum_ref)
    step = 64
    for c in range(2):
        ng_across(c).wait()

        @pl.loop(0, part // step)
        def _(r):
            inner = pl.ds(pl.multiple_of(r * step, step), step)
            at = pl.ds(pl.multiple_of(c * part + r * step, step), step)
            grad = ng[at, :].astype(F32) + ng_s[at, :].astype(F32) + ng_far[c, inner, :].astype(F32)
            normed, scale = norm_stats(resid_ref[at, :])
            g = grad * gain_ref[...]
            gn = g * normed
            mean_g = jnp.mean(g, axis=-1, keepdims=True)
            mean_gn = jnp.mean(gn, axis=-1, keepdims=True)
            og = og_ref[at, :].astype(F32)
            rgrad = og + scale * (g - mean_g - normed * mean_gn)
            rgrad_ref[at, :] = rgrad
            mg = rgrad.astype(BF)
            mg_ref[at, :] = mg
            dsum_ref[0:1, :] += jnp.sum(mg.astype(F32), axis=0, keepdims=True)
            dsum_ref[1:2, :] += jnp.sum(grad * normed, axis=0, keepdims=True)
            dsum_ref[2:3, :] += jnp.sum(grad, axis=0, keepdims=True)
            dsum_ref[3:4, :] += jnp.sum(og, axis=0, keepdims=True)

        mg_beside(c).start()
        put(4 + c).start()
        put(6 + c).start()

    for kind in range(2):
        for d in range(2):
            ring_copy(kind, d).wait()
            total = rbuf[kind, d].astype(F32) + ffg[kind][part_of(d, 1), d].astype(F32)
            carry_ref[kind, d] = total.astype(BF)
    for c in range(2):
        mg_beside(c).wait()
    for k in range(8):
        put(k).wait()


def ff(n2, og_all, we, wr, be, resid, gain, n):
    rows, width = n2.shape
    units = we.shape[1]
    part = rows // 2
    vmem = pl.BlockSpec(memory_space=pltpu.VMEM)
    anyspace = pl.BlockSpec(memory_space=pl.ANY)
    return pl.pallas_call(
        functools.partial(ff_kernel, n),
        in_specs=[anyspace] * 5 + [vmem] * 2,
        out_specs=[anyspace] * 6 + [vmem] * 3,
        out_shape=[
            jax.ShapeDtypeStruct((rows, width), F32),
            jax.ShapeDtypeStruct((2 * rows, width), BF),
            jax.ShapeDtypeStruct((n, 2, units // (2 * n), width), BF),
            jax.ShapeDtypeStruct((n, 2, width // (2 * n), units), BF),
            jax.ShapeDtypeStruct((rows, width), BF),
            jax.ShapeDtypeStruct((rows, width), BF),
            jax.ShapeDtypeStruct((1, units), F32),
            jax.ShapeDtypeStruct((4, width), F32),
            jax.ShapeDtypeStruct((2, 2, units // (2 * n), width), BF),
        ],
        scratch_shapes=[
            pltpu.VMEM((rows, width), F32),
            pltpu.VMEM((rows, width), BF),
            pltpu.VMEM((n, 2, units // (2 * n), width), BF),
            pltpu.VMEM((n, 2, width // (2 * n), units), BF),
            pltpu.VMEM((rows, width), BF),
            pltpu.VMEM((rows, width), BF),
            pltpu.VMEM((4 * rows, width), BF),
            pltpu.VMEM(we.shape, BF),
            pltpu.VMEM(wr.shape, BF),
            pltpu.VMEM((rows, width), F32),
            pltpu.VMEM((4 * rows, width), BF),
            pltpu.VMEM((4 * rows, units), BF),
            pltpu.VMEM((4 * rows, units), BF),
            pltpu.VMEM((4 * rows, width), BF),
            pltpu.VMEM((4 * rows, width), BF),
            pltpu.VMEM((2, part, width), BF),
            pltpu.VMEM((2, part, width), BF),
            pltpu.VMEM((rows, width), BF),
            pltpu.VMEM((rows, width), BF),
            pltpu.VMEM((2, part, width), BF),
            pltpu.VMEM((2, part, width), BF),
            pltpu.VMEM((2, 2, units // (2 * n), width), BF),
            pltpu.SemaphoreType.DMA((15,)),
            pltpu.SemaphoreType.DMA((15,)),
            pltpu.SemaphoreType.DMA((2, 2)),
            pltpu.SemaphoreType.DMA((2, 2)),
            pltpu.SemaphoreType.DMA((6,)),
            pltpu.SemaphoreType.DMA((8,)),
        ],
        compiler_params=pltpu.CompilerParams(
            collective_id=2, has_side_effects=True, vmem_limit_bytes=60 << 20
        ),
        name="ff",
    )(n2, og_all, we, wr, resid, be, gain)


def finish_kernel(
    q_hbm, m_hbm, r_hbm, e_hbm, in_hbm, bo_hbm, small_ref,
    bo_out, in_out, q_out, m_out, r_out, e_out, g1_ref, s1_ref, mb_ref, g2_ref, s2_ref, rb_ref, eb_ref, qb_ref,
    q_in, m_in, r_in, e_in, q_wide, m_wide, r_wide, e_wide, in_mid, bo_mid, read, write,
):
    enter = (
        pltpu.make_async_copy(in_hbm, in_mid, read.at[12]),
        pltpu.make_async_copy(bo_hbm, bo_mid, read.at[13]),
    )
    leave = (
        pltpu.make_async_copy(in_mid, in_out, write.at[0]),
        pltpu.make_async_copy(bo_mid, bo_out, write.at[1]),
    )
    quarter = r_in.shape[0] // 4
    jobs = []
    for c in range(4):
        at = pl.ds(c * quarter, quarter)
        for src, mid, wide, dst in ((r_hbm, r_in, r_wide, r_out), (e_hbm, e_in, e_wide, e_out)):
            jobs.append((src.at[at], mid.at[at], wide.at[at], dst.at[at]))
    for k in range(3):
        jobs.append((q_hbm.at[k], q_in.at[k], q_wide.at[k], q_out.at[k]))
    gets = [pltpu.make_async_copy(job[0], job[1], read.at[k]) for k, job in enumerate(jobs)]
    get_m = pltpu.make_async_copy(m_hbm, m_in, read.at[len(jobs)])
    get_m.start()
    for copy in enter:
        copy.start()
    for get in gets:
        get.start()
    for k, ref in enumerate((g1_ref, s1_ref, mb_ref, g2_ref, s2_ref, rb_ref, eb_ref)):
        ref[...] = small_ref[k : k + 1, :]
    cols = qb_ref.shape[1]
    for k in range(2):
        qb_ref[k : k + 1, :] = small_ref[7:8, k * cols : (k + 1) * cols]
    for k in range(2):
        enter[k].wait()
        leave[k].start()
    get_m.wait()
    m_wide[...] = m_in[...].astype(F32).T
    puts = [pltpu.make_async_copy(m_wide, m_out, write.at[2])]
    puts[0].start()
    for k, (_src, mid, wide, dst) in enumerate(jobs):
        gets[k].wait()
        step = 64

        @pl.loop(0, mid.shape[0] // step)
        def _(r):
            at = pl.ds(pl.multiple_of(r * step, step), step)
            wide[at] = mid[at].astype(F32)

        put = pltpu.make_async_copy(wide, dst, write.at[3 + k])
        put.start()
        puts.append(put)
    for copy in leave:
        copy.wait()
    for put in puts:
        put.wait()


def finish(q, m, r, e, in_grad, block_out, small):
    vmem = pl.BlockSpec(memory_space=pltpu.VMEM)
    anyspace = pl.BlockSpec(memory_space=pl.ANY)
    width = small.shape[1]
    row = jax.ShapeDtypeStruct((1, width), F32)
    return pl.pallas_call(
        finish_kernel,
        in_specs=[anyspace] * 6 + [vmem],
        out_specs=[anyspace] * 6 + [vmem] * 8,
        out_shape=[
            jax.ShapeDtypeStruct(block_out.shape, BF),
            jax.ShapeDtypeStruct(in_grad.shape, F32),
            jax.ShapeDtypeStruct(q.shape, F32),
            jax.ShapeDtypeStruct(m.shape[::-1], F32),
            jax.ShapeDtypeStruct(r.shape, F32),
            jax.ShapeDtypeStruct(e.shape, F32),
        ]
        + [row] * 7
        + [jax.ShapeDtypeStruct((2, q.shape[2]), F32)],
        scratch_shapes=[
            pltpu.VMEM(q.shape, BF),
            pltpu.VMEM(m.shape, BF),
            pltpu.VMEM(r.shape, BF),
            pltpu.VMEM(e.shape, BF),
            pltpu.VMEM(q.shape, F32),
            pltpu.VMEM(m.shape[::-1], F32),
            pltpu.VMEM(r.shape, F32),
            pltpu.VMEM(e.shape, F32),
            pltpu.VMEM(in_grad.shape, F32),
            pltpu.VMEM(block_out.shape, BF),
            pltpu.SemaphoreType.DMA((14,)),
            pltpu.SemaphoreType.DMA((14,)),
        ],
        compiler_params=pltpu.CompilerParams(vmem_limit_bytes=60 << 20),
        name="finish",
    )(q, m, r, e, in_grad, block_out, small)


def body(
    block_in,
    segments,
    first_gain,
    first_shift,
    w_qkv,
    qv_bias,
    w_mix,
    mix_bias,
    second_gain,
    second_shift,
    w_expand,
    expand_bias,
    w_reduce,
    reduce_bias,
    out_grad,
):
    width = block_in.shape[1]
    cols = w_qkv.shape[2]
    units = w_expand.shape[1]
    dp_size = lax.axis_size("dp")
    flat = (1, width)
    wq = w_qkv.transpose(1, 0, 2)
    rows1, qkv, att, resid, n2, wq_far, wm_far, og_all = forward(
        block_in,
        segments,
        first_gain.reshape(flat),
        first_shift.reshape(flat),
        qv_bias,
        mix_bias.reshape(flat),
        second_gain.reshape(flat),
        second_shift.reshape(flat),
        wq,
        w_mix,
        out_grad,
        dp_size,
    )
    resid_grad, mg_all, reduce_grad, expand_grad, br_near, br_far, unit_sums, sums2, carry = ff(
        n2, og_all, w_expand, w_reduce, expand_bias.reshape(1, units), resid, second_gain.reshape(flat), dp_size
    )
    in_grad, qkv_grad, mix_grad, reduce_all, expand_all, small, block_out = backward(
        mg_all,
        qkv,
        att,
        rows1,
        wq,
        wq_far,
        w_mix,
        wm_far,
        block_in,
        resid_grad,
        reduce_grad,
        expand_grad,
        carry,
        resid,
        br_near,
        br_far,
        segments,
        first_gain.reshape(flat),
        sums2,
        unit_sums,
        reduce_bias.reshape(flat),
        dp_size,
    )
    block_out, in_grad, qkv_grad, mix_grad, reduce_all, expand_all, *rest, qv_bias_grad = finish(
        qkv_grad, mix_grad, reduce_all, expand_all, in_grad, block_out, small
    )
    g1, s1, mb, g2, s2, rb, eb = (item.reshape(-1) for item in rest)
    return (
        block_out,
        in_grad,
        g1,
        s1,
        qkv_grad.transpose(1, 0, 2),
        qv_bias_grad,
        mix_grad,
        mb,
        g2,
        s2,
        expand_all,
        eb,
        reduce_all,
        rb,
    )


def solution(mesh):
    both = P(("dp", "tensor"), None)
    return jax.shard_map(
        body,
        mesh=mesh,
        in_specs=(
            both,
            P("dp", None),
            P(),
            P(),
            P(None, None, "tensor"),
            P(None, "tensor"),
            P("tensor", None),
            P(),
            P(),
            P(),
            P(None, "tensor"),
            P("tensor"),
            P("tensor", None),
            P(),
            both,
        ),
        out_specs=(
            both,
            both,
            P(),
            P(),
            P(None, None, "tensor"),
            P(None, "tensor"),
            P("tensor", None),
            P(),
            P(),
            P(),
            P(None, "tensor"),
            P("tensor"),
            P("tensor", None),
            P(),
        ),
        check_vma=False,
    )
```

```python
import functools

import jax
import jax.numpy as jnp
from jax import lax
from jax.experimental import pallas as pl
from jax.experimental.pallas import tpu as pltpu
from jax.sharding import PartitionSpec as P

HD = 64
PAIR = 2 * HD
QB = 256
EPS = 1e-5
BF = jnp.bfloat16
F32 = jnp.float32
SCALE = HD ** (-0.5)
MESH_ID = pl.DeviceIdType.MESH
AHEAD = 3
NT = (((1,), (1,)), ((), ()))
TN = (((0,), (0,)), ((), ()))


def dot(a, b, dims=(((1,), (0,)), ((), ()))):
    return lax.dot_general(a, b, dims, preferred_element_type=F32)


def norm_stats(values):
    mean = jnp.mean(values, axis=-1, keepdims=True)
    centered = values - mean
    variance = jnp.mean(centered * centered, axis=-1, keepdims=True)
    scale = lax.rsqrt(variance + EPS)
    return centered * scale, scale


def fill_bias(seg_ref, row, bias_ref, blocks):
    segr = seg_ref[pl.ds(row, 1), :].astype(F32)
    segc = jnp.broadcast_to(segr, (8, segr.shape[1])).T[:, 0:1]
    off = 0
    for i in range(blocks):
        keys = (i + 1) * QB
        kpos = lax.broadcasted_iota(jnp.int32, (keys, QB), 0)
        qpos = lax.broadcasted_iota(jnp.int32, (keys, QB), 1) + i * QB
        same = segc[:keys, :] == segr[:, i * QB : (i + 1) * QB]
        allowed = jnp.logical_and(kpos <= qpos, same)
        bias_ref[off : off + keys, :] = jnp.where(allowed, 0.0, -1e30)
        off += keys


def half_masks():
    lane = lax.broadcasted_iota(jnp.int32, (1, PAIR), 1)
    return (lane < HD, lane >= HD)


def ring_index(at, n):
    at = (at + 2 * n) % n
    far = at // (n // 2)
    return (1 - far) * 2 * at + far * (2 * (n - 1 - at) + 1)


def ring_place(n):
    mine = lax.axis_index("dp")
    odd = mine % 2
    pos = (1 - odd) * (mine // 2) + odd * (n - 1 - mine // 2)
    return mine, pos, (ring_index(pos + 1, n), ring_index(pos - 1, n))


def meet(tensor_peers, dp_peers):
    barrier = pltpu.get_barrier_semaphore()
    for other in tensor_peers:
        pl.semaphore_signal(barrier, inc=1, device_id={"tensor": other}, device_id_type=MESH_ID)
    for other in dp_peers:
        pl.semaphore_signal(barrier, inc=1, device_id={"dp": other}, device_id_type=MESH_ID)
    pl.semaphore_wait(barrier, len(tensor_peers) + len(dp_peers))


def both_heads(a, masks):
    zero = jnp.zeros_like(a)
    return jnp.concatenate([jnp.where(masks[0], a, zero), jnp.where(masks[1], a, zero)], axis=0)


def twice(a):
    return jnp.concatenate([a, a], axis=1)


def fwd_kernel(
    n,
    x_ref, seg_ref, g1_ref, s1_ref, bq_ref, mixb_ref, g2_ref, s2_ref, wq_hbm, wm_hbm, og_ref,
    rows1_out, qkv_out, att_out, resid_out, n2_out, wqf_out, wmf_out, oga_ref,
    rows1_ref, qkv_ref, att_ref, resid_ref, n2_ref, w_all, wm_all,
    b_all, bqf, bias_ref, psend, pgot, send, recv, ring_send, ring_recv, local, out,
):
    rows, width = x_ref.shape
    seq = rows1_ref.shape[0]
    cols = w_all.shape[3]
    wqf_ref = w_all.at[1]
    wmf_ref = wm_all.at[1]
    cols3 = 3 * cols
    half = rows // 2
    blocks = seq // QB
    me = lax.axis_index("tensor")
    core = me % 2
    sib = me + 1 - 2 * core
    far = (me + 2) % 4
    mine, pos, sides = ring_place(n)
    meet((sib, far), sides)

    def remote(src, dst, k, other):
        return pltpu.make_async_remote_copy(
            src_ref=src,
            dst_ref=dst,
            send_sem=send.at[k],
            recv_sem=recv.at[k],
            device_id={"tensor": other},
            device_id_type=MESH_ID,
        )

    slab = width // n
    wide = cols // 2

    def slab_rows(chunk):
        return pl.ds(pl.multiple_of(chunk * slab, slab), slab)

    mix_slab = wm_hbm.shape[0] // n
    around = mix_slab % 16 == 0
    streams = 4 if around else 3

    def mix_rows(chunk):
        return pl.ds(pl.multiple_of(chunk * mix_slab, mix_slab), mix_slab)

    def piece():
        return remote(wq_hbm.at[:, slab_rows(mine)], wqf_ref.at[:, slab_rows(mine)], 0, far)

    def bias_across():
        return remote(bq_ref, bqf, 1, far)

    def own_half(c):
        return pl.ds(pl.multiple_of(core * rows + c * half, half), half)

    def rows_beside(c):
        return remote(rows1_ref.at[own_half(c)], rows1_ref.at[own_half(c)], 2 + c, sib)

    def mix_across():
        if around:
            return remote(wm_hbm.at[mix_rows(mine)], wmf_ref.at[mix_rows(mine)], 4, far)
        return remote(wm_hbm, wmf_ref, 4, far)

    def og_across(c):
        return remote(
            og_ref.at[pl.ds(c * half, half)], oga_ref.at[pl.ds((2 + c) * rows, half)], 5 + c, far
        )

    def og_beside():
        return remote(og_ref, oga_ref.at[pl.ds(rows, rows)], 7, sib)

    def og_forward(c):
        return remote(
            oga_ref.at[pl.ds((2 + c) * rows, half)],
            oga_ref.at[pl.ds((2 + c) * rows + half, half)],
            8 + c,
            sib,
        )

    def part_beside():
        return remote(psend, pgot, 10, sib)

    def og_own():
        return pltpu.make_async_copy(og_ref, oga_ref.at[pl.ds(0, rows)], local.at[0])

    reach = n // 2

    def hop(k, d, s, part=False):
        chunk = ring_index(pos - s if d == 0 else pos + s, n)
        side = width // 2 if k == 3 else wide
        lanes = slice(d * side, (d + 1) * side) if part else slice(None)
        ref = wmf_ref.at[mix_rows(chunk), lanes] if k == 3 else wqf_ref.at[k, slab_rows(chunk), lanes]
        return pltpu.make_async_remote_copy(
            src_ref=ref,
            dst_ref=ref,
            send_sem=ring_send.at[k, d],
            recv_sem=ring_recv.at[k, d, s],
            device_id={"dp": sides[d]},
            device_id_type=MESH_ID,
        )

    def tick(s):
        for k in range(streams):
            for d in range(2):
                hop(k, d, s).wait()

                @pl.when(s < reach - 2)
                def _():
                    hop(k, d, s + 1).start()

                @pl.when(s == reach - 2)
                def _():
                    hop(k, d, s + 1, True).start()

    def last_tick():
        for k in range(3):
            for d in range(2):
                hop(k, d, reach - 1, True).wait()

    def put(k):
        near = pl.ds(0, cols3)
        far_part = pl.ds(cols3, cols3)
        low, high = pl.ds(0, half), pl.ds(half, half)
        src, dst = (
            (rows1_ref, rows1_out),
            (qkv_ref.at[:, near], qkv_out.at[:, near]),
            (qkv_ref.at[:, far_part], qkv_out.at[:, far_part]),
            (wqf_ref, wqf_out),
            (wmf_ref, wmf_out),
            (att_ref, att_out),
            (resid_ref.at[low], resid_out.at[low]),
            (resid_ref.at[high], resid_out.at[high]),
            (n2_ref.at[low], n2_out.at[low]),
            (n2_ref.at[high], n2_out.at[high]),
        )[k]
        return pltpu.make_async_copy(src, dst, out.at[k])

    piece().start()
    if around:
        mix_across().start()
    bias_across().start()
    loads = (
        pltpu.make_async_copy(wq_hbm, w_all.at[0], local.at[1]),
        pltpu.make_async_copy(wm_hbm, wm_all.at[0], local.at[2]),
    )
    for load in loads:
        load.start()
    step = 128
    for c in range(2):

        @pl.loop(0, half // step)
        def _(r):
            normed = norm_stats(x_ref[pl.ds(pl.multiple_of(c * half + r * step, step), step), :].astype(F32))[0]
            to = pl.ds(pl.multiple_of(core * rows + c * half + r * step, step), step)
            rows1_ref[to, :] = (normed * g1_ref[...] + s1_ref[...]).astype(BF)

        rows_beside(c).start()
    piece().wait()
    for k in range(3):
        for d in range(2):
            hop(k, d, 0).start()
    if around:
        mix_across().wait()
        for d in range(2):
            hop(3, d, 0).start()
    else:
        mix_across().start()
    for c in range(2):
        og_across(c).start()
    og_beside().start()
    og_own().start()
    fill_bias(seg_ref, me // 2, bias_ref, blocks)

    def fill_shift(g, ref):
        b_all[g, 0:1] = ref[0:1]
        b_all[g, 1:2] = jnp.zeros_like(ref[0:1])
        b_all[g, 2:3] = ref[1:2]

    fill_shift(0, bq_ref)
    for c in range(2):
        rows_beside(c).wait()
    for load in loads:
        load.wait()
    put(0).start()
    masks = half_masks()
    pairs = cols // PAIR
    ticks = 1 + pairs

    @pl.loop(0, 2 * pairs)
    def _(p):
        group = p // pairs

        @pl.when(p == pairs)
        def _():
            @pl.loop(ticks, reach - 1)
            def _(s):
                tick(s)

            last_tick()
            bias_across().wait()
            fill_shift(1, bqf)
            put(3).start()

        @pl.when(p % pairs == 0)
        def _():
            @pl.loop(0, 3)
            def _(k):
                to = pl.ds(pl.multiple_of(group * cols3 + k * cols, cols), cols)
                part = dot(rows1_ref[...], w_all[group, k]) + b_all[group, pl.ds(k, 1)]
                qkv_ref[:, to] = part.astype(BF)

        @pl.when(p == 0)
        def _():
            put(1).start()
            tick(0)

        @pl.when(p == pairs)
        def _():
            put(2).start()

        base = group * cols3 + (p % pairs) * PAIR

        def lanes(k):
            return pl.ds(pl.multiple_of(base + k * cols, PAIR), PAIR)

        vt = qkv_ref[:, lanes(2)].T
        off = 0
        for i in range(blocks):
            keys = (i + 1) * QB
            at = slice(i * QB, (i + 1) * QB)
            qi = qkv_ref[at, lanes(0)] * jnp.asarray(SCALE, BF)
            kk = qkv_ref[:keys, lanes(1)]
            s = dot(kk, both_heads(qi, masks), NT) + twice(bias_ref[off : off + keys, :])
            e = jnp.exp(s - jnp.max(s, axis=0, keepdims=True))
            inverse = 1.0 / jnp.sum(e, axis=0, keepdims=True)
            e = e.astype(BF)
            outs = []
            for h in range(2):
                side = slice(h * QB, (h + 1) * QB)
                outs.append(dot(vt[h * HD : (h + 1) * HD, :keys], e[:, side]) * inverse[:, side])
            att_ref[at, pl.ds(pl.multiple_of(p * PAIR, PAIR), PAIR)] = jnp.concatenate(outs, axis=0).T.astype(BF)
            off += keys
            if i == blocks - 1:

                @pl.when(p < pairs)
                def _():
                    tick(1 + p)

    if around:
        for d in range(2):
            hop(3, d, reach - 1, True).wait()
    else:
        mix_across().wait()
    put(4).start()
    put(5).start()
    nb = 256

    def mixed(start, at):
        sel = pl.ds(pl.multiple_of(start, rows), rows)
        total = dot(att_ref[sel, 0:cols], wm_all[0, :, at])
        return total + dot(att_ref[sel, cols : 2 * cols], wm_all[1, :, at])

    @pl.loop(0, width // nb)
    def _(k):
        at = pl.ds(pl.multiple_of(k * nb, nb), nb)
        psend[:, at] = mixed((1 - core) * rows, at).astype(BF)

    part_beside().start()

    @pl.loop(0, width // nb)
    def _(k):
        at = pl.ds(pl.multiple_of(k * nb, nb), nb)
        resid_ref[:, at] = x_ref[:, at].astype(F32) + mixed(core * rows, at) + mixb_ref[:, at]

    for c in range(2):
        og_across(c).wait()
        og_forward(c).start()
    part_beside().wait()

    for c in range(2):

        @pl.loop(0, half // step)
        def _(r):
            at = pl.ds(pl.multiple_of(c * half + r * step, step), step)
            full = resid_ref[at, :] + pgot[at, :].astype(F32)
            resid_ref[at, :] = full
            n2_ref[at, :] = (norm_stats(full)[0] * g2_ref[...] + s2_ref[...]).astype(BF)

        put(6 + c).start()
        put(8 + c).start()

    for k in range(10):
        put(k).wait()
    og_own().wait()
    og_beside().wait()
    for c in range(2):
        og_forward(c).wait()


def forward(x, segments, g1, s1, bq, mixb, g2, s2, wq, wm, og, n):
    rows, width = x.shape
    seq = segments.shape[1]
    cols = wq.shape[2]
    blocks = seq // QB
    vmem = pl.BlockSpec(memory_space=pltpu.VMEM)
    anyspace = pl.BlockSpec(memory_space=pl.ANY)
    return pl.pallas_call(
        functools.partial(fwd_kernel, n),
        in_specs=[vmem] * 8 + [anyspace] * 3,
        out_specs=[anyspace] * 8,
        out_shape=[
            jax.ShapeDtypeStruct((seq, width), BF),
            jax.ShapeDtypeStruct((seq, 6 * cols), BF),
            jax.ShapeDtypeStruct((seq, 2 * cols), BF),
            jax.ShapeDtypeStruct((rows, width), F32),
            jax.ShapeDtypeStruct((rows, width), BF),
            jax.ShapeDtypeStruct(wq.shape, BF),
            jax.ShapeDtypeStruct(wm.shape, BF),
            jax.ShapeDtypeStruct((4 * rows, width), BF),
        ],
        scratch_shapes=[
            pltpu.VMEM((seq, width), BF),
            pltpu.VMEM((seq, 6 * cols), BF),
            pltpu.VMEM((seq, 2 * cols), BF),
            pltpu.VMEM((rows, width), F32),
            pltpu.VMEM((rows, width), BF),
            pltpu.VMEM((2,) + wq.shape, BF),
            pltpu.VMEM((2,) + wm.shape, BF),
            pltpu.VMEM((2, 3, cols), F32),
            pltpu.VMEM((2, cols), F32),
            pltpu.VMEM((QB * blocks * (blocks + 1) // 2, QB), F32),
            pltpu.VMEM((rows, width), BF),
            pltpu.VMEM((rows, width), BF),
            pltpu.SemaphoreType.DMA((11,)),
            pltpu.SemaphoreType.DMA((11,)),
            pltpu.SemaphoreType.DMA((4, 2)),
            pltpu.SemaphoreType.DMA((4, 2, n // 2)),
            pltpu.SemaphoreType.DMA((3,)),
            pltpu.SemaphoreType.DMA((10,)),
        ],
        compiler_params=pltpu.CompilerParams(
            collective_id=3, has_side_effects=True, vmem_limit_bytes=56 << 20
        ),
        name="forward",
    )(x, segments, g1, s1, bq, mixb, g2, s2, wq, wm, og)


def ring_part(
    n, between, g_ref, norm_ref, qsum_ref, dsum_ref, usum_ref, rbias_ref, resid_hbm, brn_hbm, brf_hbm,
    qo_ref, mo_ref, ro_ref, eo_ref, so_ref, bo_ref,
    buf, rows8, small_ref, sbuf, sall, speer, ssum, resid, brn, bro,
    send, recv, fsend, frecv, ssend, srecv, tsend, trecv, local,
):
    mine, pos, sides = ring_place(n)
    me = lax.axis_index("tensor")
    far = (me + 2) % 4
    peers = [(me + k) % 4 for k in range(1, 4)]
    loads = (
        pltpu.make_async_copy(resid_hbm, resid, local.at[0]),
        pltpu.make_async_copy(brn_hbm, brn, local.at[1]),
    )
    for load in loads:
        load.start()

    cols = qsum_ref.shape[1]
    piece = small_ref.shape[2]
    per = rows8.shape[1] // piece
    rows8[0:2] = norm_ref[...]
    rows8[2:6] = dsum_ref[...]
    rows8[6:7] = usum_ref[...]
    rows8[7:8] = jnp.zeros_like(rows8[7:8])
    for k in range(2):
        rows8[7:8, k * cols : (k + 1) * cols] = qsum_ref[k : k + 1, :]

    def in_row(c):
        return slice(c // per, c // per + 1), slice(c % per * piece, (c % per + 1) * piece)

    for c in range(n):
        small_ref[c] = rows8[in_row(c)]

    def remote(src, dst, kind, d, s):
        return pltpu.make_async_remote_copy(
            src_ref=src,
            dst_ref=dst,
            send_sem=send.at[kind, d],
            recv_sem=recv.at[kind, d, s],
            device_id={"dp": sides[d]},
            device_id_type=MESH_ID,
        )

    def little(src, dst, kind, s):
        return pltpu.make_async_remote_copy(
            src_ref=src,
            dst_ref=dst,
            send_sem=ssend.at[kind],
            recv_sem=srecv.at[kind, s],
            device_id={"dp": sides[0]},
            device_id_type=MESH_ID,
        )

    def beside(src, dst, k, other):
        return pltpu.make_async_remote_copy(
            src_ref=src,
            dst_ref=dst,
            send_sem=tsend.at[k],
            recv_sem=trecv.at[k],
            device_id={"tensor": other},
            device_id_type=MESH_ID,
        )

    def share(k):
        return beside(small_ref, speer.at[k], k, peers[k])

    def branch():
        return beside(brf_hbm, bro, 3, far)

    def part(d, s):
        return ring_index(pos - 1 - s if d == 0 else pos + 1 + s, n)

    def held(d, s):
        return ring_index(pos - s if d == 0 else pos + s, n)

    streams = [(k, d) for k in range(4) for d in range(2)]

    def source(k, chunk, d):
        return g_ref.at[k, chunk, d]

    def slot(k, s, d):
        return buf.at[s, d, k]

    def put_at(k, chunk, d):
        return qo_ref.at[k, chunk, d] if k < 3 else mo_ref.at[chunk, d]

    def add(k, d, s):
        ref = slot(k, s, d)
        total = ref[...].astype(F32) + source(k, part(d, s + 1), d)[...].astype(F32)
        ref[...] = total.astype(BF)

    def gather(k, d, s):
        ref = put_at(k, held(d, s), d)
        return remote(ref, ref, 4 + k, d, s)

    left = n - 1 - AHEAD
    half = ro_ref.shape[3] // 2

    def ff_hop(kind, c, d, s):
        ref = (ro_ref, eo_ref)[kind].at[held(d, s), d, :, pl.ds(c * half, half)]
        k = 2 * kind + c
        return pltpu.make_async_remote_copy(
            src_ref=ref,
            dst_ref=ref,
            send_sem=fsend.at[k, d],
            recv_sem=frecv.at[k, d, s - AHEAD],
            device_id={"dp": sides[d]},
            device_id_type=MESH_ID,
        )

    def beside_step(kind, s, act):
        @pl.when(s < left)
        def _():
            for d in range(2):
                act(ff_hop(kind, 0, d, AHEAD + s))

        @pl.when(s >= n - 1 - left)
        def _():
            for d in range(2):
                act(ff_hop(kind, 1, d, AHEAD + s - (n - 1 - left)))

    def start(copy):
        copy.start()

    def finish(copy):
        copy.wait()

    def gather_small(s):
        ref = sall.at[held(0, s)]
        return little(ref, ref, 1, s)

    for k, d in streams:
        remote(source(k, part(d, 0), d), slot(k, 0, d), k, d, 0).start()
    for k in range(3):
        share(k).start()
    branch().start()
    between()
    for k in range(3):
        share(k).wait()
    ssum[...] = small_ref[...]
    shared = n * 6 // 8
    ssum[0:shared] = ssum[0:shared] + speer[0, 0:shared] + speer[1, 0:shared] + speer[2, 0:shared]
    little(ssum.at[part(0, 0)], sbuf.at[0], 0, 0).start()

    @pl.loop(0, n - 2)
    def _(s):
        beside_step(0, s, start)
        for k, d in streams:
            remote(slot(k, s, d), slot(k, s, d), k, d, s).wait()
            add(k, d, s)
            remote(slot(k, s, d), slot(k, s + 1, d), k, d, s + 1).start()
        little(sbuf.at[s], sbuf.at[s], 0, s).wait()
        sbuf[s] = sbuf[s] + ssum[part(0, s + 1)]
        little(sbuf.at[s], sbuf.at[s + 1], 0, s + 1).start()
        beside_step(0, s, finish)

    last = n - 2
    beside_step(0, last, start)
    puts = []
    for k, d in streams:
        remote(slot(k, last, d), slot(k, last, d), k, d, last).wait()
        add(k, d, last)
        put = pltpu.make_async_copy(slot(k, last, d), put_at(k, mine, d), local.at[2 + 2 * k + d])
        put.start()
        puts.append(put)
    for (k, d), put in zip(streams, puts):
        put.wait()
        gather(k, d, 0).start()
    little(sbuf.at[last], sbuf.at[last], 0, last).wait()
    sall[mine] = sbuf[last] + ssum[mine]
    gather_small(0).start()
    beside_step(0, last, finish)

    @pl.loop(0, n - 2)
    def _(s):
        beside_step(1, s, start)
        for k, d in streams:
            gather(k, d, s).wait()
            gather(k, d, s + 1).start()
        gather_small(s).wait()
        gather_small(s + 1).start()
        beside_step(1, s, finish)

    beside_step(1, last, start)

    branch().wait()
    for load in loads:
        load.wait()
    step = 128

    @pl.loop(0, bo_ref.shape[0] // step)
    def _(r):
        at = pl.ds(pl.multiple_of(r * step, step), step)
        total = resid[at, :] + brn[at, :].astype(F32) + bro[at, :].astype(F32) + rbias_ref[...]
        bo_ref[at, :] = total.astype(BF)

    for k, d in streams:
        gather(k, d, last).wait()
    gather_small(last).wait()
    for c in range(n):
        so_ref[in_row(c)] = sall[c]
    beside_step(1, last, finish)


def bwd_kernel(
    n,
    mg_hbm, qkv_hbm, att_hbm, rows1_hbm, wq_hbm, wqf_hbm, wm_hbm, wmf_hbm, x_hbm, rgrad_hbm, rg_hbm, eg_hbm, carry_hbm,
    resid_hbm, brn_hbm, brf_hbm, seg_ref, g1_ref, dsum_ref, usum_ref, rbias_ref,
    in_out, qo_ref, mo_ref, ro_ref, eo_ref, so_ref, bo_ref,
    in_ref, qg_ref, qsum_ref, nsum_ref,
    mg, qkv, att, rows1, wq, wqf, wm, wmf, x, rgrad, ffg,
    rbuf, dqkv, ag, bias_ref, dk_ref, dv_ref, q_send, q_got, m_send, m_got, s_got, s_send, psend, pgot, n1g,
    send, recv, ring_send, ring_recv, gather_send, gather_recv, local, out,
    *ring_scratch,
):
    rows, width = in_ref.shape
    seq = mg.shape[0]
    cols = wq.shape[2]
    cols3 = 3 * cols
    pairs = cols // PAIR
    blocks = seq // QB
    me = lax.axis_index("tensor")
    core = me % 2
    sib = me + 1 - 2 * core
    far = (me + 2) % 4
    mine, pos, sides = ring_place(n)

    pairs_in = (
        (mg_hbm, mg), (wmf_hbm, wmf), (att_hbm, att), (qkv_hbm, qkv), (rg_hbm, ffg.at[0]), (eg_hbm, ffg.at[1]),
        (rows1_hbm, rows1), (wm_hbm, wm), (wqf_hbm, wqf), (wq_hbm, wq), (x_hbm, x), (rgrad_hbm, rgrad),
    )

    def load(k):
        return pltpu.make_async_copy(pairs_in[k][0], pairs_in[k][1], local.at[k])

    for k in range(len(pairs_in)):
        load(k).start()
    meet([(me + k) % 4 for k in range(1, 4)], sides)

    def remote(src, dst, k, other):
        return pltpu.make_async_remote_copy(
            src_ref=src,
            dst_ref=dst,
            send_sem=send.at[k],
            recv_sem=recv.at[k],
            device_id={"tensor": other},
            device_id_type=MESH_ID,
        )

    def q_across(k):
        return remote(q_send.at[k], q_got.at[k], k, far)

    def m_across():
        return remote(m_send, m_got, 3, far)

    def s_across():
        return remote(s_send, s_got, 4, far)

    def part_beside():
        return remote(psend, pgot, 5, sib)

    def ring_copy(src, kind, d, s):
        return pltpu.make_async_remote_copy(
            src_ref=src,
            dst_ref=rbuf.at[s, kind, d],
            send_sem=ring_send.at[kind, d],
            recv_sem=ring_recv.at[kind, d, s],
            device_id={"dp": sides[d]},
            device_id_type=MESH_ID,
        )

    def part(d, s):
        return ring_index(pos - 1 - s if d == 0 else pos + 1 + s, n)

    def tick(kind, s):
        for d in range(2):
            ring_copy(rbuf.at[s, kind, d], kind, d, s).wait()
            mixed = rbuf[s, kind, d].astype(F32) + ffg[kind, part(d, s + 1), d].astype(F32)
            rbuf[s, kind, d] = mixed.astype(BF)

            @pl.when(s < n - 2)
            def _():
                ring_copy(rbuf.at[s, kind, d], kind, d, s + 1).start()

    outs_hbm = (ro_ref, eo_ref)

    def put_in():
        return pltpu.make_async_copy(in_ref, in_out, out.at[0])

    def gather(kind, d, s):
        chunk = ring_index(pos - s if d == 0 else pos + s, n)
        ref = outs_hbm[kind].at[chunk, d]
        return pltpu.make_async_remote_copy(
            src_ref=ref,
            dst_ref=ref,
            send_sem=gather_send.at[kind, d],
            recv_sem=gather_recv.at[kind, d, s],
            device_id={"dp": sides[d]},
            device_id_type=MESH_ID,
        )

    def gather_tick(kind, s):
        for d in range(2):
            gather(kind, d, s).wait()

            @pl.when(s + 1 < AHEAD)
            def _():
                gather(kind, d, s + 1).start()

    def gather_begin():
        owns = [
            pltpu.make_async_copy(rbuf.at[n - 2, kind], outs_hbm[kind].at[mine], local.at[12 + kind])
            for kind in range(2)
        ]
        for item in owns:
            item.start()
        for kind in range(2):
            owns[kind].wait()
            for d in range(2):
                gather(kind, d, 0).start()

    for kind in range(2):
        for d in range(2):
            ring_copy(carry_hbm.at[kind, d], kind, d, 2 - kind).start()

    fill_bias(seg_ref, me // 2, bias_ref, blocks)
    masks = half_masks()
    for k in range(6):
        load(k).wait()
    m_send[...] = dot(mg[...], att[:, cols : 2 * cols], TN).astype(BF)
    m_across().start()
    ag[...] = dot(mg[...], wmf[...], NT).astype(BF)

    turns = 2 * pairs + blocks * pairs
    hops = [(kind, s) for s in range(AHEAD) for kind in range(2)]

    def next_hop():
        if hops:
            gather_tick(*hops.pop(0))

    @pl.loop(0, 2 * pairs)
    def _(q):
        first = q < pairs
        group = 1 - q // pairs
        slot = q % pairs
        base = group * cols3 + slot * PAIR

        @pl.when(q == pairs)
        def _():
            ag[...] = dot(mg[...], wm[...], NT).astype(BF)

        def lanes(k):
            return pl.ds(pl.multiple_of(base + k * cols, PAIR), PAIR)

        own = pl.ds(pl.multiple_of(slot * PAIR, PAIR), PAIR)
        kt = qkv[:, lanes(1)].T
        dk_ref[...] = jnp.zeros_like(dk_ref)
        dv_ref[...] = jnp.zeros_like(dv_ref)
        off = 0
        qsum = jnp.zeros((1, PAIR), F32)
        for i in range(blocks):
            keys = (i + 1) * QB
            at = slice(i * QB, (i + 1) * QB)
            qi = qkv[at, lanes(0)] * jnp.asarray(SCALE, BF)
            gi = ag[at, own]
            kk = qkv[:keys, lanes(1)]
            vv = qkv[:keys, lanes(2)]
            q2 = both_heads(qi, masks)
            g2 = both_heads(gi, masks)
            s = dot(kk, q2, NT) + twice(bias_ref[off : off + keys, :])
            e = jnp.exp(s - jnp.max(s, axis=0, keepdims=True))
            prob = e * (1.0 / jnp.sum(e, axis=0, keepdims=True))
            weighted = prob * dot(vv, g2, NT)
            ds = (weighted - prob * jnp.sum(weighted, axis=0, keepdims=True)).astype(BF)
            dv_ref[:keys, :] += dot(prob.astype(BF), g2)
            dk_ref[:keys, :] += dot(ds, q2)
            outs = []
            for h in range(2):
                outs.append(dot(kt[h * HD : (h + 1) * HD, :keys], ds[:, h * QB : (h + 1) * QB]))
            dq = (jnp.concatenate(outs, axis=0).T * SCALE).astype(BF)
            dqkv[at, lanes(0)] = dq
            qsum += jnp.sum(dq.astype(F32), axis=0, keepdims=True)
            off += keys
            late = 2 * pairs + blocks * (q - pairs) + i

            @pl.when(jnp.logical_and(q >= pairs, late < 2 * (n - 2) - 1))
            def _():
                tick(1 - i % 2, 1 + i % 2 + late // 2)

            if i % 2 == 1:

                @pl.when(first)
                def _():
                    tick(1 - i // 2, 1 + i // 2 + q)

        dv = dv_ref[...].astype(BF)
        dqkv[:, lanes(1)] = dk_ref[...].astype(BF)
        dqkv[:, lanes(2)] = dv
        vsum = jnp.sum(dv.astype(F32), axis=0, keepdims=True)
        for (name, sel) in ((s_send, first), (qsum_ref, jnp.logical_not(first))):

            @pl.when(sel)
            def _():
                name[0:1, own] = qsum
                name[1:2, own] = vsum

        @pl.when(q == pairs - 1)
        def _():
            s_across().start()
            load(6).wait()
            load(7).wait()

            @pl.loop(0, 3)
            def _(k):
                to = pl.ds(pl.multiple_of(cols3 + k * cols, cols), cols)
                q_send[k] = dot(rows1[...], dqkv[:, to], TN).astype(BF)
                q_across(k).start()

    if n - 2 > turns // 2:
        tick(1, 1 + turns // 2)

        @pl.loop(2 + turns // 2, n - 1)
        def _(s):
            for kind in range(2):
                tick(kind, s)

    gather_begin()
    for k in (8, 9):
        load(k).wait()
    nb = 256

    def back(start, at):
        sel = pl.ds(pl.multiple_of(start, rows), rows)
        total = dot(dqkv[sel, 0:cols], wq[0, at, :], NT)
        for k in range(1, 6):
            w = wq if k < 3 else wqf
            total += dot(dqkv[sel, k * cols : (k + 1) * cols], w[k % 3, at, :], NT)
        return total

    @pl.loop(0, width // nb)
    def _(k):
        at = pl.ds(pl.multiple_of(k * nb, nb), nb)
        psend[:, at] = back((1 - core) * rows, at).astype(BF)

    part_beside().start()
    next_hop()

    @pl.loop(0, width // nb)
    def _(k):
        at = pl.ds(pl.multiple_of(k * nb, nb), nb)
        n1g[:, at] = back(core * rows, at)

    next_hop()
    part_beside().wait()
    load(10).wait()
    load(11).wait()
    nsum_ref[...] = jnp.zeros_like(nsum_ref)
    step = 128

    @pl.loop(0, rows // step)
    def _(r):
        at = pl.ds(pl.multiple_of(r * step, step), step)
        grad = n1g[at, :] + pgot[at, :].astype(F32)
        normed, scale = norm_stats(x[at, :].astype(F32))
        g = grad * g1_ref[...]
        mean_g = jnp.mean(g, axis=-1, keepdims=True)
        mean_gn = jnp.mean(g * normed, axis=-1, keepdims=True)
        in_ref[at, :] = rgrad[at, :] + scale * (g - mean_g - normed * mean_gn)
        nsum_ref[0:1, :] += jnp.sum(grad * normed, axis=0, keepdims=True)
        nsum_ref[1:2, :] += jnp.sum(grad, axis=0, keepdims=True)

    put_in().start()
    next_hop()
    mixed = dot(mg[...], att[:, 0:cols], TN)
    m_across().wait()
    pieces = qg_ref.shape[1:]
    qg_ref[3] = (mixed + m_got[...].astype(F32)).astype(BF).reshape(pieces)
    s_across().wait()
    qsum_ref[...] += s_got[...]
    next_hop()

    @pl.loop(0, 3)
    def _(k):
        to = pl.ds(pl.multiple_of(k * cols, cols), cols)
        qg = dot(rows1[...], dqkv[:, to], TN)
        q_across(k).wait()
        qg_ref[k] = (qg + q_got[k].astype(F32)).astype(BF).reshape(pieces)

    def rest_of_hops():
        while hops:
            next_hop()

    ring_part(
        n, rest_of_hops, qg_ref, nsum_ref, qsum_ref, dsum_ref, usum_ref, rbias_ref, resid_hbm, brn_hbm, brf_hbm,
        qo_ref, mo_ref, ro_ref, eo_ref, so_ref, bo_ref,
        *ring_scratch,
    )
    put_in().wait()


def backward(
    mg, qkv, att, rows1, wq, wqf, wm, wmf, x, rgrad, rg, eg, carry, resid, brn, brf,
    segments, g1, dsum, usum, rbias, n,
):
    rows, width = x.shape
    seq = mg.shape[0]
    cols = wq.shape[2]
    blocks = seq // QB
    vmem = pl.BlockSpec(memory_space=pltpu.VMEM)
    anyspace = pl.BlockSpec(memory_space=pl.ANY)
    split = rg.shape
    chunk = split[2:]
    pieces = (4, n, 2, width // (2 * n), cols)
    small = (n, 1, 8 * width // n)
    in_grad, qo, mo, ro, eo, so, bo = pl.pallas_call(
        functools.partial(bwd_kernel, n),
        in_specs=[anyspace] * 16 + [vmem] * 5,
        out_specs=[anyspace] * 5 + [vmem] * 2,
        out_shape=[
            jax.ShapeDtypeStruct((rows, width), F32),
            jax.ShapeDtypeStruct((3,) + pieces[1:], BF),
            jax.ShapeDtypeStruct(pieces[1:], BF),
            jax.ShapeDtypeStruct(split, BF),
            jax.ShapeDtypeStruct(split, BF),
            jax.ShapeDtypeStruct((8, width), F32),
            jax.ShapeDtypeStruct((rows, width), BF),
        ],
        scratch_shapes=[
            pltpu.VMEM((rows, width), F32),
            pltpu.VMEM(pieces, BF),
            pltpu.VMEM((2, cols), F32),
            pltpu.VMEM((2, width), F32),
            pltpu.VMEM(mg.shape, BF),
            pltpu.VMEM(qkv.shape, BF),
            pltpu.VMEM(att.shape, BF),
            pltpu.VMEM(rows1.shape, BF),
            pltpu.VMEM(wq.shape, BF),
            pltpu.VMEM(wq.shape, BF),
            pltpu.VMEM(wm.shape, BF),
            pltpu.VMEM(wm.shape, BF),
            pltpu.VMEM(x.shape, BF),
            pltpu.VMEM(rgrad.shape, F32),
            pltpu.VMEM((2,) + split, BF),
            pltpu.VMEM((n - 1, 2, 2) + chunk, BF),
            pltpu.VMEM(qkv.shape, BF),
            pltpu.VMEM((seq, cols), BF),
            pltpu.VMEM((QB * blocks * (blocks + 1) // 2, QB), F32),
            pltpu.VMEM((seq, PAIR), F32),
            pltpu.VMEM((seq, PAIR), F32),
            pltpu.VMEM((3, width, cols), BF),
            pltpu.VMEM((3, width, cols), BF),
            pltpu.VMEM((width, cols), BF),
            pltpu.VMEM((width, cols), BF),
            pltpu.VMEM((2, cols), F32),
            pltpu.VMEM((2, cols), F32),
            pltpu.VMEM((rows, width), BF),
            pltpu.VMEM((rows, width), BF),
            pltpu.VMEM((rows, width), F32),
            pltpu.SemaphoreType.DMA((6,)),
            pltpu.SemaphoreType.DMA((6,)),
            pltpu.SemaphoreType.DMA((2, 2)),
            pltpu.SemaphoreType.DMA((2, 2, n - 1)),
            pltpu.SemaphoreType.DMA((2, 2)),
            pltpu.SemaphoreType.DMA((2, 2, n - 1)),
            pltpu.SemaphoreType.DMA((14,)),
            pltpu.SemaphoreType.DMA((1,)),
            pltpu.VMEM((n - 1, 2, 4) + pieces[3:], BF),
            pltpu.VMEM((8, width), F32),
            pltpu.VMEM(small, F32),
            pltpu.VMEM((n - 1,) + small[1:], F32),
            pltpu.VMEM(small, F32),
            pltpu.VMEM((3,) + small, F32),
            pltpu.VMEM(small, F32),
            pltpu.VMEM((rows, width), F32),
            pltpu.VMEM((rows, width), BF),
            pltpu.VMEM((rows, width), BF),
            pltpu.SemaphoreType.DMA((8, 2)),
            pltpu.SemaphoreType.DMA((8, 2, n - 1)),
            pltpu.SemaphoreType.DMA((4, 2)),
            pltpu.SemaphoreType.DMA((4, 2, n - 1 - AHEAD)),
            pltpu.SemaphoreType.DMA((2,)),
            pltpu.SemaphoreType.DMA((2, n - 1)),
            pltpu.SemaphoreType.DMA((4,)),
            pltpu.SemaphoreType.DMA((4,)),
            pltpu.SemaphoreType.DMA((10,)),
        ],
        compiler_params=pltpu.CompilerParams(
            collective_id=4, has_side_effects=True, vmem_limit_bytes=60 << 20
        ),
        name="backward",
    )(
        mg, qkv, att, rows1, wq, wqf, wm, wmf, x, rgrad, rg, eg, carry, resid, brn, brf,
        segments, g1, dsum, usum, rbias,
    )
    wide = (-1, width)
    mixed = mo.reshape(width, cols)
    return in_grad, qo.reshape(3, width, cols), mixed, ro.reshape(wide), eo.reshape(wide), so, bo


GA = 0.7978845608028654
GB = 0.044715


def ff_kernel(
    n,
    n2_ref, og_hbm, we_hbm, wr_hbm, resid_hbm, be_ref, gain_ref,
    rgrad_out, mg_out, rg_out, eg_out, brn_out, brf_out, usum_ref, dsum_ref, carry_ref,
    rgrad_ref, mg_ref, rg_ref, eg_ref, brn_ref, brf_ref,
    og_ref, we_ref, wr_ref, resid_ref, n2b, act, pg, ng, br, ng_d, br_d, ng_s, br_s, ng_far, ng_out,
    rbuf, rbuf2, send, recv, ring_send, ring_recv, local, out,
):
    rows, width = n2_ref.shape
    units = we_ref.shape[1]
    part = rows // 2
    nb = 256
    me = lax.axis_index("tensor")
    core = me % 2
    sib = me + 1 - 2 * core
    far = (me + 2) % 4

    mine, pos, sides = ring_place(n)
    meet((sib, far), sides)
    h = rg_ref.shape[2]

    def remote(src, dst, k, other):
        return pltpu.make_async_remote_copy(
            src_ref=src,
            dst_ref=dst,
            send_sem=send.at[k],
            recv_sem=recv.at[k],
            device_id={"tensor": other},
            device_id_type=MESH_ID,
        )

    def y_at(c):
        return pl.ds((2 + c) * rows, part)

    def d_at(c):
        return pl.ds((2 + c) * rows + part, part)

    def rows_across(c):
        return remote(n2_ref.at[pl.ds(c * part, part)], n2b.at[y_at(c)], c, far)

    def rows_beside():
        return remote(n2_ref, n2b.at[pl.ds(rows, rows)], 2, sib)

    def rows_forward(c):
        return remote(n2b.at[y_at(c)], n2b.at[d_at(c)], 3 + c, sib)

    def ng_beside():
        return remote(ng.at[pl.ds(rows, rows)], ng_s, 5, sib)

    def br_beside():
        return remote(br.at[pl.ds(rows, rows)], br_s, 6, sib)

    def ng_combine(c):
        return remote(ng.at[d_at(c)], ng_d.at[c], 7 + c, sib)

    def br_combine(c):
        return remote(br.at[d_at(c)], br_d.at[c], 9 + c, sib)

    def ng_across(c):
        return remote(ng_out.at[c], ng_far.at[c], 11 + c, far)

    def own_half(c):
        return pl.ds(pl.multiple_of(core * rows + c * part, part), part)

    def mg_beside(c):
        return remote(mg_ref.at[pl.ds(c * part, part)], mg_out.at[own_half(c)], 13 + c, sib)

    def put(k):
        low, high = pl.ds(0, part), pl.ds(part, part)
        src, dst = (
            (rg_ref, rg_out),
            (eg_ref, eg_out),
            (brn_ref, brn_out),
            (brf_ref, brf_out),
            (rgrad_ref.at[low], rgrad_out.at[low]),
            (rgrad_ref.at[high], rgrad_out.at[high]),
            (mg_ref.at[low], mg_out.at[own_half(0)]),
            (mg_ref.at[high], mg_out.at[own_half(1)]),
        )[k]
        return pltpu.make_async_copy(src, dst, out.at[k])

    for c in range(2):
        rows_across(c).start()
    rows_beside().start()
    first = pl.ds(0, rows)
    rest = pl.ds(rows, 3 * rows)
    loads = [
        pltpu.make_async_copy(n2_ref, n2b.at[first], local.at[0]),
        pltpu.make_async_copy(we_hbm, we_ref, local.at[1]),
        pltpu.make_async_copy(og_hbm.at[first], og_ref.at[first], local.at[2]),
        pltpu.make_async_copy(wr_hbm, wr_ref, local.at[3]),
        pltpu.make_async_copy(og_hbm.at[rest], og_ref.at[rest], local.at[4]),
        pltpu.make_async_copy(resid_hbm, resid_ref, local.at[5]),
    ]
    for load in loads:
        load.start()
    usum_ref[...] = jnp.zeros_like(usum_ref)
    for load in loads[:4]:
        load.wait()

    @pl.loop(0, 4)
    def _(b):
        at = pl.ds(pl.multiple_of(b * rows, rows), rows)
        c = b - 2

        @pl.when(b == 1)
        def _():
            rows_beside().wait()
            loads[4].wait()

        @pl.when(b >= 2)
        def _():
            rows_across(c).wait()
            rows_forward(c).start()
            rows_forward(c).wait()

        for k in range(units // nb):
            cols = slice(k * nb, (k + 1) * nb)
            u = dot(n2b[at, :], we_ref[:, cols]) + be_ref[:, cols]
            act_grad = dot(og_ref[at, :], wr_ref[cols, :], NT)
            sq = u * u
            th = jnp.tanh(u * (GA + (GA * GB) * sq))
            cdf = 0.5 * (1.0 + th)
            slope = cdf + (0.5 * u) * (1.0 - th * th) * (GA + (3.0 * GA * GB) * sq)
            pre = (act_grad * slope).astype(BF)
            act[at, cols] = (u * cdf).astype(BF)
            pg[at, cols] = pre
            usum_ref[:, cols] += jnp.sum(pre.astype(F32), axis=0, keepdims=True)
        @pl.loop(0, width // nb)
        def _(k):
            cols = pl.ds(pl.multiple_of(k * nb, nb), nb)
            ng[at, cols] = dot(pg[at, :], we_ref[cols, :], NT).astype(BF)

        @pl.when(b == 1)
        def _():
            ng_beside().start()

        @pl.when(b >= 2)
        def _():
            ng_combine(c).start()

        @pl.loop(0, width // nb)
        def _(k):
            cols = pl.ds(pl.multiple_of(k * nb, nb), nb)
            br[at, cols] = dot(act[at, :], wr_ref[:, cols]).astype(BF)

        @pl.when(b == 1)
        def _():
            br_beside().start()

        @pl.when(b >= 2)
        def _():
            br_combine(c).start()
            ng_combine(c).wait()
            ng_out[c] = (ng[y_at(c), :].astype(F32) + ng_d[c].astype(F32)).astype(BF)
            ng_across(c).start()

    def part_of(d, s):
        return ring_index(pos - 1 - s if d == 0 else pos + 1 + s, n)

    ffg = (rg_ref, eg_ref)

    def ring_copy(kind, d):
        return pltpu.make_async_remote_copy(
            src_ref=ffg[kind].at[part_of(d, 0), d],
            dst_ref=rbuf.at[kind, d],
            send_sem=ring_send.at[kind, d],
            recv_sem=ring_recv.at[kind, d],
            device_id={"dp": sides[d]},
            device_id_type=MESH_ID,
        )

    def second_hop(d):
        return pltpu.make_async_remote_copy(
            src_ref=rbuf.at[0, d],
            dst_ref=rbuf2.at[d],
            send_sem=ring_send.at[2, d],
            recv_sem=ring_recv.at[2, d],
            device_id={"dp": sides[d]},
            device_id_type=MESH_ID,
        )

    @pl.loop(0, width // nb)
    def _(k):
        cols = pl.ds(pl.multiple_of(k * nb, nb), nb)
        grad = dot(act[...], og_ref[:, cols], TN).astype(BF)
        rg_ref[:, :, :, cols] = grad.reshape(n, 2, h, nb)

    for d in range(2):
        ring_copy(0, d).start()
    put(0).start()

    @pl.loop(0, width // nb)
    def _(k):
        cols = pl.ds(pl.multiple_of(k * nb, nb), nb)
        grad = dot(n2b[...], pg[:, cols], TN).astype(BF)
        eg_ref[:, :, :, cols] = grad.reshape(n, 2, h, nb)

    for d in range(2):
        ring_copy(1, d).start()
    put(1).start()
    br_beside().wait()
    brn_ref[...] = (br[0:rows, :].astype(F32) + br_s[...].astype(F32)).astype(BF)
    for c in range(2):
        br_combine(c).wait()
        brf_ref[c * part : (c + 1) * part, :] = (
            br[y_at(c), :].astype(F32) + br_d[c].astype(F32)
        ).astype(BF)
    put(2).start()
    put(3).start()
    ng_beside().wait()
    loads[5].wait()
    dsum_ref[...] = jnp.zeros_like(dsum_ref)
    step = 128
    for c in range(2):
        ng_across(c).wait()

        @pl.loop(0, part // step)
        def _(r):
            inner = pl.ds(pl.multiple_of(r * step, step), step)
            at = pl.ds(pl.multiple_of(c * part + r * step, step), step)
            grad = ng[at, :].astype(F32) + ng_s[at, :].astype(F32) + ng_far[c, inner, :].astype(F32)
            normed, scale = norm_stats(resid_ref[at, :])
            g = grad * gain_ref[...]
            gn = g * normed
            mean_g = jnp.mean(g, axis=-1, keepdims=True)
            mean_gn = jnp.mean(gn, axis=-1, keepdims=True)
            og = og_ref[at, :].astype(F32)
            rgrad = og + scale * (g - mean_g - normed * mean_gn)
            rgrad_ref[at, :] = rgrad
            mg = rgrad.astype(BF)
            mg_ref[at, :] = mg
            dsum_ref[0:1, :] += jnp.sum(mg.astype(F32), axis=0, keepdims=True)
            dsum_ref[1:2, :] += jnp.sum(grad * normed, axis=0, keepdims=True)
            dsum_ref[2:3, :] += jnp.sum(grad, axis=0, keepdims=True)
            dsum_ref[3:4, :] += jnp.sum(og, axis=0, keepdims=True)

        mg_beside(c).start()
        put(4 + c).start()
        put(6 + c).start()
        if c == 0:
            for d in range(2):
                ring_copy(0, d).wait()
                total = rbuf[0, d].astype(F32) + rg_ref[part_of(d, 1), d].astype(F32)
                rbuf[0, d] = total.astype(BF)
                second_hop(d).start()

    for d in range(2):
        second_hop(d).wait()
        total = rbuf2[d].astype(F32) + rg_ref[part_of(d, 2), d].astype(F32)
        carry_ref[0, d] = total.astype(BF)
    for d in range(2):
        ring_copy(1, d).wait()
        total = rbuf[1, d].astype(F32) + eg_ref[part_of(d, 1), d].astype(F32)
        carry_ref[1, d] = total.astype(BF)
    for c in range(2):
        mg_beside(c).wait()
    for k in range(8):
        put(k).wait()


def ff(n2, og_all, we, wr, be, resid, gain, n):
    rows, width = n2.shape
    units = we.shape[1]
    part = rows // 2
    vmem = pl.BlockSpec(memory_space=pltpu.VMEM)
    anyspace = pl.BlockSpec(memory_space=pl.ANY)
    return pl.pallas_call(
        functools.partial(ff_kernel, n),
        in_specs=[anyspace] * 5 + [vmem] * 2,
        out_specs=[anyspace] * 6 + [vmem] * 3,
        out_shape=[
            jax.ShapeDtypeStruct((rows, width), F32),
            jax.ShapeDtypeStruct((2 * rows, width), BF),
            jax.ShapeDtypeStruct((n, 2, units // (2 * n), width), BF),
            jax.ShapeDtypeStruct((n, 2, width // (2 * n), units), BF),
            jax.ShapeDtypeStruct((rows, width), BF),
            jax.ShapeDtypeStruct((rows, width), BF),
            jax.ShapeDtypeStruct((1, units), F32),
            jax.ShapeDtypeStruct((4, width), F32),
            jax.ShapeDtypeStruct((2, 2, units // (2 * n), width), BF),
        ],
        scratch_shapes=[
            pltpu.VMEM((rows, width), F32),
            pltpu.VMEM((rows, width), BF),
            pltpu.VMEM((n, 2, units // (2 * n), width), BF),
            pltpu.VMEM((n, 2, width // (2 * n), units), BF),
            pltpu.VMEM((rows, width), BF),
            pltpu.VMEM((rows, width), BF),
            pltpu.VMEM((4 * rows, width), BF),
            pltpu.VMEM(we.shape, BF),
            pltpu.VMEM(wr.shape, BF),
            pltpu.VMEM((rows, width), F32),
            pltpu.VMEM((4 * rows, width), BF),
            pltpu.VMEM((4 * rows, units), BF),
            pltpu.VMEM((4 * rows, units), BF),
            pltpu.VMEM((4 * rows, width), BF),
            pltpu.VMEM((4 * rows, width), BF),
            pltpu.VMEM((2, part, width), BF),
            pltpu.VMEM((2, part, width), BF),
            pltpu.VMEM((rows, width), BF),
            pltpu.VMEM((rows, width), BF),
            pltpu.VMEM((2, part, width), BF),
            pltpu.VMEM((2, part, width), BF),
            pltpu.VMEM((2, 2, units // (2 * n), width), BF),
            pltpu.VMEM((2, units // (2 * n), width), BF),
            pltpu.SemaphoreType.DMA((15,)),
            pltpu.SemaphoreType.DMA((15,)),
            pltpu.SemaphoreType.DMA((3, 2)),
            pltpu.SemaphoreType.DMA((3, 2)),
            pltpu.SemaphoreType.DMA((6,)),
            pltpu.SemaphoreType.DMA((8,)),
        ],
        compiler_params=pltpu.CompilerParams(
            collective_id=2, has_side_effects=True, vmem_limit_bytes=60 << 20
        ),
        name="ff",
    )(n2, og_all, we, wr, resid, be, gain)


def finish_kernel(
    q_hbm, m_hbm, r_hbm, e_hbm, in_hbm, bo_hbm, small_ref,
    bo_out, in_out, q_out, m_out, r_out, e_out, g1_ref, s1_ref, mb_ref, g2_ref, s2_ref, rb_ref, eb_ref, qb_ref,
    q_in, m_in, r_in, e_in, q_wide, m_wide, r_wide, e_wide, in_mid, bo_mid, read, write,
):
    enter = (
        pltpu.make_async_copy(in_hbm, in_mid, read.at[12]),
        pltpu.make_async_copy(bo_hbm, bo_mid, read.at[13]),
    )
    leave = (
        pltpu.make_async_copy(in_mid, in_out, write.at[0]),
        pltpu.make_async_copy(bo_mid, bo_out, write.at[1]),
    )
    quarter = r_in.shape[0] // 4
    jobs = []
    for c in range(4):
        at = pl.ds(c * quarter, quarter)
        for src, mid, wide, dst in ((r_hbm, r_in, r_wide, r_out), (e_hbm, e_in, e_wide, e_out)):
            jobs.append((src.at[at], mid.at[at], wide.at[at], dst.at[at]))
    for k in range(3):
        jobs.append((q_hbm.at[k], q_in.at[k], q_wide.at[k], q_out.at[k]))
    gets = [pltpu.make_async_copy(job[0], job[1], read.at[k]) for k, job in enumerate(jobs)]
    get_m = pltpu.make_async_copy(m_hbm, m_in, read.at[len(jobs)])
    get_m.start()
    for copy in enter:
        copy.start()
    for get in gets:
        get.start()
    for k, ref in enumerate((g1_ref, s1_ref, mb_ref, g2_ref, s2_ref, rb_ref, eb_ref)):
        ref[...] = small_ref[k : k + 1, :]
    cols = qb_ref.shape[1]
    for k in range(2):
        qb_ref[k : k + 1, :] = small_ref[7:8, k * cols : (k + 1) * cols]
    for k in range(2):
        enter[k].wait()
        leave[k].start()
    get_m.wait()
    m_wide[...] = m_in[...].astype(F32).T
    puts = [pltpu.make_async_copy(m_wide, m_out, write.at[2])]
    puts[0].start()
    for k, (_src, mid, wide, dst) in enumerate(jobs):
        gets[k].wait()
        step = 128

        @pl.loop(0, mid.shape[0] // step)
        def _(r):
            at = pl.ds(pl.multiple_of(r * step, step), step)
            wide[at] = mid[at].astype(F32)

        put = pltpu.make_async_copy(wide, dst, write.at[3 + k])
        put.start()
        puts.append(put)
    for copy in leave:
        copy.wait()
    for put in puts:
        put.wait()


def finish(q, m, r, e, in_grad, block_out, small):
    vmem = pl.BlockSpec(memory_space=pltpu.VMEM)
    anyspace = pl.BlockSpec(memory_space=pl.ANY)
    width = small.shape[1]
    row = jax.ShapeDtypeStruct((1, width), F32)
    return pl.pallas_call(
        finish_kernel,
        in_specs=[anyspace] * 6 + [vmem],
        out_specs=[anyspace] * 6 + [vmem] * 8,
        out_shape=[
            jax.ShapeDtypeStruct(block_out.shape, BF),
            jax.ShapeDtypeStruct(in_grad.shape, F32),
            jax.ShapeDtypeStruct(q.shape, F32),
            jax.ShapeDtypeStruct(m.shape[::-1], F32),
            jax.ShapeDtypeStruct(r.shape, F32),
            jax.ShapeDtypeStruct(e.shape, F32),
        ]
        + [row] * 7
        + [jax.ShapeDtypeStruct((2, q.shape[2]), F32)],
        scratch_shapes=[
            pltpu.VMEM(q.shape, BF),
            pltpu.VMEM(m.shape, BF),
            pltpu.VMEM(r.shape, BF),
            pltpu.VMEM(e.shape, BF),
            pltpu.VMEM(q.shape, F32),
            pltpu.VMEM(m.shape[::-1], F32),
            pltpu.VMEM(r.shape, F32),
            pltpu.VMEM(e.shape, F32),
            pltpu.VMEM(in_grad.shape, F32),
            pltpu.VMEM(block_out.shape, BF),
            pltpu.SemaphoreType.DMA((14,)),
            pltpu.SemaphoreType.DMA((14,)),
        ],
        compiler_params=pltpu.CompilerParams(vmem_limit_bytes=60 << 20),
        name="finish",
    )(q, m, r, e, in_grad, block_out, small)


def body(
    block_in,
    segments,
    first_gain,
    first_shift,
    w_qkv,
    qv_bias,
    w_mix,
    mix_bias,
    second_gain,
    second_shift,
    w_expand,
    expand_bias,
    w_reduce,
    reduce_bias,
    out_grad,
):
    width = block_in.shape[1]
    cols = w_qkv.shape[2]
    units = w_expand.shape[1]
    dp_size = lax.axis_size("dp")
    flat = (1, width)
    wq = w_qkv.transpose(1, 0, 2)
    rows1, qkv, att, resid, n2, wq_far, wm_far, og_all = forward(
        block_in,
        segments,
        first_gain.reshape(flat),
        first_shift.reshape(flat),
        qv_bias,
        mix_bias.reshape(flat),
        second_gain.reshape(flat),
        second_shift.reshape(flat),
        wq,
        w_mix,
        out_grad,
        dp_size,
    )
    resid_grad, mg_all, reduce_grad, expand_grad, br_near, br_far, unit_sums, sums2, carry = ff(
        n2, og_all, w_expand, w_reduce, expand_bias.reshape(1, units), resid, second_gain.reshape(flat), dp_size
    )
    in_grad, qkv_grad, mix_grad, reduce_all, expand_all, small, block_out = backward(
        mg_all,
        qkv,
        att,
        rows1,
        wq,
        wq_far,
        w_mix,
        wm_far,
        block_in,
        resid_grad,
        reduce_grad,
        expand_grad,
        carry,
        resid,
        br_near,
        br_far,
        segments,
        first_gain.reshape(flat),
        sums2,
        unit_sums,
        reduce_bias.reshape(flat),
        dp_size,
    )
    block_out, in_grad, qkv_grad, mix_grad, reduce_all, expand_all, *rest, qv_bias_grad = finish(
        qkv_grad, mix_grad, reduce_all, expand_all, in_grad, block_out, small
    )
    g1, s1, mb, g2, s2, rb, eb = (item.reshape(-1) for item in rest)
    return (
        block_out,
        in_grad,
        g1,
        s1,
        qkv_grad.transpose(1, 0, 2),
        qv_bias_grad,
        mix_grad,
        mb,
        g2,
        s2,
        expand_all,
        eb,
        reduce_all,
        rb,
    )


def solution(mesh):
    both = P(("dp", "tensor"), None)
    return jax.shard_map(
        body,
        mesh=mesh,
        in_specs=(
            both,
            P("dp", None),
            P(),
            P(),
            P(None, None, "tensor"),
            P(None, "tensor"),
            P("tensor", None),
            P(),
            P(),
            P(),
            P(None, "tensor"),
            P("tensor"),
            P("tensor", None),
            P(),
            both,
        ),
        out_specs=(
            both,
            both,
            P(),
            P(),
            P(None, None, "tensor"),
            P(None, "tensor"),
            P("tensor", None),
            P(),
            P(),
            P(),
            P(None, "tensor"),
            P("tensor"),
            P("tensor", None),
            P(),
        ),
        check_vma=False,
    )
```
